32 devices in a mesh: groups: 2 (over x), ctx: 16 (over z, y, core).
Axes of the slice: x: 2, y: 2, z: 4, core: 2. Of those that a mesh axis runs over, the one named last changes fastest.
Arguments:
- queries: bfloat16 [16384, 1024], P(('groups', 'ctx')), parts along dimension 0, may hold values from -24 to 24
- key_rows: bfloat16 [16384, 1024], P(('groups', 'ctx')), parts along dimension 0, may hold values from -12 to 12
- value_rows: bfloat16 [16384, 1024], P(('groups', 'ctx')), parts along dimension 0, may hold values from -6 to 6
- step_rates: float32 [2, 16384], P(None, ('groups', 'ctx')), parts along dimension 1, may hold values from 0.002 to 0.02
- w_gate: bfloat16 [2048, 512], P('groups'), parts along dimension 0, may hold values from -2 to 2
- w_up: bfloat16 [2048, 512], P('groups'), parts along dimension 0, may hold values from -2 to 2
- w_down: bfloat16 [2048, 512], P('groups'), parts along dimension 0, may hold values from -2 to 2
Outputs:
- layer_out: bfloat16 [16384, 1024], P(('groups', 'ctx')), parts along dimension 0
- new_weights: bfloat16 [6144, 512], P(('groups', 'ctx')), parts along dimension 0
The draws below stay inside these ranges and needn't reach their ends.
There are 2 independent parts, one for each index of `groups`. The reference program is written for one: setup_inputs(seed, part) draws one part's arguments, and reference() takes and returns one part's arrays. A program takes and returns all parts, laid end to end along the dimension named above; each array names one. Nothing has to cross between parts.
All inputs are finite; a program needn't handle non-finite values.
Results may differ from the reference program's by a relative error of at most 0.012.
The reference program's roundings to bfloat16 on the way count: a program that leaves them out, or rounds other values in their place, can miss the bound.
Values may be sent and summed in bfloat16 or wider, within the bound.
No kernel may reach another device: no remote copies, remote signals or barrier semaphores. Data moves between devices by JAX's collectives and lax.ppermute only.
A program may use at most 64 MiB of HBM per device.

```python
import math
import jax
import jax.numpy as jnp
from jax import lax

H = 2
HD = 512
WINDOW = 1024
TOK_DEV = 512
TOKENS = 8192


def query_key_pair(key):
    base_value = jax.random.fold_in(key, 11)
    query_draw_seed, key_draw_seed, query_scale_seed, key_scale_seed = jax.random.split(base_value, 4)
    row_values = TOKENS
    width = H * HD
    query_vals = jnp.clip(jax.random.normal(query_draw_seed, (row_values, width), jnp.float32), -4.0, 4.0)
    key_vals = jnp.clip(jax.random.normal(key_draw_seed, (row_values, width), jnp.float32), -4.0, 4.0)
    q_scale = jnp.exp(jax.random.uniform(query_scale_seed, (row_values, 1), jnp.float32, math.log(0.3), math.log(3.0)))
    scale_draw_seed = jnp.exp(jax.random.uniform(key_scale_seed, (row_values, 1), jnp.float32, math.log(0.3), math.log(3.0)))
    query_vals = query_vals * q_scale
    key_vals = key_vals * scale_draw_seed
    return (query_vals, key_vals)


def draw_queries(key, part):
    return query_key_pair(key)[0].astype(jnp.bfloat16)


def draw_key_rows(key, part):
    return query_key_pair(key)[1].astype(jnp.bfloat16)


def fast_rows(key, salt):
    base_value = jax.random.fold_in(key, salt)
    k_entries, scale_draw_seed = jax.random.split(base_value)
    row_values = H * HD
    entries = jnp.clip(jax.random.normal(k_entries, (row_values, HD), jnp.float32), -4.0, 4.0)
    scale = jnp.exp(jax.random.uniform(scale_draw_seed, (row_values, 1), jnp.float32, math.log(0.3), math.log(3.0)))
    return (entries * scale * (1.0 / math.sqrt(HD))).astype(jnp.bfloat16)


def draw_w_gate(key, part):
    return fast_rows(key, 21)


def draw_w_up(key, part):
    return fast_rows(key, 22)


def draw_w_down(key, part):
    return fast_rows(key, 23)


def block_scale(key, dims, cuts, smallest, top_value):
    def one(axis_at, blocks):
        draws = jax.random.uniform(jax.random.fold_in(jax.random.fold_in(key, 6), axis_at), (blocks,), jnp.float32, smallest / len(cuts), top_value / len(cuts))
        return jnp.repeat(jnp.exp(draws), dims[axis_at] // blocks).reshape((-1,) + (1,) * (len(dims) - axis_at - 1))

    factor_of = one(*cuts[0])
    for cut in cuts[1:]:
        factor_of = factor_of * one(*cut)
    return factor_of


def gaussian(key, shape, scale, reach, pieces=(), kind=jnp.bfloat16):
    drawn = jax.random.normal(key, shape, jnp.float32) * scale
    if len(pieces) > 0:
        drawn = block_scale(key, shape, pieces, -0.22, 0.18) * drawn
    return jnp.clip(drawn, min=-reach, max=reach).astype(kind)


def setup_inputs(seed: int = 0, part: int = 0) -> dict:
    key_of = jax.random.split(jax.random.key(seed), 8)
    own_keys = jax.random.split(jax.random.fold_in(key_of[7], part), 8)
    return {
        "queries": draw_queries(jax.random.fold_in(jax.random.fold_in(key_of[7], part), 71), part),
        "key_rows": draw_key_rows(jax.random.fold_in(jax.random.fold_in(key_of[7], part), 71), part),
        "value_rows": gaussian(own_keys[2], (TOKENS, H * HD), 1.0, 6.0, ((0, 16),)),
        "step_rates": jnp.clip(jnp.exp(math.log(0.02) - 2.30258502 * jax.random.uniform(own_keys[3], (H, TOKENS), jnp.float32) ** block_scale(own_keys[3], (H, TOKENS), ((1, 16),), -0.2, 0.2)), 0.002, 0.02),
        "w_gate": draw_w_gate(jax.random.fold_in(jax.random.fold_in(key_of[7], part), 71), part),
        "w_up": draw_w_up(jax.random.fold_in(jax.random.fold_in(key_of[7], part), 71), part),
        "w_down": draw_w_down(jax.random.fold_in(jax.random.fold_in(key_of[7], part), 71), part),
    }


def rms_rows(row_values):
    values = row_values.astype(jnp.float32).reshape(row_values.shape[0], H, HD)
    return (values * lax.rsqrt(lax.optimization_barrier(jnp.mean(values * values, -1, keepdims=True)) + 1e-06)).astype(jnp.bfloat16)

def attend(queries, key_rows, value_rows):
    block_rows = min(512, TOK_DEV)
    count = TOKENS // block_rows
    padding = jnp.zeros((WINDOW, H * HD), jnp.bfloat16)
    key_pad = jnp.concatenate([padding, key_rows], 0)
    value_pad = jnp.concatenate([padding, value_rows], 0)

    def one_block(which):
        first = (which * block_rows).astype(jnp.int32)
        q_block = lax.dynamic_slice_in_dim(queries, first, block_rows, 0).reshape(block_rows, H, HD).astype(jnp.float32)
        k_block = lax.dynamic_slice_in_dim(key_pad, first, WINDOW + block_rows, 0).reshape(WINDOW + block_rows, H, HD).astype(jnp.float32)
        v_block = lax.dynamic_slice_in_dim(value_pad, first, WINDOW + block_rows, 0).reshape(WINDOW + block_rows, H, HD).astype(jnp.float32)
        scores = jnp.einsum('qhd,khd->hqk', q_block, k_block) * (1.0 / math.sqrt(HD))
        q_pos = first + jnp.arange(block_rows, dtype=jnp.int32)
        k_pos = first - WINDOW + jnp.arange(WINDOW + block_rows, dtype=jnp.int32)
        allowed = (k_pos[None, :] <= q_pos[:, None]) & (k_pos[None, :] > q_pos[:, None] - WINDOW) & (k_pos[None, :] >= 0)
        scores = jnp.where(allowed[None], scores, -jnp.inf)
        highest = lax.optimization_barrier(jnp.max(scores, -1, keepdims=True))
        expo = jnp.exp(scores - highest)
        weights = (expo / lax.optimization_barrier(jnp.sum(expo, -1, keepdims=True))).astype(jnp.bfloat16)
        result = jnp.einsum('hqk,khd->qhd', weights.astype(jnp.float32), v_block)
        return result.astype(jnp.bfloat16)
    blocks = lax.map(one_block, jnp.arange(count, dtype=jnp.int32))
    return blocks.reshape(TOKENS, H, HD)

def normalize_rows(old_rows, grad_rows):
    old_values = old_rows.astype(jnp.float32)
    raised = old_values - grad_rows
    factor = jnp.sqrt(lax.optimization_barrier(jnp.mean(old_values * old_values, -1, keepdims=True)) + 1e-06) * lax.rsqrt(lax.optimization_barrier(jnp.mean(raised * raised, -1, keepdims=True)) + 1e-06)
    return (raised * factor).astype(jnp.bfloat16)

def reference(queries, key_rows, value_rows, step_rates, w_gate, w_up, w_down):
    q_norm = rms_rows(queries)
    k_norm = rms_rows(key_rows)
    attended = attend(queries, key_rows, value_rows)
    gate_m = w_gate.reshape(H, HD, HD).astype(jnp.float32)
    up_m = w_up.reshape(H, HD, HD).astype(jnp.float32)
    down_m = w_down.reshape(H, HD, HD).astype(jnp.float32)
    k_vals = k_norm.astype(jnp.float32)
    pre_gate = jnp.einsum('thd,hjd->thj', k_vals, gate_m)
    pre_up = jnp.einsum('thd,hjd->thj', k_vals, up_m)
    sig = jax.nn.sigmoid(pre_gate)
    active = pre_gate * sig
    gated = (active * pre_up).astype(jnp.bfloat16)
    errors = (-step_rates.T[:, :, None] * attended.astype(jnp.float32)).astype(jnp.bfloat16)
    err_vals = errors.astype(jnp.float32)
    grad_down = jnp.einsum('tho,thj->hoj', err_vals, gated.astype(jnp.float32))
    back = jnp.einsum('tho,hoj->thj', err_vals, down_m)
    d_gate = (back * pre_up * sig * (1.0 + pre_gate * (1.0 - sig))).astype(jnp.bfloat16)
    d_up = (back * active).astype(jnp.bfloat16)
    grad_gate = jnp.einsum('thj,thd->hjd', d_gate.astype(jnp.float32), k_vals)
    grad_up = jnp.einsum('thj,thd->hjd', d_up.astype(jnp.float32), k_vals)
    grads = jnp.concatenate([grad_gate.reshape(H * HD, HD), grad_up.reshape(H * HD, HD), grad_down.reshape(H * HD, HD)], 0)
    old_rows = jnp.concatenate([w_gate, w_up, w_down], 0)
    new_weights = normalize_rows(old_rows, grads)
    new_gate = new_weights[:H * HD].reshape(H, HD, HD).astype(jnp.float32)
    new_up = new_weights[H * HD:2 * H * HD].reshape(H, HD, HD).astype(jnp.float32)
    new_down = new_weights[2 * H * HD:].reshape(H, HD, HD).astype(jnp.float32)
    q_vals = q_norm.astype(jnp.float32)
    q_gate = jnp.einsum('thd,hjd->thj', q_vals, new_gate)
    q_up = jnp.einsum('thd,hjd->thj', q_vals, new_up)
    q_gated = (q_gate * jax.nn.sigmoid(q_gate) * q_up).astype(jnp.bfloat16)
    fast_out = jnp.einsum('thj,hoj->tho', q_gated.astype(jnp.float32), new_down)
    layer_out = (attended.astype(jnp.float32) + fast_out).astype(jnp.bfloat16).reshape(TOKENS, H * HD)
    return (layer_out, new_weights)
```

```python
import functools
import math

import jax
import jax.numpy as jnp
from jax import lax
from jax.experimental import pallas as pl
from jax.experimental.pallas import tpu as pltpu
from jax.sharding import Mesh, PartitionSpec as P

H = 2
HD = 512
BLK = 512
BF = jnp.bfloat16
F32 = jnp.float32
SWAP = [(0, 1), (1, 0)]
PARAMS = pltpu.CompilerParams(vmem_limit_bytes=56 << 20)


def mm(a, b, dims):
    return lax.dot_general(a, b, (dims, ((), ())), preferred_element_type=F32)


def mm_t(a, b):
    return mm(a, b, ((1,), (1,)))


def mm_n(a, b):
    return mm(a, b, ((1,), (0,)))


def mm_rows(a, b):
    return mm(a, b, ((0,), (0,)))


def rms(x):
    v = x.astype(F32)
    return (v * lax.rsqrt(jnp.mean(v * v, -1, keepdims=True) + 1e-06)).astype(BF)


def attend_block(q, kbuf, vbuf, ia, ib, ic, a_ok, b_ok, out):
    half = BLK // 2
    scale = 1.0 / math.sqrt(HD)
    p = lax.broadcasted_iota(jnp.int32, (half, half), 0)
    j = lax.broadcasted_iota(jnp.int32, (half, half), 1)
    causal = j <= p
    neg = jnp.float32(-jnp.inf)
    for c in range(2):
        rows = pl.ds(c * half, half)
        qc = q[rows, :]
        tiles = []
        for t in range(2):
            cols = pl.ds(t * half, half)
            if t <= c:
                sc = mm_t(qc, kbuf[ic, cols, :]) * scale
            if t >= c:
                sa = mm_t(qc, kbuf[ia, cols, :]) * scale
                sa = jnp.where(a_ok, sa, neg)
            tiles.append(sc if t < c else sa if t > c else jnp.where(causal, sc, sa))
        sb = mm_t(qc, kbuf[ib]) * scale
        tiles.append(jnp.where(b_ok, sb, neg))
        top = functools.reduce(jnp.maximum, [jnp.max(s, -1, keepdims=True) for s in tiles])
        expo = [jnp.exp(s - top) for s in tiles]
        total = functools.reduce(jnp.add, [jnp.sum(e, -1, keepdims=True) for e in expo])
        inv = 1.0 / total
        w = [(e * inv).astype(BF) for e in expo]
        acc = mm_n(w[2], vbuf[ib])
        zero = jnp.zeros((half, half), BF)
        for t in range(2):
            cols = pl.ds(t * half, half)
            if t <= c:
                acc += mm_n(jnp.where(causal, w[t], zero) if t == c else w[t], vbuf[ic, cols, :])
            if t >= c:
                acc += mm_n(jnp.where(causal, zero, w[t]) if t == c else w[t], vbuf[ia, cols, :])
        out[rows, :] = acc.astype(BF)


def main_kernel(
    where, q_own, q_for, *rest
):
    ks, vs = rest[:5], rest[5:10]
    r_own, r_for, wg, wu, wd = rest[10:15]
    att_own, att_for, keep, send = rest[15:19]
    qbuf, kbuf, vbuf, kn, err, gated, dgate, dup, sems = rest[19:]
    y, k, z = where[0], where[1], where[2]
    copies = []
    for n, (src, dst) in enumerate(
        [(q_own, qbuf.at[0]), (q_for, qbuf.at[1])]
        + [(ks[i], kbuf.at[i]) for i in range(5)]
        + [(vs[i], vbuf.at[i]) for i in range(5)]
    ):
        copy = pltpu.make_async_copy(src, dst, sems.at[n])
        copy.start()
        copies.append(copy)
    for copy in copies:
        copy.wait()
    inner = z > 0
    lower_own = y == 0
    ia_own = jnp.where(lower_own, 2, 1)
    ib_own = jnp.where(y == k, 4, 3)
    ia_for = jnp.where(lower_own, 0, 2)
    ib_for = jnp.where(y == k, 3, 4)
    a_own = inner | (y == 1)
    a_for = inner | (y == 0)
    b_own = inner | (y == 1) | (k == 1)
    b_for = inner | (y == 0) | (k == 1)
    attend_block(qbuf.at[0], kbuf, vbuf, ia_own, ib_own, 0, a_own, b_own, att_own)
    attend_block(qbuf.at[1], kbuf, vbuf, ia_for, ib_for, 1, a_for, b_for, att_for)
    for n, (att, rate) in enumerate([(att_own, r_own), (att_for, r_for)]):
        for c in range(2):
            half = BLK // 2
            rows = pl.ds(c * half, half)
            trows = pl.ds(n * BLK + c * half, half)
            knc = rms(kbuf[n, rows, :])
            e = (-rate[rows, :] * att[rows, :].astype(F32)).astype(BF)
            hg = mm_t(knc, wg[...])
            hu = mm_t(knc, wu[...])
            back = mm_n(e, wd[...])
            sig = jax.nn.sigmoid(hg)
            act = hg * sig
            kn[trows, :] = knc
            err[trows, :] = e
            gated[trows, :] = (act * hu).astype(BF)
            dgate[trows, :] = (back * hu * sig * (1.0 + hg * (1.0 - sig))).astype(BF)
            dup[trows, :] = (back * act).astype(BF)
    part = HD // 2
    for kind, (a, b) in enumerate([(dgate, kn), (dup, kn), (err, gated)]):
        for side in range(2):
            g = mm_rows(a[:, side * part : (side + 1) * part], b[...])

            @pl.when(k == side)
            def _():
                keep[kind] = g

            @pl.when(k != side)
            def _():
                send[kind] = g.astype(BF)


def main_call(where, q_own, q_for, ks, vs, r_own, r_for, w_gate, w_up, w_down):
    anyspec = pl.BlockSpec(memory_space=pl.ANY)
    whole = lambda shape: pl.BlockSpec(shape, lambda i, s: (0,) * len(shape))
    head = pl.BlockSpec((HD, HD), lambda i, s: (s[0], 0))
    part = HD // 2
    return pl.pallas_call(
        main_kernel,
        grid_spec=pltpu.PrefetchScalarGridSpec(
            num_scalar_prefetch=1,
            grid=(1,),
            in_specs=[anyspec] * 12 + [whole((BLK, 1))] * 2 + [head] * 3,
            out_specs=[
                whole((BLK, HD)),
                whole((BLK, HD)),
                whole((3, part, HD)),
                whole((3, part, HD)),
            ],
            scratch_shapes=[
                pltpu.VMEM((2, BLK, HD), BF),
                pltpu.VMEM((5, BLK, HD), BF),
                pltpu.VMEM((5, BLK, HD), BF),
            ]
            + [pltpu.VMEM((2 * BLK, HD), BF)] * 5
            + [pltpu.SemaphoreType.DMA((12,))],
        ),
        out_shape=[
            jax.ShapeDtypeStruct((BLK, HD), BF),
            jax.ShapeDtypeStruct((BLK, HD), BF),
            jax.ShapeDtypeStruct((3, part, HD), F32),
            jax.ShapeDtypeStruct((3, part, HD), BF),
        ],
        compiler_params=PARAMS,
        name="attend_grads",
    )(where, q_own, q_for, *ks, *vs, r_own, r_for, w_gate, w_up, w_down)


def chip_sum_kernel(zs, rows, where, keep, got, own, *sends):
    z = where[2]
    for d in range(zs):
        at = lax.rem(z + d, zs) * rows
        src = pl.ds(pl.multiple_of(at, rows), rows)
        for kind in range(3):
            total = keep[kind, src, :] + got[kind, src, :].astype(F32)
            if d == 0:
                own[kind] = total
            else:
                sends[d - 1][kind] = total.astype(BF)


def chip_sum_call(zs, where, keep, got):
    rows = HD // 2 // zs
    vm = pl.BlockSpec(memory_space=pltpu.VMEM)
    shape = (3, rows, HD)
    return pl.pallas_call(
        functools.partial(chip_sum_kernel, zs, rows),
        in_specs=[pl.BlockSpec(memory_space=pltpu.SMEM), vm, vm],
        out_specs=[vm] * zs,
        out_shape=[jax.ShapeDtypeStruct(shape, F32)]
        + [jax.ShapeDtypeStruct(shape, BF)] * (zs - 1),
        compiler_params=PARAMS,
        name="chip_sum",
    )(where, keep, got)


def update_kernel(where, own, *rest):
    got, olds, out = rest[:-4], rest[-4:-1], rest[-1]
    for kind in range(3):
        grad = own[kind]
        for g in got:
            grad = grad + g[kind].astype(F32)
        old = olds[kind][...].astype(F32)
        raised = old - grad
        factor = jnp.sqrt(jnp.mean(old * old, -1, keepdims=True) + 1e-06) * lax.rsqrt(
            jnp.mean(raised * raised, -1, keepdims=True) + 1e-06
        )
        out[kind] = (raised * factor).astype(BF)


def update_call(zs, where, own, got, w_gate, w_up, w_down):
    rows = HD // 2 // zs
    shape = (3, rows, HD)
    whole = pl.BlockSpec(shape, lambda i, s: (0, 0, 0))
    old = pl.BlockSpec((rows, HD), lambda i, s: ((s[0] * 2 + s[1]) * zs + s[2], 0))
    return pl.pallas_call(
        update_kernel,
        grid_spec=pltpu.PrefetchScalarGridSpec(
            num_scalar_prefetch=1,
            grid=(1,),
            in_specs=[whole] * zs + [old] * 3,
            out_specs=whole,
        ),
        out_shape=jax.ShapeDtypeStruct(shape, BF),
        compiler_params=PARAMS,
        name="update",
    )(where, own, *got, w_gate, w_up, w_down)


def read_block(q, att, w, out):
    half = BLK // 2
    for c in range(2):
        rows = pl.ds(c * half, half)
        qn = rms(q[rows, :])
        hg = mm_t(qn, w[0:HD, :])
        hu = mm_t(qn, w[HD : 2 * HD, :])
        g = (hg * jax.nn.sigmoid(hg) * hu).astype(BF)
        fast = mm_t(g, w[2 * HD : 3 * HD, :])
        out[rows, :] = (att[rows, :].astype(F32) + fast).astype(BF)


def window(w, out, first, count):
    step = math.gcd(count, HD)
    for c in range(count // step):
        r = first + c * step
        block = lax.div(r, HD)
        at = lax.div(block, 2) * HD + lax.rem(r, HD)
        out[c * step : (c + 1) * step, :] = w[pl.ds(pl.multiple_of(at, step), step), :]


def read_foreign_kernel(zs, count, where, *rest):
    mine, theirs = rest[:zs], rest[zs : 2 * zs]
    q, att, out, full, given, kept = rest[2 * zs :]
    y, k, z = where[0], where[1], where[2]
    rows = HD // 2 // zs
    for side, pieces in ((k, mine), (1 - k, theirs)):
        for d in range(zs):
            at = side * (HD // 2) + lax.rem(z - d + zs, zs) * rows
            for kind in range(3):
                full[pl.ds(pl.multiple_of(kind * HD + at, rows), rows), :] = pieces[d][kind]
    me = (z * 2 + y) * 2 + k
    partner = (z * 2 + 1 - y) * 2 + k
    window(full, given, partner * count, count)
    window(full, kept, me * count, count)
    read_block(q, att, full, out)


def read_foreign_call(zs, count, where, mine, theirs, q, att):
    vm = pl.BlockSpec(memory_space=pltpu.VMEM)
    return pl.pallas_call(
        functools.partial(read_foreign_kernel, zs, count),
        in_specs=[pl.BlockSpec(memory_space=pltpu.SMEM)] + [vm] * (2 * zs + 2),
        out_specs=[vm] * 4,
        out_shape=[
            jax.ShapeDtypeStruct((BLK, HD), BF),
            jax.ShapeDtypeStruct((3 * HD, HD), BF),
            jax.ShapeDtypeStruct((count, HD), BF),
            jax.ShapeDtypeStruct((count, HD), BF),
        ],
        compiler_params=PARAMS,
        name="read_foreign",
    )(where, *mine, *theirs, q, att)


def read_own_kernel(q, att, w, out):
    read_block(q, att, w, out)


def read_own_call(q, att, w):
    vm = pl.BlockSpec(memory_space=pltpu.VMEM)
    return pl.pallas_call(
        read_own_kernel,
        in_specs=[vm] * 3,
        out_specs=vm,
        out_shape=jax.ShapeDtypeStruct((BLK, HD), BF),
        compiler_params=PARAMS,
        name="read_own",
    )(q, att, w)


def local(queries, key_rows, value_rows, step_rates, w_gate, w_up, w_down):
    zs = lax.axis_size("z")
    z, y, k = lax.axis_index("z"), lax.axis_index("y"), lax.axis_index("core")
    where = jnp.stack([y, k, z]).astype(jnp.int32)

    def head_of(rows, head):
        return lax.dynamic_slice(rows, (0, head * HD), (BLK, HD))

    def rate_of(head):
        return lax.dynamic_slice(step_rates, (head, 0), (1, BLK))

    def swap(value, axis):
        return lax.ppermute(value, axis, SWAP)

    def shift(value, d, ring=True):
        pairs = [(i, (i + d) % zs) for i in range(zs) if ring or i + d < zs]
        return lax.ppermute(value, "z", pairs)

    k_for = swap(head_of(key_rows, 1 - y), "y")
    v_for = swap(head_of(value_rows, 1 - y), "y")
    q_for = swap(head_of(queries, 1 - y), "y")
    r_for = swap(rate_of(1 - y), "y")
    k_own, v_own, q_own = (head_of(a, y) for a in (key_rows, value_rows, queries))
    r_own = rate_of(y)

    sides = []
    for own, foreign in ((k_own, k_for), (v_own, v_for)):
        low = jnp.where(y == 0, own, foreign)
        high = jnp.where(y == 0, foreign, own)
        halo = shift(high, 1, ring=False)
        low_other = swap(low, "core")
        cross_other = swap(jnp.where(k == 0, high, halo), "core")
        sides.append((own, foreign, halo, low_other, cross_other))

    att_own, att_for, keep, send = main_call(
        where,
        q_own,
        q_for,
        sides[0],
        sides[1],
        r_own.reshape(BLK, 1),
        r_for.reshape(BLK, 1),
        w_gate,
        w_up,
        w_down,
    )
    got = swap(send, "core")
    own_sum, *sends = chip_sum_call(zs, where, keep, got)
    arrived = [shift(s, d) for d, s in enumerate(sends, 1)]
    piece = update_call(zs, where, own_sum, arrived, w_gate, w_up, w_down)
    mine = [piece] + [shift(piece, d) for d in range(1, zs)]
    theirs = [swap(p, "core") for p in mine]
    count = 3 * H * HD // (4 * zs)
    out_for, full, given, kept = read_foreign_call(zs, count, where, mine, theirs, q_for, att_for)
    out_got = swap(out_for, "y")
    rows_got = swap(given, "y")
    out_own = read_own_call(q_own, att_own, full)
    layer_out = jnp.where(
        y == 0,
        jnp.concatenate([out_own, out_got], 1),
        jnp.concatenate([out_got, out_own], 1),
    )
    rows = ((z * 2 + y) * 2 + k) * count + jnp.arange(count, dtype=jnp.int32)
    head = lax.rem(lax.div(rows, HD), 2)
    own_weights = jnp.where((head == y)[:, None], kept, rows_got)
    return (layer_out, own_weights)


def solution(mesh):
    groups, ctx = mesh.devices.shape
    split = Mesh(mesh.devices.reshape(groups, ctx // 4, 2, 2), ("groups", "z", "y", "core"))
    tokens = ("groups", "z", "y", "core")
    return jax.shard_map(
        local,
        mesh=split,
        in_specs=(
            P(tokens, None),
            P(tokens, None),
            P(tokens, None),
            P(None, tokens),
            P("groups", None),
            P("groups", None),
            P("groups", None),
        ),
        out_specs=(P(tokens, None), P(tokens, None)),
        check_vma=False,
    )
```

```python
import functools
import math

import jax
import jax.numpy as jnp
from jax import lax
from jax.experimental import pallas as pl
from jax.experimental.pallas import tpu as pltpu
from jax.sharding import Mesh, PartitionSpec as P

H = 2
HD = 512
BLK = 512
HALF = 256
RATE_ROWS = 16
BF = jnp.bfloat16
F32 = jnp.float32
SWAP = [(0, 1), (1, 0)]
PARAMS = pltpu.CompilerParams(vmem_limit_bytes=20 << 20)
VM = pl.BlockSpec(memory_space=pltpu.VMEM)
SM = pl.BlockSpec(memory_space=pltpu.SMEM)


def mm(a, b, dims):
    return lax.dot_general(a, b, (dims, ((), ())), preferred_element_type=F32)


def mm_t(a, b):
    return mm(a, b, ((1,), (1,)))


def mm_n(a, b):
    return mm(a, b, ((1,), (0,)))


def mm_rows(a, b):
    return mm(a, b, ((0,), (0,)))


def rms(x):
    v = x.astype(F32)
    return (v * lax.rsqrt(jnp.mean(v * v, -1, keepdims=True) + 1e-06)).astype(BF)


def shape(dims, dtype=BF):
    return jax.ShapeDtypeStruct(dims, dtype)


def call(kernel, name, outs, scratch=()):
    def run(where, *args):
        return pl.pallas_call(
            kernel,
            in_specs=[SM] + [VM] * len(args),
            out_specs=[VM] * len(outs),
            out_shape=outs,
            scratch_shapes=scratch,
            compiler_params=PARAMS,
            name=name,
        )(where, *args)

    return run


def call_blocks(kernel, name, specs, outs, scratch=()):
    def run(where, *args):
        def whole(dims):
            return pl.BlockSpec(dims, lambda i, s: (0,) * len(dims))

        in_specs = [whole(a.shape) if p is None else p for a, p in zip(args, specs, strict=True)]
        return pl.pallas_call(
            kernel,
            grid_spec=pltpu.PrefetchScalarGridSpec(
                num_scalar_prefetch=1,
                grid=(1,),
                in_specs=in_specs,
                out_specs=[whole(o.shape) for o in outs],
                scratch_shapes=scratch,
            ),
            out_shape=outs,
            compiler_params=PARAMS,
            name=name,
        )(where, *args)

    return run


def pack_kernel(where, key, value, out):
    out[:, 0:HD] = key[...]
    out[:, HD : 2 * HD] = value[...]


def pack(where, key_rows, value_rows, first, count, own):
    def block(i, s):
        return (first // count, s[0] if own else 1 - s[0])

    return pl.pallas_call(
        pack_kernel,
        grid_spec=pltpu.PrefetchScalarGridSpec(
            num_scalar_prefetch=1,
            grid=(1,),
            in_specs=[pl.BlockSpec((count, HD), block)] * 2,
            out_specs=pl.BlockSpec((count, 2 * HD), lambda i, s: (0, 0)),
        ),
        out_shape=shape((count, 2 * HD)),
        compiler_params=PARAMS,
        name="pack",
    )(where, key_rows, value_rows)


def pick_kernel(where, foreign, key, value, out):
    own = where[0] == 1
    out[:, 0:HD] = jnp.where(own, key[...], foreign[:, 0:HD])
    out[:, HD : 2 * HD] = jnp.where(own, value[...], foreign[:, HD : 2 * HD])


def pick(where, foreign, key_rows, value_rows, n):
    part = pl.BlockSpec((HALF, HD), lambda i, s: (n, s[0]))
    return call_blocks(pick_kernel, "pick", [None, part, part], [shape((HALF, 2 * HD))])(
        where, foreign, key_rows, value_rows
    )[0]


def pack_q_kernel(where, query, rates, sent):
    sent[0:BLK, :] = query[...]
    rate = jnp.where(where[0] == 0, rates[1:2, :], rates[0:1, :])
    parts = []
    for _ in range(3):
        part = rate.astype(BF)
        parts.append(part)
        rate = rate - part.astype(F32)
    row = lax.broadcasted_iota(jnp.int32, (RATE_ROWS, BLK), 0)
    tail = jnp.zeros((RATE_ROWS, BLK), F32)
    for n, part in enumerate(parts):
        tail = jnp.where(row == n, part.astype(F32), tail)
    sent[BLK : BLK + RATE_ROWS, :] = tail.astype(BF)


def factors(core, key, wg, wu, put):
    for c in range(2):
        rows = pl.ds(c * HALF, HALF)
        kc = rms(key(c))
        put(0, rows, slice(None), kc)
        for side in range(2):
            units = pl.ds(side * HALF, HALF)
            hg = mm_t(kc, wg[units, :])
            hu = mm_t(kc, wu[units, :])
            sig = jax.nn.sigmoid(hg)
            a = hg * sig
            put(1, rows, units, (a * hu).astype(BF))

            @pl.when(core == side)
            def _():
                put(2, rows, slice(None), hu * sig * (1.0 + hg * (1.0 - sig)))
                put(3, rows, slice(None), a)


def pre_own_kernel(where, own, own2, wg, wu, *outs):
    for n, kv in enumerate((own, own2)):

        def put(i, rows, columns, value):
            outs[4 * n + i][rows, columns] = value

        factors(where[1], lambda c: kv[c * HALF : (c + 1) * HALF, 0:HD], wg, wu, put)


def pick_factors(where, halves, mine, wg, wu, outs, work):
    def put(i, rows, columns, value):
        work[i][rows, columns] = value

    factors(where[1], lambda c: halves[c][:, 0:HD], wg, wu, put)
    bottom = where[0] == 0
    for i in range(4):
        outs[i][...] = jnp.where(bottom, mine[i][...], work[i][...])
        outs[4 + i][...] = jnp.where(bottom, work[i][...], mine[i][...])


def pre_kernel(where, own, for_a, for_b, own2, for2_a, for2_b, *rest):
    mine, (wg, wu), (low, high, mid, low2), outs = rest[:4], rest[4:6], rest[6:10], rest[10:18]
    bottom = where[0] == 0
    first = where[1] == 0
    for c, (f, f2) in enumerate(((for_a, for2_a), (for_b, for2_b))):
        rows = pl.ds(c * HALF, HALF)
        low[rows, :] = jnp.where(bottom, own[rows, :], f[...])
        high[rows, :] = jnp.where(bottom, f[...], own[rows, :])
        l2 = jnp.where(bottom, own2[rows, :], f2[...])
        low2[rows, :] = l2
        mid[rows, :] = jnp.where(first, l2, jnp.where(bottom, f2[...], own2[rows, :]))
    pick_factors(where, (for_a, for_b), mine, wg, wu, outs, rest[18:])


def pre_other_kernel(where, for2_a, for2_b, *rest):
    pick_factors(where, (for2_a, for2_b), rest[:4], *rest[4:6], rest[6:14], rest[14:])


FACTORS = [
    shape((BLK, HD)),
    shape((BLK, HD)),
    shape((BLK, HALF), F32),
    shape((BLK, HALF), F32),
]


def pre_own(where, own, own2, w_gate, w_up):
    head = pl.BlockSpec((HD, HD), lambda i, s: (s[0], 0))
    return call_blocks(pre_own_kernel, "pre_own", [None] * 2 + [head] * 2, FACTORS * 2)(
        where, own, own2, w_gate, w_up
    )


def pre(kernel, where, pairs, mine, w_gate, w_up, outs):
    head = pl.BlockSpec((HD, HD), lambda i, s: (s[0], 0))
    specs = [None] * (len(pairs) + 4) + [head] * 2
    work = [pltpu.VMEM(f.shape, f.dtype) for f in FACTORS]
    return call_blocks(kernel, "pre", specs, outs + FACTORS * 2, work)(
        where, *pairs, *mine, w_gate, w_up
    )


def attend(q, rate, tile_a, tile_b, tile_c, a_ok, b_ok, att, err):
    scale = 1.0 / math.sqrt(HD)
    p = lax.broadcasted_iota(jnp.int32, (HALF, HALF), 0)
    j = lax.broadcasted_iota(jnp.int32, (HALF, HALF), 1)
    causal = j <= p
    neg = jnp.float32(-jnp.inf)
    zero = jnp.zeros((HALF, HALF), BF)

    def key(tile):
        return tile[:, 0:HD]

    def value(tile):
        return tile[:, HD : 2 * HD]

    for c in range(2):
        rows = pl.ds(c * HALF, HALF)
        qc = q(rows)
        tiles = []
        for t in range(2):
            if t <= c:
                sc = mm_t(qc, key(tile_c(t))) * scale
            if t >= c:
                sa = mm_t(qc, key(tile_a(t))) * scale
                if a_ok is not None:
                    sa = jnp.where(a_ok, sa, neg)
            tiles.append(sc if t < c else sa if t > c else jnp.where(causal, sc, sa))
        for t in range(2):
            sb = mm_t(qc, key(tile_b(t))) * scale
            tiles.append(sb if b_ok is None else jnp.where(b_ok, sb, neg))
        top = functools.reduce(jnp.maximum, [jnp.max(s, -1, keepdims=True) for s in tiles])
        expo = [jnp.exp(s - top) for s in tiles]
        total = functools.reduce(jnp.add, [jnp.sum(e, -1, keepdims=True) for e in expo])
        inv = 1.0 / total
        w = [(e * inv).astype(BF) for e in expo]
        acc = mm_n(w[2], value(tile_b(0))) + mm_n(w[3], value(tile_b(1)))
        for t in range(2):
            if t <= c:
                acc += mm_n(
                    jnp.where(causal, w[t], zero) if t == c else w[t], value(tile_c(t))
                )
            if t >= c:
                acc += mm_n(
                    jnp.where(causal, zero, w[t]) if t == c else w[t], value(tile_a(t))
                )
        out = acc.astype(BF)
        att[rows, :] = out
        err[rows, :] = (-rate[c * HALF : (c + 1) * HALF] * out.astype(F32)).astype(BF)


def column(mine, side, rates, q_for):
    parts = q_for[BLK : BLK + RATE_ROWS, :].astype(F32)
    other = parts[0:1, :] + parts[1:2, :] + parts[2:3, :]
    own = jnp.where(side == 0, rates[0:1, :], rates[1:2, :])
    line = jnp.where(mine, own, other)
    return jnp.transpose(jnp.broadcast_to(line, (8, BLK)))[:, 0:1]


def rows_of(ref):
    return lambda t: ref[t * HALF : (t + 1) * HALF, :]


def upper_kernel(where, q_own, q_for, rates, a, b, c, att, err):
    mine = where[0] == 1
    q = lambda rows: jnp.where(mine, q_own[rows, :], q_for[rows, :])
    r = column(mine, where[0], rates, q_for)
    attend(q, r, rows_of(a), rows_of(b), rows_of(c), None, None, att, err)


def lower_kernel(
    where, q_own, q_for, rates, halo_a, halo_b, halo2_a, halo2_b, low2, c, att, err, b
):
    mine = where[0] == 0
    first = where[1] == 0
    inner = where[2] > 0
    for t, h in enumerate((halo2_a, halo2_b)):
        rows = pl.ds(t * HALF, HALF)
        b[rows, :] = jnp.where(first, h[...], low2[rows, :])
    q = lambda rows: jnp.where(mine, q_own[rows, :], q_for[rows, :])
    r = column(mine, where[0], rates, q_for)
    halo = (halo_a, halo_b)
    attend(
        q, r, lambda t: halo[t][...], rows_of(b), rows_of(c), inner, inner | ~first, att, err
    )


def back_products(errs, kns, slopes, acts, w):
    gate = up = None
    for e, kn, slope, act in zip(errs, kns, slopes, acts, strict=True):
        back = mm_n(e[...], w[...])
        g = mm_rows((back * slope[...]).astype(BF), kn[...])
        u = mm_rows((back * act[...]).astype(BF), kn[...])
        gate = g if gate is None else gate + g
        up = u if up is None else up + u
    return gate, up


def down_products(errs, gateds):
    acc = None
    for e, g in zip(errs, gateds, strict=True):
        d = mm_rows(e[...], g[...])
        acc = d if acc is None else acc + d
    return acc


def grad_first_kernel(where, e0, e1, h0, h1, k0, k1, g0, g1, s0, s1, a0, a1, w, total):
    gate, up = back_products((e0, e1), (k0, k1), (s0, s1), (a0, a1), w)
    total[0] = gate
    total[1] = up
    total[2] = down_products((h0, h1), (g0, g1))


def grad_second_kernel(
    zs, where, e0, e1, h0, h1, k0, k1, g0, g1, s0, s1, a0, a1, before, w, own, *rest
):
    sends, total = rest[:-1], rest[-1]
    gate, up = back_products((e0, e1), (k0, k1), (s0, s1), (a0, a1), w)
    total[0] = before[0] + gate
    total[1] = before[1] + up
    total[2] = before[2] + down_products((h0, h1), (g0, g1))
    rows = HALF // zs
    for d in range(zs):
        src = pl.ds(pl.multiple_of(lax.rem(where[2] + d, zs) * rows, rows), rows)
        for kind in range(3):
            if d == 0:
                own[kind] = total[kind, src, :]
            else:
                sends[d - 1][kind] = total[kind, src, :].astype(BF)


def update_kernel(where, own, *rest):
    got, olds, (first, last) = rest[:-5], rest[-5:-2], rest[-2:]
    for kind, out in enumerate((first.at[0], first.at[1], last.at[0])):
        grad = own[kind]
        for g in got:
            grad = grad + g[kind].astype(F32)
        old = olds[kind][...].astype(F32)
        raised = old - grad
        factor = jnp.sqrt(jnp.mean(old * old, -1, keepdims=True) + 1e-06) * lax.rsqrt(
            jnp.mean(raised * raised, -1, keepdims=True) + 1e-06
        )
        out[...] = (raised * factor).astype(BF)


def update(zs, where, own, got, olds):
    rows = HALF // zs
    old = pl.BlockSpec((rows, HD), lambda i, s: ((s[0] * 2 + s[1]) * zs + s[2], 0))
    return call_blocks(
        update_kernel,
        "update",
        [None] * zs + [old] * 3,
        [shape((2, rows, HD)), shape((1, rows, HD))],
    )(where, own, *got, *olds)


def gather(zs, where, pieces, kinds, full):
    rows = HALF // zs
    for side, some in ((where[1], pieces[:zs]), (1 - where[1], pieces[zs:])):
        for d in range(zs):
            at = side * HALF + lax.rem(where[2] - d + zs, zs) * rows
            for kind in range(kinds):
                full[pl.ds(pl.multiple_of(kind * HD + at, rows), rows), :] = some[d][kind]


def windows(where, count, put):
    y, core, z = where[0], where[1], where[2]
    step = math.gcd(count, HD)
    for n, side in enumerate((1 - y, y)):
        first = ((z * 2 + side) * 2 + core) * count
        for c in range(count // step):
            r = first + c * step
            put(n, c * step, step, lax.div(r, 2 * HD), pl.multiple_of(lax.rem(r, HD), step))


def read_first_kernel(zs, count, where, *rest):
    pieces, (q_for, q_own) = rest[: 2 * zs], rest[2 * zs : 2 * zs + 2]
    g_for, g_own, given, kept, full = rest[2 * zs + 2 :]
    gather(zs, where, pieces, 2, full)
    outs = (given, kept)

    def put(n, to, step, kind, row):
        at = pl.multiple_of(lax.min(kind, 1) * HD + row, step)
        outs[n][to : to + step, :] = full[pl.ds(at, step), :]

    windows(where, count, put)
    for q, g in ((q_for, g_for), (q_own, g_own)):
        for c in range(2):
            rows = pl.ds(c * HALF, HALF)
            qn = rms(q[rows, :])
            hg = mm_t(qn, full[0:HD, :])
            hu = mm_t(qn, full[HD : 2 * HD, :])
            g[rows, :] = (hg * jax.nn.sigmoid(hg) * hu).astype(BF)


def read_down_kernel(zs, count, where, *rest):
    pieces = rest[: 2 * zs]
    g_for, att_low, att_up, some_given, some_kept, sent, full, kept = rest[2 * zs :]
    gather(zs, where, pieces, 1, full)
    low = where[0] == 1
    sent[0:BLK, :] = (
        jnp.where(low, att_low[...], att_up[...]).astype(F32) + mm_t(g_for[...], full[...])
    ).astype(BF)
    outs, before = (sent, kept), (some_given, some_kept)

    def put(n, to, step, kind, row):
        rows = slice(to, to + step)
        at = slice(to + BLK, to + BLK + step) if n == 0 else rows
        outs[n][at, :] = jnp.where(kind == 2, full[pl.ds(row, step), :], before[n][rows, :])

    windows(where, count, put)


def read_own_kernel(where, g_own, att_low, att_up, w, out):
    low = where[0] == 0
    out[...] = (
        jnp.where(low, att_low[...], att_up[...]).astype(F32) + mm_t(g_own[...], w[...])
    ).astype(BF)


def read_own(where, g_own, att_low, att_up, w):
    whole = pl.BlockSpec((BLK, HD), lambda i, s: (0, 0))
    return pl.pallas_call(
        read_own_kernel,
        grid_spec=pltpu.PrefetchScalarGridSpec(
            num_scalar_prefetch=1,
            grid=(1,),
            in_specs=[whole] * 4,
            out_specs=pl.BlockSpec((BLK, HD), lambda i, s: (0, s[0])),
        ),
        out_shape=shape((BLK, H * HD)),
        compiler_params=PARAMS,
        name="read_own",
    )(where, g_own, att_low, att_up, w)


def place_kernel(count, where, got, kept, half_filled, out, weights):
    y, core, z = where[0], where[1], where[2]
    out[...] = got[0:BLK, :]
    step = math.gcd(count, HD)
    first = ((z * 2 + y) * 2 + core) * count
    for c in range(count // step):
        rows = slice(c * step, (c + 1) * step)
        head = lax.rem(lax.div(first + c * step, HD), 2)
        weights[rows, :] = jnp.where(
            head == y, kept[rows, :], got[BLK + c * step : BLK + (c + 1) * step, :]
        )


def place(where, count, got, kept, half_filled):
    def whole(rows):
        return pl.BlockSpec((rows, HD), lambda i, s: (0, 0))

    return pl.pallas_call(
        functools.partial(place_kernel, count),
        grid_spec=pltpu.PrefetchScalarGridSpec(
            num_scalar_prefetch=1,
            grid=(1,),
            in_specs=[whole(BLK + count), whole(count), pl.BlockSpec(memory_space=pl.ANY)],
            out_specs=[pl.BlockSpec((BLK, HD), lambda i, s: (0, 1 - s[0])), whole(count)],
        ),
        out_shape=[shape((BLK, H * HD)), shape((count, HD))],
        input_output_aliases={3: 0},
        compiler_params=PARAMS,
        name="place",
    )(where, got, kept, half_filled)


def local(queries, key_rows, value_rows, step_rates, w_gate, w_up, w_down):
    zs = lax.axis_size("z")
    z, y, core = lax.axis_index("z"), lax.axis_index("y"), lax.axis_index("core")
    where = jnp.stack([y, core, z]).astype(jnp.int32)
    rows = HALF // zs
    count = 3 * H * HD // (4 * zs)

    def swap(value, axis):
        return lax.ppermute(value, axis, SWAP)

    def shift(value, d, ring=True):
        return lax.ppermute(
            value, "z", [(i, (i + d) % zs) for i in range(zs) if ring or i + d < zs]
        )

    two = [shape((BLK, HD))] * 2

    def after(value, earlier):
        return lax.optimization_barrier((value, earlier))[0]

    q_other = pl.BlockSpec((BLK, HD), lambda i, s: (0, 1 - s[0]))
    sent_a = pack(where, key_rows, value_rows, 0, HALF, False)
    sent_b = pack(where, after(key_rows, sent_a), value_rows, HALF, HALF, False)
    sent_q = call_blocks(
        pack_q_kernel, "pack_q", [q_other, None], [shape((BLK + RATE_ROWS, HD))]
    )(where, after(queries, sent_b), step_rates)[0]
    own = pack(where, after(key_rows, sent_b), value_rows, 0, BLK, True)
    theirs = [swap(sent_a, "y"), swap(sent_b, "y")]
    q_for = swap(sent_q, "y")
    q_own = jnp.where(y == 0, queries[:, :HD], queries[:, HD:])
    own2 = swap(own, "core")
    gone = pick(where, theirs[0], key_rows, value_rows, 0)
    halo_a = shift(gone, 1, ring=False)
    theirs2 = [swap(after(theirs[0], gone), "core")]
    theirs[1], own2, theirs2[0] = lax.optimization_barrier((theirs[1], own2, theirs2[0]))
    gone = pick(where, theirs[1], key_rows, value_rows, 1)
    halo_b = shift(gone, 1, ring=False)
    theirs2.append(swap(after(theirs[1], gone), "core"))
    theirs2, halo_a = lax.optimization_barrier((theirs2, halo_a))
    mine = pre_own(where, own, own2, w_gate, w_up)
    kv_low, kv_high, kv_mid, kv_low2, *blocks = pre(
        pre_kernel,
        where,
        (own, *theirs, own2, *theirs2),
        mine[:4],
        w_gate,
        w_up,
        [shape((BLK, 2 * HD))] * 4,
    )
    theirs2, q_for, blocks = lax.optimization_barrier((theirs2, q_for, blocks))
    blocks += pre(pre_other_kernel, where, theirs2, mine[4:], w_gate, w_up, [])
    blocks, q_for, halo = lax.optimization_barrier((blocks, q_for, (halo_a, halo_b)))
    low, high, low2, high2 = (blocks[4 * n : 4 * n + 4] for n in range(4))
    halo2 = [swap(h, "core") for h in halo]

    att_up, err_up = call(upper_kernel, "attend_upper", two)(
        where, q_own, q_for, step_rates, kv_low, kv_mid, kv_high
    )
    err_up2 = swap(err_up, "core")
    att_low, err_low = call(
        lower_kernel, "attend_lower", two, [pltpu.VMEM((BLK, 2 * HD), BF)]
    )(where, q_own, q_for, step_rates, *halo, *halo2, kv_low2, kv_low)
    err_low2 = swap(err_low, "core")

    w_half = pl.BlockSpec((HD, HALF), lambda i, s: (s[0], s[1]))
    err_half = pl.BlockSpec((BLK, HALF), lambda i, s: (0, s[1]))

    def grads(kernel, name, outs, errs, pair, *more, scratch=()):
        specs = [None] * 2 + [err_half] * 2 + [None] * (8 + len(more)) + [w_half]
        factors = [pair[i][n] for n in range(4) for i in range(2)]
        return call_blocks(kernel, name, specs, outs, scratch)(
            where, *errs, *errs, *factors, *more, w_down
        )

    total = shape((3, HALF, HD), F32)
    first = grads(grad_first_kernel, "grad_first", [total], (err_up, err_up2), (high, high2))[0]
    own_sum, *sends = grads(
        functools.partial(grad_second_kernel, zs),
        "grad_second",
        [shape((3, rows, HD), F32)] + [shape((3, rows, HD))] * (zs - 1),
        (err_low, err_low2),
        (low, low2),
        first,
        scratch=[pltpu.VMEM(total.shape, F32)],
    )
    got = [shift(s, d) for d, s in enumerate(sends, 1)]
    piece_a, piece_b = update(zs, where, own_sum, got, (w_gate, w_up, w_down))

    def around(piece):
        return [piece] + [shift(piece, d) for d in range(1, zs)]

    def both(mine):
        return mine + [swap(p, "core") for p in mine]

    pieces_a = both(around(piece_a))
    pieces_b = around(piece_b)
    window = shape((count, HD))
    g_for, g_own, some_given, some_kept = call(
        functools.partial(read_first_kernel, zs, count),
        "read_first",
        two + [window] * 2,
        [pltpu.VMEM((2 * HD, HD), BF)],
    )(where, *pieces_a, q_for, q_own)
    g_for, pieces_b = lax.optimization_barrier((g_for, pieces_b))
    pieces_b = both(pieces_b)
    sent, full, kept = call(
        functools.partial(read_down_kernel, zs, count),
        "read_down",
        [shape((BLK + count, HD)), shape((HD, HD)), window],
    )(where, *pieces_b, g_for, att_low, att_up, some_given, some_kept)
    got_out = swap(sent, "y")
    half_filled = read_own(where, g_own, att_low, att_up, full)
    return tuple(place(where, count, got_out, kept, half_filled))


def solution(mesh):
    groups, ctx = mesh.devices.shape
    split = Mesh(mesh.devices.reshape(groups, ctx // 4, 2, 2), ("groups", "z", "y", "core"))
    tokens = ("groups", "z", "y", "core")
    return jax.shard_map(
        local,
        mesh=split,
        in_specs=(
            P(tokens, None),
            P(tokens, None),
            P(tokens, None),
            P(None, tokens),
            P("groups", None),
            P("groups", None),
            P("groups", None),
        ),
        out_specs=(P(tokens, None), P(tokens, None)),
        check_vma=False,
    )
```

```python
import functools
import math

import jax
import jax.numpy as jnp
from jax import lax
from jax.experimental import pallas as pl
from jax.experimental.pallas import tpu as pltpu
from jax.sharding import Mesh, PartitionSpec as P

H = 2
HD = 512
BLK = 512
HALF = 256
RATE_ROWS = 16
BF = jnp.bfloat16
F32 = jnp.float32
SWAP = [(0, 1), (1, 0)]
PARAMS = pltpu.CompilerParams(vmem_limit_bytes=20 << 20)
VM = pl.BlockSpec(memory_space=pltpu.VMEM)
SM = pl.BlockSpec(memory_space=pltpu.SMEM)


def mm(a, b, dims):
    return lax.dot_general(a, b, (dims, ((), ())), preferred_element_type=F32)


def mm_t(a, b):
    return mm(a, b, ((1,), (1,)))


def mm_n(a, b):
    return mm(a, b, ((1,), (0,)))


def mm_rows(a, b):
    return mm(a, b, ((0,), (0,)))


def rms(x):
    v = x.astype(F32)
    return (v * lax.rsqrt(jnp.mean(v * v, -1, keepdims=True) + 1e-06)).astype(BF)


def in_hbm(value):
    return pltpu.with_memory_space_constraint(value, pltpu.HBM)


def shape(dims, dtype=BF):
    return jax.ShapeDtypeStruct(dims, dtype)


def call(kernel, name, outs, scratch=()):
    def run(where, *args):
        return pl.pallas_call(
            kernel,
            in_specs=[SM] + [VM] * len(args),
            out_specs=[VM] * len(outs),
            out_shape=outs,
            scratch_shapes=scratch,
            compiler_params=PARAMS,
            name=name,
        )(where, *args)

    return run


def call_blocks(kernel, name, specs, outs, scratch=()):
    def run(where, *args):
        def whole(dims):
            return pl.BlockSpec(dims, lambda i, s: (0,) * len(dims))

        in_specs = [whole(a.shape) if p is None else p for a, p in zip(args, specs, strict=True)]
        return pl.pallas_call(
            kernel,
            grid_spec=pltpu.PrefetchScalarGridSpec(
                num_scalar_prefetch=1,
                grid=(1,),
                in_specs=in_specs,
                out_specs=[whole(o.shape) for o in outs],
                scratch_shapes=scratch,
            ),
            out_shape=outs,
            compiler_params=PARAMS,
            name=name,
        )(where, *args)

    return run


def pack_kernel(where, key, value, out):
    out[:, 0:HD] = key[...]
    out[:, HD : 2 * HD] = value[...]


def pack(where, key_rows, value_rows, first, count, own):
    def block(i, s):
        return (first // count, s[0] if own else 1 - s[0])

    return pl.pallas_call(
        pack_kernel,
        grid_spec=pltpu.PrefetchScalarGridSpec(
            num_scalar_prefetch=1,
            grid=(1,),
            in_specs=[pl.BlockSpec((count, HD), block)] * 2,
            out_specs=pl.BlockSpec((count, 2 * HD), lambda i, s: (0, 0)),
        ),
        out_shape=shape((count, 2 * HD)),
        compiler_params=PARAMS,
        name="pack",
    )(where, in_hbm(key_rows), in_hbm(value_rows))


def pick_kernel(where, foreign, key, value, out):
    own = where[0] == 1
    out[:, 0:HD] = jnp.where(own, key[...], foreign[:, 0:HD])
    out[:, HD : 2 * HD] = jnp.where(own, value[...], foreign[:, HD : 2 * HD])


def pick(where, foreign, key_rows, value_rows, n):
    part = pl.BlockSpec((HALF, HD), lambda i, s: (n, s[0]))
    return call_blocks(pick_kernel, "pick", [None, part, part], [shape((HALF, 2 * HD))])(
        where, foreign, in_hbm(key_rows), in_hbm(value_rows)
    )[0]


def pack_q_kernel(where, query, rates, sent):
    sent[0:BLK, :] = query[...]
    rate = jnp.where(where[0] == 0, rates[1:2, :], rates[0:1, :])
    parts = []
    for _ in range(3):
        part = rate.astype(BF)
        parts.append(part)
        rate = rate - part.astype(F32)
    row = lax.broadcasted_iota(jnp.int32, (RATE_ROWS, BLK), 0)
    tail = jnp.zeros((RATE_ROWS, BLK), F32)
    for n, part in enumerate(parts):
        tail = jnp.where(row == n, part.astype(F32), tail)
    sent[BLK : BLK + RATE_ROWS, :] = tail.astype(BF)


def factors(core, key, wg, wu, put):
    for c in range(2):
        rows = pl.ds(c * HALF, HALF)
        kc = rms(key(c))
        put(0, rows, slice(None), kc)
        for side in range(2):
            units = pl.ds(side * HALF, HALF)
            hg = mm_t(kc, wg[units, :])
            hu = mm_t(kc, wu[units, :])
            sig = jax.nn.sigmoid(hg)
            a = hg * sig
            put(1, rows, units, (a * hu).astype(BF))

            @pl.when(core == side)
            def _():
                put(2, rows, slice(None), hu * sig * (1.0 + hg * (1.0 - sig)))
                put(3, rows, slice(None), a)


def pre_own_kernel(where, own, own2, wg, wu, *outs):
    for n, kv in enumerate((own, own2)):

        def put(i, rows, columns, value):
            outs[4 * n + i][rows, columns] = value

        factors(where[1], lambda c: kv[c * HALF : (c + 1) * HALF, 0:HD], wg, wu, put)


def pick_factors(where, halves, mine, wg, wu, outs, work):
    def put(i, rows, columns, value):
        work[i][rows, columns] = value

    factors(where[1], lambda c: halves[c][:, 0:HD], wg, wu, put)
    bottom = where[0] == 0
    for i in range(4):
        outs[i][...] = jnp.where(bottom, mine[i][...], work[i][...])
        outs[4 + i][...] = jnp.where(bottom, work[i][...], mine[i][...])


def pre_kernel(where, *rest):
    pick_factors(where, rest[:2], rest[2:6], *rest[6:8], rest[8:16], rest[16:])


FACTORS = [
    shape((BLK, HD)),
    shape((BLK, HD)),
    shape((BLK, HALF), F32),
    shape((BLK, HALF), F32),
]


def pre_own(where, own, own2, wg, wu):
    return call(pre_own_kernel, "pre_own", FACTORS * 2)(where, own, own2, wg, wu)


def pre(where, halves, mine, wg, wu):
    work = [pltpu.VMEM(f.shape, f.dtype) for f in FACTORS]
    outs = call(pre_kernel, "pre", FACTORS * 2, work)(where, *halves, *mine, wg, wu)
    return outs[:4], outs[4:]


def attend(q, rate, tile_a, tile_b, tile_c, a_ok, b_ok, att, err):
    scale = 1.0 / math.sqrt(HD)
    p = lax.broadcasted_iota(jnp.int32, (HALF, HALF), 0)
    j = lax.broadcasted_iota(jnp.int32, (HALF, HALF), 1)
    causal = j <= p
    neg = jnp.float32(-jnp.inf)
    zero = jnp.zeros((HALF, HALF), BF)

    def key(tile):
        return tile[:, 0:HD]

    def value(tile):
        return tile[:, HD : 2 * HD]

    for c in range(2):
        rows = pl.ds(c * HALF, HALF)
        qc = q(rows)
        tiles = []
        for t in range(2):
            if t <= c:
                sc = mm_t(qc, key(tile_c(t))) * scale
            if t >= c:
                sa = mm_t(qc, key(tile_a(t))) * scale
                if a_ok is not None:
                    sa = jnp.where(a_ok, sa, neg)
            tiles.append(sc if t < c else sa if t > c else jnp.where(causal, sc, sa))
        for t in range(2):
            sb = mm_t(qc, key(tile_b(t))) * scale
            tiles.append(sb if b_ok is None else jnp.where(b_ok, sb, neg))
        top = functools.reduce(jnp.maximum, [jnp.max(s, -1, keepdims=True) for s in tiles])
        expo = [jnp.exp(s - top) for s in tiles]
        total = functools.reduce(jnp.add, [jnp.sum(e, -1, keepdims=True) for e in expo])
        inv = 1.0 / total
        w = [(e * inv).astype(BF) for e in expo]
        acc = mm_n(w[2], value(tile_b(0))) + mm_n(w[3], value(tile_b(1)))
        for t in range(2):
            if t <= c:
                acc += mm_n(
                    jnp.where(causal, w[t], zero) if t == c else w[t], value(tile_c(t))
                )
            if t >= c:
                acc += mm_n(
                    jnp.where(causal, zero, w[t]) if t == c else w[t], value(tile_a(t))
                )
        out = acc.astype(BF)
        att[rows, :] = out
        err[rows, :] = (-rate[c * HALF : (c + 1) * HALF] * out.astype(F32)).astype(BF)


def column(mine, side, rates, q_for):
    parts = q_for[BLK : BLK + RATE_ROWS, :].astype(F32)
    other = parts[0:1, :] + parts[1:2, :] + parts[2:3, :]
    own = jnp.where(side == 0, rates[0:1, :], rates[1:2, :])
    line = jnp.where(mine, own, other)
    return jnp.transpose(jnp.broadcast_to(line, (8, BLK)))[:, 0:1]


def rows_of(ref):
    return lambda t: ref[t * HALF : (t + 1) * HALF, :]


def upper_kernel(
    where, q_own, q_for, rates, own, for_a, for_b, own2, for2_a, for2_b, *rest
):
    att, err, low, low2, high, mid = rest
    bottom = where[0] == 0
    first = where[1] == 0
    for c, (f, f2) in enumerate(((for_a, for2_a), (for_b, for2_b))):
        rows = pl.ds(c * HALF, HALF)
        low[rows, :] = jnp.where(bottom, own[rows, :], f[...])
        high[rows, :] = jnp.where(bottom, f[...], own[rows, :])
        l2 = jnp.where(bottom, own2[rows, :], f2[...])
        low2[rows, :] = l2
        mid[rows, :] = jnp.where(first, l2, jnp.where(bottom, f2[...], own2[rows, :]))
    mine = where[0] == 1
    q = lambda rows: jnp.where(mine, q_own[rows, :], q_for[rows, :])
    r = column(mine, where[0], rates, q_for)
    attend(q, r, rows_of(low), rows_of(mid), rows_of(high), None, None, att, err)


def lower_kernel(
    where, q_own, q_for, rates, halo_a, halo_b, halo2_a, halo2_b, low2, c, att, err, b
):
    mine = where[0] == 0
    first = where[1] == 0
    inner = where[2] > 0
    for t, h in enumerate((halo2_a, halo2_b)):
        rows = pl.ds(t * HALF, HALF)
        b[rows, :] = jnp.where(first, h[...], low2[rows, :])
    q = lambda rows: jnp.where(mine, q_own[rows, :], q_for[rows, :])
    r = column(mine, where[0], rates, q_for)
    halo = (halo_a, halo_b)
    attend(
        q, r, lambda t: halo[t][...], rows_of(b), rows_of(c), inner, inner | ~first, att, err
    )


def half_of(core, ref):
    return jnp.where(core == 0, ref[:, 0:HALF], ref[:, HALF:HD])


def add_products(where, errs, kns, gateds, slopes, acts, w, total):
    core = where[1]
    w_half = half_of(core, w)
    for e, kn, gated, slope, act in zip(errs, kns, gateds, slopes, acts, strict=True):
        back = mm_n(e[...], w_half)
        total[0] += mm_rows((back * slope[...]).astype(BF), kn[...])
        total[1] += mm_rows((back * act[...]).astype(BF), kn[...])
        total[2] += mm_rows(half_of(core, e), gated[...])


def grad_first_kernel(where, e0, e1, k0, k1, g0, g1, s0, s1, a0, a1, w, total):
    total[...] = jnp.zeros_like(total)
    add_products(where, (e0, e1), (k0, k1), (g0, g1), (s0, s1), (a0, a1), w, total)


def grad_second_kernel(
    zs, where, e0, e1, k0, k1, g0, g1, s0, s1, a0, a1, w, before, own, *rest
):
    sends, total = rest[:-1], rest[-1]
    total[...] = before[...]
    add_products(where, (e0, e1), (k0, k1), (g0, g1), (s0, s1), (a0, a1), w, total)
    rows = HALF // zs
    for d in range(zs):
        src = pl.ds(pl.multiple_of(lax.rem(where[2] + d, zs) * rows, rows), rows)
        for kind in range(3):
            if d == 0:
                own[kind] = total[kind, src, :]
            else:
                sends[d - 1][kind] = total[kind, src, :].astype(BF)


def update_kernel(zs, where, own, *rest):
    got, olds, (first, last) = rest[:-5], rest[-5:-2], rest[-2:]
    rows = HALF // zs
    mine = pl.ds(pl.multiple_of(where[1] * HALF + where[2] * rows, rows), rows)
    for kind, out in enumerate((first.at[0], first.at[1], last.at[0])):
        grad = own[kind]
        for g in got:
            grad = grad + g[kind].astype(F32)
        old = olds[kind][mine, :].astype(F32)
        raised = old - grad
        factor = jnp.sqrt(jnp.mean(old * old, -1, keepdims=True) + 1e-06) * lax.rsqrt(
            jnp.mean(raised * raised, -1, keepdims=True) + 1e-06
        )
        out[...] = (raised * factor).astype(BF)


def gather(zs, where, pieces, kinds, full):
    rows = HALF // zs
    for side, some in ((where[1], pieces[:zs]), (1 - where[1], pieces[zs:])):
        for d in range(zs):
            at = side * HALF + lax.rem(where[2] - d + zs, zs) * rows
            for kind in range(kinds):
                full[pl.ds(pl.multiple_of(kind * HD + at, rows), rows), :] = some[d][kind]


def windows(where, count, put):
    y, core, z = where[0], where[1], where[2]
    step = math.gcd(count, HD)
    for n, side in enumerate((1 - y, y)):
        first = ((z * 2 + side) * 2 + core) * count
        for c in range(count // step):
            r = first + c * step
            put(n, c * step, step, lax.div(r, 2 * HD), pl.multiple_of(lax.rem(r, HD), step))


def read_first_kernel(zs, count, where, *rest):
    pieces, (q_for, q_own) = rest[: 2 * zs], rest[2 * zs : 2 * zs + 2]
    g_for, g_own, given, kept, full = rest[2 * zs + 2 :]
    gather(zs, where, pieces, 2, full)
    outs = (given, kept)

    def put(n, to, step, kind, row):
        at = pl.multiple_of(lax.min(kind, 1) * HD + row, step)
        outs[n][to : to + step, :] = full[pl.ds(at, step), :]

    windows(where, count, put)
    for q, g in ((q_for, g_for), (q_own, g_own)):
        for c in range(2):
            rows = pl.ds(c * HALF, HALF)
            qn = rms(q[rows, :])
            hg = mm_t(qn, full[0:HD, :])
            hu = mm_t(qn, full[HD : 2 * HD, :])
            g[rows, :] = (hg * jax.nn.sigmoid(hg) * hu).astype(BF)


def read_down_kernel(zs, count, where, *rest):
    pieces = rest[: 2 * zs]
    g_for, att_low, att_up, some_given, some_kept, sent, full, kept = rest[2 * zs :]
    gather(zs, where, pieces, 1, full)
    low = where[0] == 1
    sent[0:BLK, :] = (
        jnp.where(low, att_low[...], att_up[...]).astype(F32) + mm_t(g_for[...], full[...])
    ).astype(BF)
    outs, before = (sent, kept), (some_given, some_kept)

    def put(n, to, step, kind, row):
        rows = slice(to, to + step)
        at = slice(to + BLK, to + BLK + step) if n == 0 else rows
        outs[n][at, :] = jnp.where(kind == 2, full[pl.ds(row, step), :], before[n][rows, :])

    windows(where, count, put)


def read_own_kernel(where, g_own, att_low, att_up, w, out):
    low = where[0] == 0
    out[...] = (
        jnp.where(low, att_low[...], att_up[...]).astype(F32) + mm_t(g_own[...], w[...])
    ).astype(BF)


def read_own(where, g_own, att_low, att_up, w):
    whole = pl.BlockSpec((BLK, HD), lambda i, s: (0, 0))
    return pl.pallas_call(
        read_own_kernel,
        grid_spec=pltpu.PrefetchScalarGridSpec(
            num_scalar_prefetch=1,
            grid=(1,),
            in_specs=[whole] * 4,
            out_specs=pl.BlockSpec((BLK, HD), lambda i, s: (0, s[0])),
        ),
        out_shape=shape((BLK, H * HD)),
        compiler_params=PARAMS,
        name="read_own",
    )(where, g_own, att_low, att_up, w)


def place_kernel(count, where, got, kept, half_filled, out, weights):
    y, core, z = where[0], where[1], where[2]
    out[...] = got[0:BLK, :]
    step = math.gcd(count, HD)
    first = ((z * 2 + y) * 2 + core) * count
    for c in range(count // step):
        rows = slice(c * step, (c + 1) * step)
        head = lax.rem(lax.div(first + c * step, HD), 2)
        weights[rows, :] = jnp.where(
            head == y, kept[rows, :], got[BLK + c * step : BLK + (c + 1) * step, :]
        )


def place(where, count, got, kept, half_filled):
    def whole(rows):
        return pl.BlockSpec((rows, HD), lambda i, s: (0, 0))

    return pl.pallas_call(
        functools.partial(place_kernel, count),
        grid_spec=pltpu.PrefetchScalarGridSpec(
            num_scalar_prefetch=1,
            grid=(1,),
            in_specs=[whole(BLK + count), whole(count), pl.BlockSpec(memory_space=pl.ANY)],
            out_specs=[pl.BlockSpec((BLK, HD), lambda i, s: (0, 1 - s[0])), whole(count)],
        ),
        out_shape=[shape((BLK, H * HD)), shape((count, HD))],
        input_output_aliases={3: 0},
        compiler_params=PARAMS,
        name="place",
    )(where, got, kept, half_filled)


def local(queries, key_rows, value_rows, step_rates, w_gate, w_up, w_down):
    zs = lax.axis_size("z")
    z, y, core = lax.axis_index("z"), lax.axis_index("y"), lax.axis_index("core")
    where = jnp.stack([y, core, z]).astype(jnp.int32)
    rows = HALF // zs
    count = 3 * H * HD // (4 * zs)

    def swap(value, axis):
        return lax.ppermute(value, axis, SWAP)

    def shift(value, d, ring=True):
        return lax.ppermute(
            value, "z", [(i, (i + d) % zs) for i in range(zs) if ring or i + d < zs]
        )

    two = [shape((BLK, HD))] * 2

    def after(value, earlier):
        return lax.optimization_barrier((value, earlier))[0]

    q_other = pl.BlockSpec((BLK, HD), lambda i, s: (0, 1 - s[0]))
    sent_a = pack(where, key_rows, value_rows, 0, HALF, False)
    sent_b = pack(where, after(key_rows, sent_a), value_rows, HALF, HALF, False)
    sent_q = call_blocks(
        pack_q_kernel, "pack_q", [q_other, None], [shape((BLK + RATE_ROWS, HD))]
    )(where, in_hbm(after(queries, sent_b)), step_rates)[0]
    own = pack(where, after(key_rows, sent_b), value_rows, 0, BLK, True)
    theirs = [swap(sent_a, "y"), swap(sent_b, "y")]
    q_own = jnp.where(y == 0, queries[:, :HD], queries[:, HD:])
    weights = [jnp.where(y == 0, w[:HD], w[HD:]) for w in (w_gate, w_up, w_down)]
    theirs[0], sent_q, q_own, (wg, wu, wd) = lax.optimization_barrier(
        (theirs[0], sent_q, q_own, weights)
    )
    q_for = swap(sent_q, "y")
    own2 = swap(own, "core")
    gone = pick(where, theirs[0], key_rows, value_rows, 0)
    halo_a = shift(gone, 1, ring=False)
    theirs2 = [swap(after(theirs[0], gone), "core")]
    mine = pre_own(where, own, own2, wg, wu)
    theirs[1], mine, theirs2[0] = lax.optimization_barrier((theirs[1], mine, theirs2[0]))
    gone = pick(where, theirs[1], key_rows, value_rows, 1)
    halo_b = shift(gone, 1, ring=False)
    theirs2.append(swap(after(theirs[1], gone), "core"))
    theirs2, halo_a = lax.optimization_barrier((theirs2, halo_a))
    low, high = pre(where, theirs, mine[:4], wg, wu)
    theirs2, low, q_for = lax.optimization_barrier((theirs2, low, q_for))
    low2, high2 = pre(where, theirs2, mine[4:], wg, wu)
    low2, q_for, halo = lax.optimization_barrier((low2, q_for, (halo_a, halo_b)))
    halo2 = [swap(h, "core") for h in halo]

    pair = shape((BLK, 2 * HD))
    att_up, err_up, kv_low, kv_low2 = call(
        upper_kernel, "attend_upper", two + [pair] * 2, [pltpu.VMEM(pair.shape, BF)] * 2
    )(where, q_own, q_for, step_rates, own, *theirs, own2, *theirs2)
    err_up2 = swap(err_up, "core")
    att_low, err_low = call(
        lower_kernel, "attend_lower", two, [pltpu.VMEM((BLK, 2 * HD), BF)]
    )(where, q_own, q_for, step_rates, *halo, *halo2, kv_low2, kv_low)
    err_low2 = swap(err_low, "core")

    def factors_of(*blocks):
        return [block[n] for n in range(4) for block in blocks]

    total = shape((3, HALF, HD), F32)
    before = call(grad_first_kernel, "grad_first", [total])(
        where, err_up, err_up2, *factors_of(high, high2), wd
    )[0]
    own_sum, *sends = call(
        functools.partial(grad_second_kernel, zs),
        "grad_second",
        [shape((3, rows, HD), F32)] + [shape((3, rows, HD))] * (zs - 1),
        [pltpu.VMEM(total.shape, F32)],
    )(where, err_low, err_low2, *factors_of(low, low2), wd, before)
    got = [shift(s, d) for d, s in enumerate(sends, 1)]
    piece_a, piece_b = call(
        functools.partial(update_kernel, zs),
        "update",
        [shape((2, rows, HD)), shape((1, rows, HD))],
    )(where, own_sum, *got, wg, wu, wd)

    def around(piece):
        return [piece] + [shift(piece, d) for d in range(1, zs)]

    def both(mine):
        return mine + [swap(p, "core") for p in mine]

    pieces_a = both(around(piece_a))
    pieces_b = around(piece_b)
    window = shape((count, HD))
    g_for, g_own, some_given, some_kept = call(
        functools.partial(read_first_kernel, zs, count),
        "read_first",
        two + [window] * 2,
        [pltpu.VMEM((2 * HD, HD), BF)],
    )(where, *pieces_a, q_for, q_own)
    g_for, pieces_b = lax.optimization_barrier((g_for, pieces_b))
    pieces_b = both(pieces_b)
    sent, full, kept = call(
        functools.partial(read_down_kernel, zs, count),
        "read_down",
        [shape((BLK + count, HD)), shape((HD, HD)), window],
    )(where, *pieces_b, g_for, att_low, att_up, some_given, some_kept)
    got_out = swap(sent, "y")
    half_filled = read_own(where, g_own, att_low, att_up, full)
    return tuple(place(where, count, got_out, kept, half_filled))


def solution(mesh):
    groups, ctx = mesh.devices.shape
    split = Mesh(mesh.devices.reshape(groups, ctx // 4, 2, 2), ("groups", "z", "y", "core"))
    tokens = ("groups", "z", "y", "core")
    return jax.shard_map(
        local,
        mesh=split,
        in_specs=(
            P(tokens, None),
            P(tokens, None),
            P(tokens, None),
            P(None, tokens),
            P("groups", None),
            P("groups", None),
            P("groups", None),
        ),
        out_specs=(P(tokens, None), P(tokens, None)),
        check_vma=False,
    )
```

```python
import functools
import math

import jax
import jax.numpy as jnp
from jax import lax
from jax.experimental import pallas as pl
from jax.experimental.pallas import tpu as pltpu
from jax.sharding import Mesh, PartitionSpec as P

H = 2
HD = 512
BLK = 512
HALF = 256
RATE_ROWS = 16
BF = jnp.bfloat16
F32 = jnp.float32
SWAP = [(0, 1), (1, 0)]
PARAMS = pltpu.CompilerParams(vmem_limit_bytes=20 << 20)
VM = pl.BlockSpec(memory_space=pltpu.VMEM)
SM = pl.BlockSpec(memory_space=pltpu.SMEM)


def mm(a, b, dims):
    return lax.dot_general(a, b, (dims, ((), ())), preferred_element_type=F32)


def mm_t(a, b):
    return mm(a, b, ((1,), (1,)))


def mm_n(a, b):
    return mm(a, b, ((1,), (0,)))


def mm_rows(a, b):
    return mm(a, b, ((0,), (0,)))


def rms(x):
    v = x.astype(F32)
    return (v * lax.rsqrt(jnp.mean(v * v, -1, keepdims=True) + 1e-06)).astype(BF)


def in_hbm(value):
    return pltpu.with_memory_space_constraint(value, pltpu.HBM)


def shape(dims, dtype=BF):
    return jax.ShapeDtypeStruct(dims, dtype)


def call(kernel, name, outs, scratch=()):
    def run(where, *args):
        return pl.pallas_call(
            kernel,
            in_specs=[SM] + [VM] * len(args),
            out_specs=[VM] * len(outs),
            out_shape=outs,
            scratch_shapes=scratch,
            compiler_params=PARAMS,
            name=name,
        )(where, *args)

    return run


def call_blocks(kernel, name, specs, outs, scratch=()):
    def run(where, *args):
        def whole(dims):
            return pl.BlockSpec(dims, lambda i, s: (0,) * len(dims))

        in_specs = [whole(a.shape) if p is None else p for a, p in zip(args, specs, strict=True)]
        return pl.pallas_call(
            kernel,
            grid_spec=pltpu.PrefetchScalarGridSpec(
                num_scalar_prefetch=1,
                grid=(1,),
                in_specs=in_specs,
                out_specs=[whole(o.shape) for o in outs],
                scratch_shapes=scratch,
            ),
            out_shape=outs,
            compiler_params=PARAMS,
            name=name,
        )(where, *args)

    return run


def pack_kernel(first, count, own, where, key, value, out, sems):
    column = where[0] if own else 1 - where[0]
    source = (pl.ds(first, count), pl.ds(pl.multiple_of(column * HD, HD), HD))
    copies = [
        pltpu.make_async_copy(ref.at[source], out.at[:, pl.ds(n * HD, HD)], sems.at[n])
        for n, ref in enumerate((key, value))
    ]
    for copy in copies:
        copy.start()
    for copy in copies:
        copy.wait()


def pack(where, key_rows, value_rows, first, count, own):
    return pl.pallas_call(
        functools.partial(pack_kernel, first, count, own),
        in_specs=[SM] + [pl.BlockSpec(memory_space=pl.ANY)] * 2,
        out_specs=VM,
        out_shape=shape((count, 2 * HD)),
        scratch_shapes=[pltpu.SemaphoreType.DMA((2,))],
        compiler_params=PARAMS,
        name="pack",
    )(where, in_hbm(key_rows), in_hbm(value_rows))


def pick_kernel(n, where, foreign, own, out):
    out[...] = jnp.where(where[0] == 0, foreign[...], own[n * HALF : (n + 1) * HALF, :])


def pick(where, foreign, own, n):
    return call(functools.partial(pick_kernel, n), "pick", [shape((HALF, 2 * HD))])(
        where, foreign, own
    )[0]


def pack_q_kernel(where, query, rates, sent):
    sent[0:BLK, :] = query[...]
    rate = jnp.where(where[0] == 0, rates[1:2, :], rates[0:1, :])
    parts = []
    for _ in range(3):
        part = rate.astype(BF)
        parts.append(part)
        rate = rate - part.astype(F32)
    row = lax.broadcasted_iota(jnp.int32, (RATE_ROWS, BLK), 0)
    tail = jnp.zeros((RATE_ROWS, BLK), F32)
    for n, part in enumerate(parts):
        tail = jnp.where(row == n, part.astype(F32), tail)
    sent[BLK : BLK + RATE_ROWS, :] = tail.astype(BF)


def factors(core, key, wg, wu, put):
    for c in range(2):
        rows = pl.ds(c * HALF, HALF)
        kc = rms(key(c))
        put(0, rows, slice(None), kc)
        for side in range(2):
            units = pl.ds(side * HALF, HALF)
            hg = mm_t(kc, wg[units, :])
            hu = mm_t(kc, wu[units, :])
            sig = jax.nn.sigmoid(hg)
            a = hg * sig
            put(1, rows, units, (a * hu).astype(BF))

            @pl.when(core == side)
            def _():
                put(2, rows, slice(None), hu * sig * (1.0 + hg * (1.0 - sig)))
                put(3, rows, slice(None), a)


def pre_own_kernel(where, own, own2, wg, wu, *outs):
    for n, kv in enumerate((own, own2)):

        def put(i, rows, columns, value):
            outs[4 * n + i][rows, columns] = value

        factors(where[1], lambda c: kv[c * HALF : (c + 1) * HALF, 0:HD], wg, wu, put)


def pick_factors(where, halves, mine, wg, wu, outs, work):
    def put(i, rows, columns, value):
        work[i][rows, columns] = value

    factors(where[1], lambda c: halves[c][:, 0:HD], wg, wu, put)
    bottom = where[0] == 0
    for i in range(4):
        outs[i][...] = jnp.where(bottom, mine[i][...], work[i][...])
        outs[4 + i][...] = jnp.where(bottom, work[i][...], mine[i][...])


def pre_kernel(where, *rest):
    pick_factors(where, rest[:2], rest[2:6], *rest[6:8], rest[8:16], rest[16:])


FACTORS = [
    shape((BLK, HD)),
    shape((BLK, HD)),
    shape((BLK, HALF), F32),
    shape((BLK, HALF), F32),
]


def pre_own(where, own, own2, wg, wu):
    return call(pre_own_kernel, "pre_own", FACTORS * 2)(where, own, own2, wg, wu)


def pre(where, halves, mine, wg, wu):
    work = [pltpu.VMEM(f.shape, f.dtype) for f in FACTORS]
    outs = call(pre_kernel, "pre", FACTORS * 2, work)(where, *halves, *mine, wg, wu)
    return outs[:4], outs[4:]


def attend(q, rate, tile_a, tile_b, tile_c, a_ok, b_ok, att, err):
    scale = 1.0 / math.sqrt(HD)
    p = lax.broadcasted_iota(jnp.int32, (HALF, HALF), 0)
    j = lax.broadcasted_iota(jnp.int32, (HALF, HALF), 1)
    causal = j <= p
    neg = jnp.float32(-jnp.inf)
    zero = jnp.zeros((HALF, HALF), BF)

    def key(tile):
        return tile[:, 0:HD]

    def value(tile):
        return tile[:, HD : 2 * HD]

    for c in range(2):
        rows = pl.ds(c * HALF, HALF)
        qc = q(rows)
        tiles = []
        for t in range(2):
            if t <= c:
                sc = mm_t(qc, key(tile_c(t))) * scale
            if t >= c:
                sa = mm_t(qc, key(tile_a(t))) * scale
                if a_ok is not None:
                    sa = jnp.where(a_ok, sa, neg)
            tiles.append(sc if t < c else sa if t > c else jnp.where(causal, sc, sa))
        for t in range(2):
            sb = mm_t(qc, key(tile_b(t))) * scale
            tiles.append(sb if b_ok is None else jnp.where(b_ok, sb, neg))
        top = functools.reduce(jnp.maximum, [jnp.max(s, -1, keepdims=True) for s in tiles])
        expo = [jnp.exp(s - top) for s in tiles]
        total = functools.reduce(jnp.add, [jnp.sum(e, -1, keepdims=True) for e in expo])
        inv = 1.0 / total
        w = [(e * inv).astype(BF) for e in expo]
        acc = mm_n(w[2], value(tile_b(0))) + mm_n(w[3], value(tile_b(1)))
        for t in range(2):
            if t <= c:
                acc += mm_n(
                    jnp.where(causal, w[t], zero) if t == c else w[t], value(tile_c(t))
                )
            if t >= c:
                acc += mm_n(
                    jnp.where(causal, zero, w[t]) if t == c else w[t], value(tile_a(t))
                )
        out = acc.astype(BF)
        att[rows, :] = out
        err[rows, :] = (-rate[c * HALF : (c + 1) * HALF] * out.astype(F32)).astype(BF)


def column(mine, side, rates, q_for):
    parts = q_for[BLK : BLK + RATE_ROWS, :].astype(F32)
    other = parts[0:1, :] + parts[1:2, :] + parts[2:3, :]
    own = jnp.where(side == 0, rates[0:1, :], rates[1:2, :])
    line = jnp.where(mine, own, other)
    return jnp.transpose(jnp.broadcast_to(line, (8, BLK)))[:, 0:1]


def rows_of(ref):
    return lambda t: ref[t * HALF : (t + 1) * HALF, :]


def upper_kernel(
    where, q_own, q_for, rates, own, for_a, for_b, own2, for2_a, for2_b, *rest
):
    att, err, low, low2, high, mid = rest
    bottom = where[0] == 0
    first = where[1] == 0
    for c, (f, f2) in enumerate(((for_a, for2_a), (for_b, for2_b))):
        rows = pl.ds(c * HALF, HALF)
        low[rows, :] = jnp.where(bottom, own[rows, :], f[...])
        high[rows, :] = jnp.where(bottom, f[...], own[rows, :])
        l2 = jnp.where(bottom, own2[rows, :], f2[...])
        low2[rows, :] = l2
        mid[rows, :] = jnp.where(first, l2, jnp.where(bottom, f2[...], own2[rows, :]))
    mine = where[0] == 1
    q = lambda rows: jnp.where(mine, q_own[rows, :], q_for[rows, :])
    r = column(mine, where[0], rates, q_for)
    attend(q, r, rows_of(low), rows_of(mid), rows_of(high), None, None, att, err)


def lower_kernel(
    where, q_own, q_for, rates, halo_a, halo_b, halo2_a, halo2_b, low2, c, att, err, b
):
    mine = where[0] == 0
    first = where[1] == 0
    inner = where[2] > 0
    for t, h in enumerate((halo2_a, halo2_b)):
        rows = pl.ds(t * HALF, HALF)
        b[rows, :] = jnp.where(first, h[...], low2[rows, :])
    q = lambda rows: jnp.where(mine, q_own[rows, :], q_for[rows, :])
    r = column(mine, where[0], rates, q_for)
    halo = (halo_a, halo_b)
    attend(
        q, r, lambda t: halo[t][...], rows_of(b), rows_of(c), inner, inner | ~first, att, err
    )


def half_of(core, ref):
    return jnp.where(core == 0, ref[:, 0:HALF], ref[:, HALF:HD])


def add_products(where, errs, kns, gateds, slopes, acts, w, total):
    core = where[1]
    w_half = half_of(core, w)
    for e, kn, gated, slope, act in zip(errs, kns, gateds, slopes, acts, strict=True):
        back = mm_n(e[...], w_half)
        total[0] += mm_rows((back * slope[...]).astype(BF), kn[...])
        total[1] += mm_rows((back * act[...]).astype(BF), kn[...])
        total[2] += mm_rows(half_of(core, e), gated[...])


def grad_first_kernel(where, e0, e1, k0, k1, g0, g1, s0, s1, a0, a1, w, total):
    total[...] = jnp.zeros_like(total)
    add_products(where, (e0, e1), (k0, k1), (g0, g1), (s0, s1), (a0, a1), w, total)


def grad_second_kernel(
    zs, where, e0, e1, k0, k1, g0, g1, s0, s1, a0, a1, w, before, own, *rest
):
    sends, total = rest[:-1], rest[-1]
    total[...] = before[...]
    add_products(where, (e0, e1), (k0, k1), (g0, g1), (s0, s1), (a0, a1), w, total)
    rows = HALF // zs
    for d in range(zs):
        src = pl.ds(pl.multiple_of(lax.rem(where[2] + d, zs) * rows, rows), rows)
        for kind in range(3):
            if d == 0:
                own[kind] = total[kind, src, :]
            else:
                sends[d - 1][kind] = total[kind, src, :].astype(BF)


def update_kernel(zs, where, own, *rest):
    got, olds, (first, last, placed) = rest[:-6], rest[-6:-3], rest[-3:]
    rows = HALF // zs
    at = where[1] * HALF + where[2] * rows
    mine = pl.ds(pl.multiple_of(at, rows), rows)
    number = where[0] * 2 * zs + where[1] * zs + where[2]
    for kind, out in enumerate((first.at[0], first.at[1], last.at[0])):
        grad = own[kind]
        for g in got:
            grad = grad + g[kind].astype(F32)
        old = olds[kind][mine, :].astype(F32)
        raised = old - grad
        factor = jnp.sqrt(jnp.mean(old * old, -1, keepdims=True) + 1e-06) * lax.rsqrt(
            jnp.mean(raised * raised, -1, keepdims=True) + 1e-06
        )
        new = (raised * factor).astype(BF)
        out[...] = new
        placed[lax.rem(kind * 4 * zs + number, 3)] = new


def owners(zs, slot):
    pairs = []
    for owner in range(4 * zs):
        head, piece = divmod((3 * owner + slot) % (4 * zs), 2 * zs)
        core, z = divmod(piece, zs)
        pairs.append(((z * 2 + head) * 2 + core, owner))
    return pairs


def gather(zs, where, pieces, kinds, full):
    rows = HALF // zs
    for side, some in ((where[1], pieces[:zs]), (1 - where[1], pieces[zs:])):
        for d in range(zs):
            at = side * HALF + lax.rem(where[2] - d + zs, zs) * rows
            for kind in range(kinds):
                full[pl.ds(pl.multiple_of(kind * HD + at, rows), rows), :] = some[d][kind]


def read_first_kernel(zs, where, *rest):
    pieces, (q_for, q_own, g_for, g_own, full) = rest[: 2 * zs], rest[2 * zs :]
    gather(zs, where, pieces, 2, full)
    for q, g in ((q_for, g_for), (q_own, g_own)):
        for c in range(2):
            rows = pl.ds(c * HALF, HALF)
            qn = rms(q[rows, :])
            hg = mm_t(qn, full[0:HD, :])
            hu = mm_t(qn, full[HD : 2 * HD, :])
            g[rows, :] = (hg * jax.nn.sigmoid(hg) * hu).astype(BF)


def read_down_kernel(zs, where, *rest):
    pieces = rest[: 2 * zs]
    g_for, att_low, att_up, out, full = rest[2 * zs :]
    gather(zs, where, pieces, 1, full)
    low = where[0] == 1
    out[...] = (
        jnp.where(low, att_low[...], att_up[...]).astype(F32) + mm_t(g_for[...], full[...])
    ).astype(BF)


def read_own_kernel(where, g_own, att_low, att_up, w, out):
    low = where[0] == 0
    out[...] = (
        jnp.where(low, att_low[...], att_up[...]).astype(F32) + mm_t(g_own[...], w[...])
    ).astype(BF)


def read_own(where, g_own, att_low, att_up, w):
    whole = pl.BlockSpec((BLK, HD), lambda i, s: (0, 0))
    return pl.pallas_call(
        read_own_kernel,
        grid_spec=pltpu.PrefetchScalarGridSpec(
            num_scalar_prefetch=1,
            grid=(1,),
            in_specs=[whole] * 4,
            out_specs=pl.BlockSpec((BLK, HD), lambda i, s: (0, s[0])),
        ),
        out_shape=shape((BLK, H * HD)),
        compiler_params=PARAMS,
        name="read_own",
    )(where, g_own, att_low, att_up, w)


def place_kernel(where, got, half_filled, out, sem):
    column = pl.ds(pl.multiple_of((1 - where[0]) * HD, HD), HD)
    copy = pltpu.make_async_copy(got, out.at[:, column], sem)
    copy.start()
    copy.wait()


def place(where, got, half_filled):
    anyspec = pl.BlockSpec(memory_space=pl.ANY)
    return pl.pallas_call(
        place_kernel,
        in_specs=[SM, VM, anyspec],
        out_specs=anyspec,
        out_shape=shape((BLK, H * HD)),
        scratch_shapes=[pltpu.SemaphoreType.DMA],
        input_output_aliases={2: 0},
        compiler_params=PARAMS,
        name="place",
    )(where, got, half_filled)


def local(queries, key_rows, value_rows, step_rates, w_gate, w_up, w_down):
    zs = lax.axis_size("z")
    z, y, core = lax.axis_index("z"), lax.axis_index("y"), lax.axis_index("core")
    where = jnp.stack([y, core, z]).astype(jnp.int32)
    rows = HALF // zs

    def swap(value, axis):
        return lax.ppermute(value, axis, SWAP)

    def shift(value, d, ring=True):
        return lax.ppermute(
            value, "z", [(i, (i + d) % zs) for i in range(zs) if ring or i + d < zs]
        )

    two = [shape((BLK, HD))] * 2

    def after(value, earlier):
        return lax.optimization_barrier((value, earlier))[0]

    q_other = pl.BlockSpec((BLK, HD), lambda i, s: (0, 1 - s[0]))
    sent_a = pack(where, key_rows, value_rows, 0, HALF, False)
    sent_b = pack(where, after(key_rows, sent_a), value_rows, HALF, HALF, False)
    sent_q = call_blocks(
        pack_q_kernel, "pack_q", [q_other, None], [shape((BLK + RATE_ROWS, HD))]
    )(where, in_hbm(after(queries, sent_b)), step_rates)[0]
    own = pack(where, after(key_rows, sent_b), value_rows, 0, BLK, True)
    theirs = [swap(sent_a, "y"), swap(sent_b, "y")]
    q_own = jnp.where(y == 0, queries[:, :HD], queries[:, HD:])
    weights = [jnp.where(y == 0, w[:HD], w[HD:]) for w in (w_gate, w_up, w_down)]
    theirs[0], sent_q, q_own, (wg, wu, wd) = lax.optimization_barrier(
        (theirs[0], sent_q, q_own, weights)
    )
    q_for = swap(sent_q, "y")
    own2 = swap(own, "core")
    gone = pick(where, theirs[0], own, 0)
    halo_a = shift(gone, 1, ring=False)
    theirs2 = [swap(after(theirs[0], gone), "core")]
    mine = pre_own(where, own, own2, wg, wu)
    theirs[1], mine, theirs2[0] = lax.optimization_barrier((theirs[1], mine, theirs2[0]))
    gone = pick(where, theirs[1], own, 1)
    halo_b = shift(gone, 1, ring=False)
    theirs2.append(swap(after(theirs[1], gone), "core"))
    theirs2, halo_a = lax.optimization_barrier((theirs2, halo_a))
    low, high = pre(where, theirs, mine[:4], wg, wu)
    theirs2, low, q_for = lax.optimization_barrier((theirs2, low, q_for))
    low2, high2 = pre(where, theirs2, mine[4:], wg, wu)
    low2, q_for = lax.optimization_barrier((low2, q_for))

    pair = shape((BLK, 2 * HD))
    att_up, err_up, kv_low, kv_low2 = call(
        upper_kernel, "attend_upper", two + [pair] * 2, [pltpu.VMEM(pair.shape, BF)] * 2
    )(where, q_own, q_for, step_rates, own, *theirs, own2, *theirs2)
    err_up, halo = lax.optimization_barrier((err_up, (halo_a, halo_b)))
    halo2 = [swap(h, "core") for h in halo]
    err_up2 = swap(err_up, "core")
    att_low, err_low = call(
        lower_kernel, "attend_lower", two, [pltpu.VMEM((BLK, 2 * HD), BF)]
    )(where, q_own, q_for, step_rates, *halo, *halo2, kv_low2, kv_low)
    err_low2 = swap(err_low, "core")

    def factors_of(*blocks):
        return [block[n] for n in range(4) for block in blocks]

    total = shape((3, HALF, HD), F32)
    before = call(grad_first_kernel, "grad_first", [total])(
        where, err_up, err_up2, *factors_of(high, high2), wd
    )[0]
    own_sum, *sends = call(
        functools.partial(grad_second_kernel, zs),
        "grad_second",
        [shape((3, rows, HD), F32)] + [shape((3, rows, HD))] * (zs - 1),
        [pltpu.VMEM(total.shape, F32)],
    )(where, err_low, err_low2, *factors_of(low, low2), wd, before)
    got = [shift(s, d) for d, s in enumerate(sends, 1)]
    piece_a, piece_b, placed = call(
        functools.partial(update_kernel, zs),
        "update",
        [shape((2, rows, HD)), shape((1, rows, HD)), shape((3, rows, HD))],
    )(where, own_sum, *got, wg, wu, wd)

    def around(piece):
        return [piece] + [shift(piece, d) for d in range(1, zs)]

    def both(mine):
        return mine + [swap(p, "core") for p in mine]

    pieces_a = both(around(piece_a))
    pieces_b = around(piece_b)
    g_for, g_own = call(
        functools.partial(read_first_kernel, zs), "read_first", two, [pltpu.VMEM((2 * HD, HD), BF)]
    )(where, *pieces_a, q_for, q_own)
    own_rows = [
        lax.ppermute(placed[slot], ("z", "y", "core"), owners(zs, slot)) for slot in range(3)
    ]
    g_for, pieces_b = lax.optimization_barrier((g_for, pieces_b))
    pieces_b = both(pieces_b)
    out_for, full = call(
        functools.partial(read_down_kernel, zs), "read_down", [shape((BLK, HD)), shape((HD, HD))]
    )(where, *pieces_b, g_for, att_low, att_up)
    out_got = swap(out_for, "y")
    half_filled = read_own(where, g_own, att_low, att_up, full)
    half_filled, own_rows = lax.optimization_barrier((half_filled, own_rows))
    return place(where, out_got, half_filled), jnp.concatenate(own_rows, 0)


def solution(mesh):
    groups, ctx = mesh.devices.shape
    split = Mesh(mesh.devices.reshape(groups, ctx // 4, 2, 2), ("groups", "z", "y", "core"))
    tokens = ("groups", "z", "y", "core")
    return jax.shard_map(
        local,
        mesh=split,
        in_specs=(
            P(tokens, None),
            P(tokens, None),
            P(tokens, None),
            P(None, tokens),
            P("groups", None),
            P("groups", None),
            P("groups", None),
        ),
        out_specs=(P(tokens, None), P(tokens, None)),
        check_vma=False,
    )
```

```python
import functools
import math

import jax
import jax.numpy as jnp
from jax import lax
from jax.experimental import pallas as pl
from jax.experimental.pallas import tpu as pltpu
from jax.sharding import Mesh, PartitionSpec as P

H = 2
HD = 512
BLK = 512
HALF = 256
RATE_ROWS = 16
BF = jnp.bfloat16
F32 = jnp.float32
SWAP = [(0, 1), (1, 0)]
PARAMS = pltpu.CompilerParams(vmem_limit_bytes=20 << 20)
VM = pl.BlockSpec(memory_space=pltpu.VMEM)
SM = pl.BlockSpec(memory_space=pltpu.SMEM)


def mm(a, b, dims):
    return lax.dot_general(a, b, (dims, ((), ())), preferred_element_type=F32)


def mm_t(a, b):
    return mm(a, b, ((1,), (1,)))


def mm_n(a, b):
    return mm(a, b, ((1,), (0,)))


def mm_rows(a, b):
    return mm(a, b, ((0,), (0,)))


def rms(x):
    v = x.astype(F32)
    return (v * lax.rsqrt(jnp.mean(v * v, -1, keepdims=True) + 1e-06)).astype(BF)


def in_hbm(value):
    return pltpu.with_memory_space_constraint(value, pltpu.HBM)


def shape(dims, dtype=BF):
    return jax.ShapeDtypeStruct(dims, dtype)


def call(kernel, name, outs, scratch=()):
    def run(where, *args):
        return pl.pallas_call(
            kernel,
            in_specs=[SM] + [VM] * len(args),
            out_specs=[VM] * len(outs),
            out_shape=outs,
            scratch_shapes=scratch,
            compiler_params=PARAMS,
            name=name,
        )(where, *args)

    return run


def call_blocks(kernel, name, specs, outs, scratch=()):
    def run(where, *args):
        def whole(dims):
            return pl.BlockSpec(dims, lambda i, s: (0,) * len(dims))

        in_specs = [whole(a.shape) if p is None else p for a, p in zip(args, specs, strict=True)]
        return pl.pallas_call(
            kernel,
            grid_spec=pltpu.PrefetchScalarGridSpec(
                num_scalar_prefetch=1,
                grid=(1,),
                in_specs=in_specs,
                out_specs=[whole(o.shape) for o in outs],
                scratch_shapes=scratch,
            ),
            out_shape=outs,
            compiler_params=PARAMS,
            name=name,
        )(where, *args)

    return run


def pack_kernel(first, count, own, where, key, value, out, sems):
    column = where[0] if own else 1 - where[0]
    source = (pl.ds(first, count), pl.ds(pl.multiple_of(column * HD, HD), HD))
    copies = [
        pltpu.make_async_copy(ref.at[source], out.at[:, pl.ds(n * HD, HD)], sems.at[n])
        for n, ref in enumerate((key, value))
    ]
    for copy in copies:
        copy.start()
    for copy in copies:
        copy.wait()


def pack(where, key_rows, value_rows, first, count, own):
    return pl.pallas_call(
        functools.partial(pack_kernel, first, count, own),
        in_specs=[SM] + [pl.BlockSpec(memory_space=pl.ANY)] * 2,
        out_specs=VM,
        out_shape=shape((count, 2 * HD)),
        scratch_shapes=[pltpu.SemaphoreType.DMA((2,))],
        compiler_params=PARAMS,
        name="pack",
    )(where, in_hbm(key_rows), in_hbm(value_rows))


def pick_kernel(n, where, foreign, own, out):
    out[...] = jnp.where(where[0] == 0, foreign[...], own[n * HALF : (n + 1) * HALF, :])


def pick(where, foreign, own, n):
    return call(functools.partial(pick_kernel, n), "pick", [shape((HALF, 2 * HD))])(
        where, foreign, own
    )[0]


def pack_q_kernel(where, query, rates, sent):
    sent[0:BLK, :] = query[...]
    rate = jnp.where(where[0] == 0, rates[1:2, :], rates[0:1, :])
    parts = []
    for _ in range(3):
        part = rate.astype(BF)
        parts.append(part)
        rate = rate - part.astype(F32)
    row = lax.broadcasted_iota(jnp.int32, (RATE_ROWS, BLK), 0)
    tail = jnp.zeros((RATE_ROWS, BLK), F32)
    for n, part in enumerate(parts):
        tail = jnp.where(row == n, part.astype(F32), tail)
    sent[BLK : BLK + RATE_ROWS, :] = tail.astype(BF)


def factors(core, key, wg, wu, put):
    for c in range(2):
        rows = pl.ds(c * HALF, HALF)
        kc = rms(key(c))
        put(0, rows, slice(None), kc)
        for side in range(2):
            units = pl.ds(side * HALF, HALF)
            hg = mm_t(kc, wg[units, :])
            hu = mm_t(kc, wu[units, :])
            sig = jax.nn.sigmoid(hg)
            a = hg * sig
            put(1, rows, units, (a * hu).astype(BF))

            @pl.when(core == side)
            def _():
                put(2, rows, slice(None), hu * sig * (1.0 + hg * (1.0 - sig)))
                put(3, rows, slice(None), a)


def pre_own_kernel(where, own, own2, wg, wu, *outs):
    for n, kv in enumerate((own, own2)):

        def put(i, rows, columns, value):
            outs[4 * n + i][rows, columns] = value

        factors(where[1], lambda c: kv[c * HALF : (c + 1) * HALF, 0:HD], wg, wu, put)


def pick_factors(where, halves, mine, wg, wu, outs, work):
    def put(i, rows, columns, value):
        work[i][rows, columns] = value

    factors(where[1], lambda c: halves[c][:, 0:HD], wg, wu, put)
    bottom = where[0] == 0
    for i in range(4):
        outs[i][...] = jnp.where(bottom, mine[i][...], work[i][...])
        outs[4 + i][...] = jnp.where(bottom, work[i][...], mine[i][...])


def pre_kernel(where, *rest):
    pick_factors(where, rest[:2], rest[2:6], *rest[6:8], rest[8:16], rest[16:])


FACTORS = [
    shape((BLK, HD)),
    shape((BLK, HD)),
    shape((BLK, HALF), F32),
    shape((BLK, HALF), F32),
]


def pre_own(where, own, own2, wg, wu):
    return call(pre_own_kernel, "pre_own", FACTORS * 2)(where, own, own2, wg, wu)


def pre(where, halves, mine, wg, wu):
    work = [pltpu.VMEM(f.shape, f.dtype) for f in FACTORS]
    outs = call(pre_kernel, "pre", FACTORS * 2, work)(where, *halves, *mine, wg, wu)
    return outs[:4], outs[4:]


def attend(q, rate, tile_a, tile_b, tile_c, a_ok, b_ok, att, err):
    scale = 1.0 / math.sqrt(HD)
    p = lax.broadcasted_iota(jnp.int32, (HALF, HALF), 0)
    j = lax.broadcasted_iota(jnp.int32, (HALF, HALF), 1)
    causal = j <= p
    neg = jnp.float32(-jnp.inf)
    zero = jnp.zeros((HALF, HALF), BF)

    def key(tile):
        return tile[:, 0:HD]

    def value(tile):
        return tile[:, HD : 2 * HD]

    for c in range(2):
        rows = pl.ds(c * HALF, HALF)
        qc = q(rows)
        tiles = []
        for t in range(2):
            if t <= c:
                sc = mm_t(qc, key(tile_c(t))) * scale
            if t >= c:
                sa = mm_t(qc, key(tile_a(t))) * scale
                if a_ok is not None:
                    sa = jnp.where(a_ok, sa, neg)
            tiles.append(sc if t < c else sa if t > c else jnp.where(causal, sc, sa))
        for t in range(2):
            sb = mm_t(qc, key(tile_b(t))) * scale
            tiles.append(sb if b_ok is None else jnp.where(b_ok, sb, neg))
        top = functools.reduce(jnp.maximum, [jnp.max(s, -1, keepdims=True) for s in tiles])
        expo = [jnp.exp(s - top) for s in tiles]
        total = functools.reduce(jnp.add, [jnp.sum(e, -1, keepdims=True) for e in expo])
        inv = 1.0 / total
        w = [(e * inv).astype(BF) for e in expo]
        acc = mm_n(w[2], value(tile_b(0))) + mm_n(w[3], value(tile_b(1)))
        for t in range(2):
            if t <= c:
                acc += mm_n(
                    jnp.where(causal, w[t], zero) if t == c else w[t], value(tile_c(t))
                )
            if t >= c:
                acc += mm_n(
                    jnp.where(causal, zero, w[t]) if t == c else w[t], value(tile_a(t))
                )
        out = acc.astype(BF)
        att[rows, :] = out
        err[rows, :] = (-rate[c * HALF : (c + 1) * HALF] * out.astype(F32)).astype(BF)


def column(mine, side, rates, q_for):
    parts = q_for[BLK : BLK + RATE_ROWS, :].astype(F32)
    other = parts[0:1, :] + parts[1:2, :] + parts[2:3, :]
    own = jnp.where(side == 0, rates[0:1, :], rates[1:2, :])
    line = jnp.where(mine, own, other)
    return jnp.transpose(jnp.broadcast_to(line, (8, BLK)))[:, 0:1]


def rows_of(ref):
    return lambda t: ref[t * HALF : (t + 1) * HALF, :]


def upper_kernel(
    where, q_own, q_for, rates, own, for_a, for_b, own2, for2_a, for2_b, *rest
):
    att, err, low, low2, high, mid = rest
    bottom = where[0] == 0
    first = where[1] == 0
    for c, (f, f2) in enumerate(((for_a, for2_a), (for_b, for2_b))):
        rows = pl.ds(c * HALF, HALF)
        low[rows, :] = jnp.where(bottom, own[rows, :], f[...])
        high[rows, :] = jnp.where(bottom, f[...], own[rows, :])
        l2 = jnp.where(bottom, own2[rows, :], f2[...])
        low2[rows, :] = l2
        mid[rows, :] = jnp.where(first, l2, jnp.where(bottom, f2[...], own2[rows, :]))
    mine = where[0] == 1
    q = lambda rows: jnp.where(mine, q_own[rows, :], q_for[rows, :])
    r = column(mine, where[0], rates, q_for)
    attend(q, r, rows_of(low), rows_of(mid), rows_of(high), None, None, att, err)


def lower_kernel(
    where, q_own, q_for, rates, halo_a, halo_b, halo2_a, halo2_b, low2, c, att, err, b
):
    mine = where[0] == 0
    first = where[1] == 0
    inner = where[2] > 0
    for t, h in enumerate((halo2_a, halo2_b)):
        rows = pl.ds(t * HALF, HALF)
        b[rows, :] = jnp.where(first, h[...], low2[rows, :])
    q = lambda rows: jnp.where(mine, q_own[rows, :], q_for[rows, :])
    r = column(mine, where[0], rates, q_for)
    halo = (halo_a, halo_b)
    attend(
        q, r, lambda t: halo[t][...], rows_of(b), rows_of(c), inner, inner | ~first, att, err
    )


def half_of(core, ref):
    return jnp.where(core == 0, ref[:, 0:HALF], ref[:, HALF:HD])


def add_products(where, errs, kns, gateds, slopes, acts, w, total):
    core = where[1]
    w_half = half_of(core, w)
    for e, kn, gated, slope, act in zip(errs, kns, gateds, slopes, acts, strict=True):
        back = mm_n(e[...], w_half)
        total[0] += mm_rows((back * slope[...]).astype(BF), kn[...])
        total[1] += mm_rows((back * act[...]).astype(BF), kn[...])
        total[2] += mm_rows(half_of(core, e), gated[...])


def grad_first_kernel(where, e0, e1, k0, k1, g0, g1, s0, s1, a0, a1, w, total):
    total[...] = jnp.zeros_like(total)
    add_products(where, (e0, e1), (k0, k1), (g0, g1), (s0, s1), (a0, a1), w, total)


def grad_second_kernel(
    zs, where, e0, e1, k0, k1, g0, g1, s0, s1, a0, a1, w, before, own, *rest
):
    sends, total = rest[:-1], rest[-1]
    total[...] = before[...]
    add_products(where, (e0, e1), (k0, k1), (g0, g1), (s0, s1), (a0, a1), w, total)
    rows = HALF // zs
    for d in range(zs):
        src = pl.ds(pl.multiple_of(lax.rem(where[2] + d, zs) * rows, rows), rows)
        for kind in range(3):
            if d == 0:
                own[kind] = total[kind, src, :]
            else:
                sends[d - 1][kind] = total[kind, src, :].astype(BF)


def update_kernel(zs, where, own, *rest):
    got, olds, (piece, placed) = rest[:-5], rest[-5:-2], rest[-2:]
    rows = HALF // zs
    at = where[1] * HALF + where[2] * rows
    mine = pl.ds(pl.multiple_of(at, rows), rows)
    number = where[0] * 2 * zs + where[1] * zs + where[2]
    for kind in range(3):
        grad = own[kind]
        for g in got:
            grad = grad + g[kind].astype(F32)
        old = olds[kind][mine, :].astype(F32)
        raised = old - grad
        factor = jnp.sqrt(jnp.mean(old * old, -1, keepdims=True) + 1e-06) * lax.rsqrt(
            jnp.mean(raised * raised, -1, keepdims=True) + 1e-06
        )
        new = (raised * factor).astype(BF)
        piece[kind] = new
        placed[lax.rem(kind * 4 * zs + number, 3)] = new


def owners(zs, slot):
    pairs = []
    for owner in range(4 * zs):
        head, piece = divmod((3 * owner + slot) % (4 * zs), 2 * zs)
        core, z = divmod(piece, zs)
        pairs.append(((z * 2 + head) * 2 + core, owner))
    return pairs


def gather(zs, where, pieces, kinds, full):
    rows = HALF // zs
    for side, some in ((where[1], pieces[:zs]), (1 - where[1], pieces[zs:])):
        for d in range(zs):
            at = side * HALF + lax.rem(where[2] - d + zs, zs) * rows
            for kind in range(kinds):
                full[pl.ds(pl.multiple_of(kind * HD + at, rows), rows), :] = some[d][kind]


def read(q, att, full, out):
    for c in range(2):
        rows = pl.ds(c * HALF, HALF)
        qn = rms(q[rows, :])
        hg = mm_t(qn, full[0:HD, :])
        hu = mm_t(qn, full[HD : 2 * HD, :])
        g = (hg * jax.nn.sigmoid(hg) * hu).astype(BF)
        out[rows, :] = (att(rows).astype(F32) + mm_t(g, full[2 * HD : 3 * HD, :])).astype(BF)


def read_foreign_kernel(zs, where, *rest):
    pieces, (q, att_low, att_up, out, full) = rest[: 2 * zs], rest[2 * zs :]
    gather(zs, where, pieces, 3, full)
    low = where[0] == 1
    read(q, lambda rows: jnp.where(low, att_low[rows, :], att_up[rows, :]), full, out)


def read_own_kernel(where, q, att_low, att_up, full, out, work, sem):
    low = where[0] == 0
    read(q, lambda rows: jnp.where(low, att_low[rows, :], att_up[rows, :]), full, work)
    column = pl.ds(pl.multiple_of(where[0] * HD, HD), HD)
    copy = pltpu.make_async_copy(work, out.at[:, column], sem)
    copy.start()
    copy.wait()


def read_own(where, q, att_low, att_up, full):
    return pl.pallas_call(
        read_own_kernel,
        in_specs=[SM] + [VM] * 4,
        out_specs=pl.BlockSpec(memory_space=pl.ANY),
        out_shape=shape((BLK, H * HD)),
        scratch_shapes=[pltpu.VMEM((BLK, HD), BF), pltpu.SemaphoreType.DMA],
        compiler_params=PARAMS,
        name="read_own",
    )(where, q, att_low, att_up, full)


def place_kernel(where, got, half_filled, out, sem):
    column = pl.ds(pl.multiple_of((1 - where[0]) * HD, HD), HD)
    copy = pltpu.make_async_copy(got, out.at[:, column], sem)
    copy.start()
    copy.wait()


def place(where, got, half_filled):
    anyspec = pl.BlockSpec(memory_space=pl.ANY)
    return pl.pallas_call(
        place_kernel,
        in_specs=[SM, VM, anyspec],
        out_specs=anyspec,
        out_shape=shape((BLK, H * HD)),
        scratch_shapes=[pltpu.SemaphoreType.DMA],
        input_output_aliases={2: 0},
        compiler_params=PARAMS,
        name="place",
    )(where, got, half_filled)


def local(queries, key_rows, value_rows, step_rates, w_gate, w_up, w_down):
    zs = lax.axis_size("z")
    z, y, core = lax.axis_index("z"), lax.axis_index("y"), lax.axis_index("core")
    where = jnp.stack([y, core, z]).astype(jnp.int32)
    rows = HALF // zs

    def swap(value, axis):
        return lax.ppermute(value, axis, SWAP)

    def shift(value, d, ring=True):
        return lax.ppermute(
            value, "z", [(i, (i + d) % zs) for i in range(zs) if ring or i + d < zs]
        )

    two = [shape((BLK, HD))] * 2

    def after(value, earlier):
        return lax.optimization_barrier((value, earlier))[0]

    q_other = pl.BlockSpec((BLK, HD), lambda i, s: (0, 1 - s[0]))
    sent_a = pack(where, key_rows, value_rows, 0, HALF, False)
    sent_b = pack(where, after(key_rows, sent_a), value_rows, HALF, HALF, False)
    sent_q = call_blocks(
        pack_q_kernel, "pack_q", [q_other, None], [shape((BLK + RATE_ROWS, HD))]
    )(where, in_hbm(after(queries, sent_b)), step_rates)[0]
    own = pack(where, after(key_rows, sent_b), value_rows, 0, BLK, True)
    theirs = [swap(sent_a, "y"), swap(sent_b, "y")]
    q_own = jnp.where(y == 0, queries[:, :HD], queries[:, HD:])
    weights = [jnp.where(y == 0, w[:HD], w[HD:]) for w in (w_gate, w_up, w_down)]
    theirs[0], sent_q, q_own, (wg, wu, wd) = lax.optimization_barrier(
        (theirs[0], sent_q, q_own, weights)
    )
    q_for = swap(sent_q, "y")
    own2 = swap(own, "core")
    gone = pick(where, theirs[0], own, 0)
    halo_a = shift(gone, 1, ring=False)
    theirs2 = [swap(after(theirs[0], gone), "core")]
    mine = pre_own(where, own, own2, wg, wu)
    theirs[1], mine, theirs2[0] = lax.optimization_barrier((theirs[1], mine, theirs2[0]))
    gone = pick(where, theirs[1], own, 1)
    halo_b = shift(gone, 1, ring=False)
    theirs2.append(swap(after(theirs[1], gone), "core"))
    theirs2, halo_a = lax.optimization_barrier((theirs2, halo_a))
    low, high = pre(where, theirs, mine[:4], wg, wu)
    theirs2, low, q_for = lax.optimization_barrier((theirs2, low, q_for))
    low2, high2 = pre(where, theirs2, mine[4:], wg, wu)
    low2, q_for = lax.optimization_barrier((low2, q_for))

    pair = shape((BLK, 2 * HD))
    att_up, err_up, kv_low, kv_low2 = call(
        upper_kernel, "attend_upper", two + [pair] * 2, [pltpu.VMEM(pair.shape, BF)] * 2
    )(where, q_own, q_for, step_rates, own, *theirs, own2, *theirs2)
    err_up, halo = lax.optimization_barrier((err_up, (halo_a, halo_b)))
    halo2 = [swap(h, "core") for h in halo]
    err_up2 = swap(err_up, "core")
    att_low, err_low = call(
        lower_kernel, "attend_lower", two, [pltpu.VMEM((BLK, 2 * HD), BF)]
    )(where, q_own, q_for, step_rates, *halo, *halo2, kv_low2, kv_low)
    err_low2 = swap(err_low, "core")

    def factors_of(*blocks):
        return [block[n] for n in range(4) for block in blocks]

    total = shape((3, HALF, HD), F32)
    before = call(grad_first_kernel, "grad_first", [total])(
        where, err_up, err_up2, *factors_of(high, high2), wd
    )[0]
    own_sum, *sends = call(
        functools.partial(grad_second_kernel, zs),
        "grad_second",
        [shape((3, rows, HD), F32)] + [shape((3, rows, HD))] * (zs - 1),
        [pltpu.VMEM(total.shape, F32)],
    )(where, err_low, err_low2, *factors_of(low, low2), wd, before)
    got = [shift(s, d) for d, s in enumerate(sends, 1)]
    piece, placed = call(
        functools.partial(update_kernel, zs), "update", [shape((3, rows, HD))] * 2
    )(where, own_sum, *got, wg, wu, wd)
    pieces = [piece] + [shift(piece, d) for d in range(1, zs)]
    pieces += [swap(p, "core") for p in pieces]
    out_for, full = call(
        functools.partial(read_foreign_kernel, zs),
        "read_foreign",
        [shape((BLK, HD)), shape((3 * HD, HD))],
    )(where, *pieces, q_for, att_low, att_up)
    out_got = swap(out_for, "y")
    own_rows = [
        lax.ppermute(placed[slot], ("z", "y", "core"), owners(zs, slot)) for slot in range(3)
    ]
    half_filled = read_own(where, q_own, att_low, att_up, full)
    half_filled, own_rows = lax.optimization_barrier((half_filled, own_rows))
    return place(where, out_got, half_filled), jnp.concatenate(own_rows, 0)


def solution(mesh):
    groups, ctx = mesh.devices.shape
    split = Mesh(mesh.devices.reshape(groups, ctx // 4, 2, 2), ("groups", "z", "y", "core"))
    tokens = ("groups", "z", "y", "core")
    return jax.shard_map(
        local,
        mesh=split,
        in_specs=(
            P(tokens, None),
            P(tokens, None),
            P(tokens, None),
            P(None, tokens),
            P("groups", None),
            P("groups", None),
            P("groups", None),
        ),
        out_specs=(P(tokens, None), P(tokens, None)),
        check_vma=False,
    )
```

```python
import functools
import math

import jax
import jax.numpy as jnp
from jax import lax
from jax.experimental import pallas as pl
from jax.experimental.pallas import tpu as pltpu
from jax.sharding import Mesh, PartitionSpec as P

H = 2
HD = 512
BLK = 512
HALF = 256
RATE_ROWS = 16
BF = jnp.bfloat16
F32 = jnp.float32
SWAP = [(0, 1), (1, 0)]
PARAMS = pltpu.CompilerParams(vmem_limit_bytes=20 << 20)
VM = pl.BlockSpec(memory_space=pltpu.VMEM)
SM = pl.BlockSpec(memory_space=pltpu.SMEM)


def mm(a, b, dims):
    return lax.dot_general(a, b, (dims, ((), ())), preferred_element_type=F32)


def mm_t(a, b):
    return mm(a, b, ((1,), (1,)))


def mm_n(a, b):
    return mm(a, b, ((1,), (0,)))


def mm_rows(a, b):
    return mm(a, b, ((0,), (0,)))


def rms(x):
    v = x.astype(F32)
    return (v * lax.rsqrt(jnp.mean(v * v, -1, keepdims=True) + 1e-06)).astype(BF)


def in_hbm(value):
    return pltpu.with_memory_space_constraint(value, pltpu.HBM)


def shape(dims, dtype=BF):
    return jax.ShapeDtypeStruct(dims, dtype)


def call(kernel, name, outs, scratch=()):
    def run(where, *args):
        return pl.pallas_call(
            kernel,
            in_specs=[SM] + [VM] * len(args),
            out_specs=[VM] * len(outs),
            out_shape=outs,
            scratch_shapes=scratch,
            compiler_params=PARAMS,
            name=name,
        )(where, *args)

    return run


def call_blocks(kernel, name, specs, outs, scratch=()):
    def run(where, *args):
        def whole(dims):
            return pl.BlockSpec(dims, lambda i, s: (0,) * len(dims))

        in_specs = [whole(a.shape) if p is None else p for a, p in zip(args, specs, strict=True)]
        return pl.pallas_call(
            kernel,
            grid_spec=pltpu.PrefetchScalarGridSpec(
                num_scalar_prefetch=1,
                grid=(1,),
                in_specs=in_specs,
                out_specs=[whole(o.shape) for o in outs],
                scratch_shapes=scratch,
            ),
            out_shape=outs,
            compiler_params=PARAMS,
            name=name,
        )(where, *args)

    return run


def pack_kernel(first, count, own, where, key, value, out, sems):
    column = where[0] if own else 1 - where[0]
    source = (pl.ds(first, count), pl.ds(pl.multiple_of(column * HD, HD), HD))
    copies = [
        pltpu.make_async_copy(ref.at[source], out.at[:, pl.ds(n * HD, HD)], sems.at[n])
        for n, ref in enumerate((key, value))
    ]
    for copy in copies:
        copy.start()
    for copy in copies:
        copy.wait()


def pack(where, key_rows, value_rows, first, count, own):
    return pl.pallas_call(
        functools.partial(pack_kernel, first, count, own),
        in_specs=[SM] + [pl.BlockSpec(memory_space=pl.ANY)] * 2,
        out_specs=VM,
        out_shape=shape((count, 2 * HD)),
        scratch_shapes=[pltpu.SemaphoreType.DMA((2,))],
        compiler_params=PARAMS,
        name="pack",
    )(where, in_hbm(key_rows), in_hbm(value_rows))


def pick_kernel(n, where, foreign, own, out):
    out[...] = jnp.where(where[0] == 0, foreign[...], own[n * HALF : (n + 1) * HALF, :])


def pick(where, foreign, own, n):
    return call(functools.partial(pick_kernel, n), "pick", [shape((HALF, 2 * HD))])(
        where, foreign, own
    )[0]


def pack_q_kernel(where, query, rates, sent):
    sent[0:BLK, :] = query[...]
    rate = jnp.where(where[0] == 0, rates[1:2, :], rates[0:1, :])
    parts = []
    for _ in range(3):
        part = rate.astype(BF)
        parts.append(part)
        rate = rate - part.astype(F32)
    row = lax.broadcasted_iota(jnp.int32, (RATE_ROWS, BLK), 0)
    tail = jnp.zeros((RATE_ROWS, BLK), F32)
    for n, part in enumerate(parts):
        tail = jnp.where(row == n, part.astype(F32), tail)
    sent[BLK : BLK + RATE_ROWS, :] = tail.astype(BF)


def factors(core, key, wg, wu, put):
    for c in range(2):
        rows = pl.ds(c * HALF, HALF)
        kc = rms(key(c))
        put(0, rows, slice(None), kc)
        for side in range(2):
            units = pl.ds(side * HALF, HALF)
            hg = mm_t(kc, wg[units, :])
            hu = mm_t(kc, wu[units, :])
            sig = jax.nn.sigmoid(hg)
            a = hg * sig
            put(1, rows, units, (a * hu).astype(BF))

            @pl.when(core == side)
            def _():
                put(2, rows, slice(None), hu * sig * (1.0 + hg * (1.0 - sig)))
                put(3, rows, slice(None), a)


def pre_own_kernel(where, own, own2, wg, wu, *outs):
    for n, kv in enumerate((own, own2)):

        def put(i, rows, columns, value):
            outs[4 * n + i][rows, columns] = value

        factors(where[1], lambda c: kv[c * HALF : (c + 1) * HALF, 0:HD], wg, wu, put)


def pick_factors(where, halves, mine, wg, wu, outs, work):
    def put(i, rows, columns, value):
        work[i][rows, columns] = value

    factors(where[1], lambda c: halves[c][:, 0:HD], wg, wu, put)
    bottom = where[0] == 0
    for i in range(4):
        outs[i][...] = jnp.where(bottom, mine[i][...], work[i][...])
        outs[4 + i][...] = jnp.where(bottom, work[i][...], mine[i][...])


def pre_kernel(where, *rest):
    pick_factors(where, rest[:2], rest[2:6], *rest[6:8], rest[8:16], rest[16:])


FACTORS = [
    shape((BLK, HD)),
    shape((BLK, HD)),
    shape((BLK, HALF), F32),
    shape((BLK, HALF), F32),
]


def pre_own(where, own, own2, wg, wu):
    return call(pre_own_kernel, "pre_own", FACTORS * 2)(where, own, own2, wg, wu)


def pre(where, halves, mine, wg, wu):
    work = [pltpu.VMEM(f.shape, f.dtype) for f in FACTORS]
    outs = call(pre_kernel, "pre", FACTORS * 2, work)(where, *halves, *mine, wg, wu)
    return outs[:4], outs[4:]


def attend(q, rate, tile_a, tile_b, tile_c, a_ok, b_ok, att, err):
    scale = 1.0 / math.sqrt(HD)
    p = lax.broadcasted_iota(jnp.int32, (HALF, HALF), 0)
    j = lax.broadcasted_iota(jnp.int32, (HALF, HALF), 1)
    causal = j <= p
    neg = jnp.float32(-jnp.inf)
    zero = jnp.zeros((HALF, HALF), BF)

    def key(tile):
        return tile[:, 0:HD]

    def value(tile):
        return tile[:, HD : 2 * HD]

    for c in range(2):
        rows = pl.ds(c * HALF, HALF)
        qc = q(rows)
        tiles = []
        for t in range(2):
            if t <= c:
                sc = mm_t(qc, key(tile_c(t))) * scale
            if t >= c:
                sa = mm_t(qc, key(tile_a(t))) * scale
                if a_ok is not None:
                    sa = jnp.where(a_ok, sa, neg)
            tiles.append(sc if t < c else sa if t > c else jnp.where(causal, sc, sa))
        for t in range(2):
            sb = mm_t(qc, key(tile_b(t))) * scale
            tiles.append(sb if b_ok is None else jnp.where(b_ok, sb, neg))
        top = functools.reduce(jnp.maximum, [jnp.max(s, -1, keepdims=True) for s in tiles])
        expo = [jnp.exp(s - top) for s in tiles]
        total = functools.reduce(jnp.add, [jnp.sum(e, -1, keepdims=True) for e in expo])
        inv = 1.0 / total
        w = [(e * inv).astype(BF) for e in expo]
        acc = mm_n(w[2], value(tile_b(0))) + mm_n(w[3], value(tile_b(1)))
        for t in range(2):
            if t <= c:
                acc += mm_n(
                    jnp.where(causal, w[t], zero) if t == c else w[t], value(tile_c(t))
                )
            if t >= c:
                acc += mm_n(
                    jnp.where(causal, zero, w[t]) if t == c else w[t], value(tile_a(t))
                )
        out = acc.astype(BF)
        att[rows, :] = out
        err[rows, :] = (-rate[c * HALF : (c + 1) * HALF] * out.astype(F32)).astype(BF)


def column(mine, side, rates, q_for):
    parts = q_for[BLK : BLK + RATE_ROWS, :].astype(F32)
    other = parts[0:1, :] + parts[1:2, :] + parts[2:3, :]
    own = jnp.where(side == 0, rates[0:1, :], rates[1:2, :])
    line = jnp.where(mine, own, other)
    return jnp.transpose(jnp.broadcast_to(line, (8, BLK)))[:, 0:1]


def rows_of(ref):
    return lambda t: ref[t * HALF : (t + 1) * HALF, :]


def upper_kernel(
    where, q_own, q_for, rates, own, for_a, for_b, own2, for2_a, for2_b, *rest
):
    att, err, low, low2, high, mid = rest
    bottom = where[0] == 0
    first = where[1] == 0
    for c, (f, f2) in enumerate(((for_a, for2_a), (for_b, for2_b))):
        rows = pl.ds(c * HALF, HALF)
        low[rows, :] = jnp.where(bottom, own[rows, :], f[...])
        high[rows, :] = jnp.where(bottom, f[...], own[rows, :])
        l2 = jnp.where(bottom, own2[rows, :], f2[...])
        low2[rows, :] = l2
        mid[rows, :] = jnp.where(first, l2, jnp.where(bottom, f2[...], own2[rows, :]))
    mine = where[0] == 1
    q = lambda rows: jnp.where(mine, q_own[rows, :], q_for[rows, :])
    r = column(mine, where[0], rates, q_for)
    attend(q, r, rows_of(low), rows_of(mid), rows_of(high), None, None, att, err)


def lower_kernel(
    where, q_own, q_for, rates, halo_a, halo_b, halo2_a, halo2_b, low2, c, att_up, *rest
):
    att_own, att_for, err, att, b = rest
    bottom = where[0] == 0
    first = where[1] == 0
    inner = where[2] > 0
    for t, h in enumerate((halo2_a, halo2_b)):
        rows = pl.ds(t * HALF, HALF)
        b[rows, :] = jnp.where(first, h[...], low2[rows, :])
    q = lambda rows: jnp.where(bottom, q_own[rows, :], q_for[rows, :])
    r = column(bottom, where[0], rates, q_for)
    halo = (halo_a, halo_b)
    attend(
        q, r, lambda t: halo[t][...], rows_of(b), rows_of(c), inner, inner | ~first, att, err
    )
    att_own[...] = jnp.where(bottom, att[...], att_up[...])
    att_for[...] = jnp.where(bottom, att_up[...], att[...])


def half_of(core, ref):
    return jnp.where(core == 0, ref[:, 0:HALF], ref[:, HALF:HD])


def add_products(where, errs, kns, gateds, slopes, acts, w, total):
    core = where[1]
    w_half = half_of(core, w)
    for e, kn, gated, slope, act in zip(errs, kns, gateds, slopes, acts, strict=True):
        back = mm_n(e[...], w_half)
        total[0] += mm_rows((back * slope[...]).astype(BF), kn[...])
        total[1] += mm_rows((back * act[...]).astype(BF), kn[...])
        total[2] += mm_rows(half_of(core, e), gated[...])


def grad_first_kernel(where, e0, e1, k0, k1, g0, g1, s0, s1, a0, a1, w, total):
    total[...] = jnp.zeros_like(total)
    add_products(where, (e0, e1), (k0, k1), (g0, g1), (s0, s1), (a0, a1), w, total)


def grad_second_kernel(
    zs, where, e0, e1, k0, k1, g0, g1, s0, s1, a0, a1, w, before, own, *rest
):
    sends, total = rest[:-1], rest[-1]
    total[...] = before[...]
    add_products(where, (e0, e1), (k0, k1), (g0, g1), (s0, s1), (a0, a1), w, total)
    rows = HALF // zs
    for d in range(zs):
        src = pl.ds(pl.multiple_of(lax.rem(where[2] + d, zs) * rows, rows), rows)
        for kind in range(3):
            if d == 0:
                own[kind] = total[kind, src, :]
            else:
                sends[d - 1][kind] = total[kind, src, :].astype(BF)


def update_kernel(zs, where, own, *rest):
    got, olds, piece = rest[:-4], rest[-4:-1], rest[-1]
    rows = HALF // zs
    mine = pl.ds(pl.multiple_of(where[1] * HALF + where[2] * rows, rows), rows)
    for kind in range(3):
        grad = own[kind]
        for g in got:
            grad = grad + g[kind].astype(F32)
        old = olds[kind][mine, :].astype(F32)
        raised = old - grad
        factor = jnp.sqrt(jnp.mean(old * old, -1, keepdims=True) + 1e-06) * lax.rsqrt(
            jnp.mean(raised * raised, -1, keepdims=True) + 1e-06
        )
        piece[kind] = (raised * factor).astype(BF)


def gather(zs, where, pieces, kinds, full):
    rows = HALF // zs
    for side, some in ((where[1], pieces[:zs]), (1 - where[1], pieces[zs:])):
        for d in range(zs):
            at = side * HALF + lax.rem(where[2] - d + zs, zs) * rows
            for kind in range(kinds):
                full[pl.ds(pl.multiple_of(kind * HD + at, rows), rows), :] = some[d][kind]


def read(q, att, full, out):
    for c in range(2):
        rows = pl.ds(c * HALF, HALF)
        qn = rms(q[rows, :])
        hg = mm_t(qn, full[0:HD, :])
        hu = mm_t(qn, full[HD : 2 * HD, :])
        g = (hg * jax.nn.sigmoid(hg) * hu).astype(BF)
        fast = mm_t(g, full[2 * HD : 3 * HD, :])
        out[rows, :] = (att[rows, :].astype(F32) + fast).astype(BF)


def write_head(head, work, out, sem):
    column = pl.ds(pl.multiple_of(head * HD, HD), HD)
    copy = pltpu.make_async_copy(work, out.at[:, column], sem)
    copy.start()
    copy.wait()


def read_own_kernel(zs, where, *rest):
    pieces, (q, att, out, full, work, sem) = rest[: 2 * zs], rest[2 * zs :]
    gather(zs, where, pieces, 3, full)
    read(q, att, full, work)
    write_head(where[0], work, out, sem)


def read_own(zs, where, pieces, q, att):
    return pl.pallas_call(
        functools.partial(read_own_kernel, zs),
        in_specs=[SM] + [VM] * (2 * zs + 2),
        out_specs=[pl.BlockSpec(memory_space=pl.ANY), VM],
        out_shape=[shape((BLK, H * HD)), shape((3 * HD, HD))],
        scratch_shapes=[pltpu.VMEM((BLK, HD), BF), pltpu.SemaphoreType.DMA],
        compiler_params=PARAMS,
        name="read_own",
    )(where, *pieces, q, att)


def read_other_kernel(zs, count, where, *rest):
    pieces, (q, att, mine, half_filled, out, weights, full, work, sem) = (
        rest[: 2 * zs],
        rest[2 * zs :],
    )
    y, core, z = where[0], where[1], where[2]
    gather(zs, where, pieces, 3, full)
    read(q, att, full, work)
    step = math.gcd(count, HD)
    first = ((z * 2 + y) * 2 + core) * count
    for c in range(count // step):
        r = first + c * step
        head = lax.rem(lax.div(r, HD), 2)
        at = lax.div(r, 2 * HD) * HD + lax.rem(r, HD)
        rows = pl.ds(pl.multiple_of(at, step), step)
        weights[c * step : (c + 1) * step, :] = jnp.where(head == y, mine[rows, :], full[rows, :])
    write_head(1 - y, work, out, sem)


def read_other(zs, where, count, pieces, q, att, mine, half_filled):
    anyspec = pl.BlockSpec(memory_space=pl.ANY)
    return pl.pallas_call(
        functools.partial(read_other_kernel, zs, count),
        in_specs=[SM] + [VM] * (2 * zs + 3) + [anyspec],
        out_specs=[anyspec, VM],
        out_shape=[shape((BLK, H * HD)), shape((count, HD))],
        scratch_shapes=[
            pltpu.VMEM((3 * HD, HD), BF),
            pltpu.VMEM((BLK, HD), BF),
            pltpu.SemaphoreType.DMA,
        ],
        input_output_aliases={2 * zs + 4: 0},
        compiler_params=PARAMS,
        name="read_other",
    )(where, *pieces, q, att, mine, half_filled)


def local(queries, key_rows, value_rows, step_rates, w_gate, w_up, w_down):
    zs = lax.axis_size("z")
    z, y, core = lax.axis_index("z"), lax.axis_index("y"), lax.axis_index("core")
    where = jnp.stack([y, core, z]).astype(jnp.int32)
    rows = HALF // zs

    def swap(value, axis):
        return lax.ppermute(value, axis, SWAP)

    def shift(value, d, ring=True):
        return lax.ppermute(
            value, "z", [(i, (i + d) % zs) for i in range(zs) if ring or i + d < zs]
        )

    two = [shape((BLK, HD))] * 2

    def after(value, earlier):
        return lax.optimization_barrier((value, earlier))[0]

    q_other = pl.BlockSpec((BLK, HD), lambda i, s: (0, 1 - s[0]))
    sent_a = pack(where, key_rows, value_rows, 0, HALF, False)
    sent_b = pack(where, after(key_rows, sent_a), value_rows, HALF, HALF, False)
    sent_q = call_blocks(
        pack_q_kernel, "pack_q", [q_other, None], [shape((BLK + RATE_ROWS, HD))]
    )(where, in_hbm(after(queries, sent_b)), step_rates)[0]
    own = pack(where, after(key_rows, sent_b), value_rows, 0, BLK, True)
    theirs = [swap(sent_a, "y"), swap(sent_b, "y")]
    q_own = jnp.where(y == 0, queries[:, :HD], queries[:, HD:])
    q_rest = jnp.where(y == 0, queries[:, HD:], queries[:, :HD])
    weights = [jnp.where(y == 0, w[:HD], w[HD:]) for w in (w_gate, w_up, w_down)]
    theirs[0], sent_q, q_own, (wg, wu, wd) = lax.optimization_barrier(
        (theirs[0], sent_q, q_own, weights)
    )
    q_for = swap(sent_q, "y")
    own2 = swap(own, "core")
    gone = pick(where, theirs[0], own, 0)
    halo_a = shift(gone, 1, ring=False)
    theirs2 = [swap(after(theirs[0], gone), "core")]
    mine = pre_own(where, own, own2, wg, wu)
    theirs[1], mine, theirs2[0] = lax.optimization_barrier((theirs[1], mine, theirs2[0]))
    gone = pick(where, theirs[1], own, 1)
    halo_b = shift(gone, 1, ring=False)
    theirs2.append(swap(after(theirs[1], gone), "core"))
    theirs2, halo_a = lax.optimization_barrier((theirs2, halo_a))
    low, high = pre(where, theirs, mine[:4], wg, wu)
    theirs2, low, q_for = lax.optimization_barrier((theirs2, low, q_for))
    low2, high2 = pre(where, theirs2, mine[4:], wg, wu)
    low2, q_for = lax.optimization_barrier((low2, q_for))

    pair = shape((BLK, 2 * HD))
    att_up, err_up, kv_low, kv_low2 = call(
        upper_kernel, "attend_upper", two + [pair] * 2, [pltpu.VMEM(pair.shape, BF)] * 2
    )(where, q_own, q_for, step_rates, own, *theirs, own2, *theirs2)
    err_up, halo = lax.optimization_barrier((err_up, (halo_a, halo_b)))
    halo2 = [swap(h, "core") for h in halo]
    err_up2 = swap(err_up, "core")
    att_own, att_for, err_low = call(
        lower_kernel,
        "attend_lower",
        [shape((BLK, HD))] * 3,
        [pltpu.VMEM((BLK, HD), BF), pltpu.VMEM((BLK, 2 * HD), BF)],
    )(where, q_own, q_for, step_rates, *halo, *halo2, kv_low2, kv_low, att_up)
    err_low2 = swap(err_low, "core")

    def factors_of(*blocks):
        return [block[n] for n in range(4) for block in blocks]

    total = shape((3, HALF, HD), F32)
    before = call(grad_first_kernel, "grad_first", [total])(
        where, err_up, err_up2, *factors_of(high, high2), wd
    )[0]
    own_sum, *sends = call(
        functools.partial(grad_second_kernel, zs),
        "grad_second",
        [shape((3, rows, HD), F32)] + [shape((3, rows, HD))] * (zs - 1),
        [pltpu.VMEM(total.shape, F32)],
    )(where, err_low, err_low2, *factors_of(low, low2), wd, before)
    got = [shift(s, d) for d, s in enumerate(sends, 1)]
    att_back = swap(after(att_for, own_sum), "y")
    got, att_back = lax.optimization_barrier((got, att_back))
    piece = call(functools.partial(update_kernel, zs), "update", [shape((3, rows, HD))])(
        where, own_sum, *got, wg, wu, wd
    )[0]
    pieces = [piece] + [shift(piece, d) for d in range(1, zs)]
    others = [swap(p, "y") for p in pieces]
    pieces2 = [swap(p, "core") for p in pieces]
    others2 = [swap(p, "core") for p in others]
    half_filled, full = read_own(zs, where, pieces + pieces2, q_own, att_own)
    count = 3 * H * HD // (4 * zs)
    return tuple(
        read_other(zs, where, count, others + others2, q_rest, att_back, full, half_filled)
    )


def solution(mesh):
    groups, ctx = mesh.devices.shape
    split = Mesh(mesh.devices.reshape(groups, ctx // 4, 2, 2), ("groups", "z", "y", "core"))
    tokens = ("groups", "z", "y", "core")
    return jax.shard_map(
        local,
        mesh=split,
        in_specs=(
            P(tokens, None),
            P(tokens, None),
            P(tokens, None),
            P(None, tokens),
            P("groups", None),
            P("groups", None),
            P("groups", None),
        ),
        out_specs=(P(tokens, None), P(tokens, None)),
        check_vma=False,
    )
```

```python
import functools
import math

import jax
import jax.numpy as jnp
from jax import lax
from jax.experimental import pallas as pl
from jax.experimental.pallas import tpu as pltpu
from jax.sharding import Mesh, PartitionSpec as P

H = 2
HD = 512
BLK = 512
HALF = 256
RATE_ROWS = 16
BF = jnp.bfloat16
F32 = jnp.float32
SWAP = [(0, 1), (1, 0)]
PARAMS = pltpu.CompilerParams(vmem_limit_bytes=20 << 20)
VM = pl.BlockSpec(memory_space=pltpu.VMEM)
SM = pl.BlockSpec(memory_space=pltpu.SMEM)


def mm(a, b, dims):
    return lax.dot_general(a, b, (dims, ((), ())), preferred_element_type=F32)


def mm_t(a, b):
    return mm(a, b, ((1,), (1,)))


def mm_n(a, b):
    return mm(a, b, ((1,), (0,)))


def mm_rows(a, b):
    return mm(a, b, ((0,), (0,)))


def rms(x):
    v = x.astype(F32)
    return (v * lax.rsqrt(jnp.mean(v * v, -1, keepdims=True) + 1e-06)).astype(BF)


def in_hbm(value):
    return pltpu.with_memory_space_constraint(value, pltpu.HBM)


def shape(dims, dtype=BF):
    return jax.ShapeDtypeStruct(dims, dtype)


def call(kernel, name, outs, scratch=()):
    def run(where, *args):
        return pl.pallas_call(
            kernel,
            in_specs=[SM] + [VM] * len(args),
            out_specs=[VM] * len(outs),
            out_shape=outs,
            scratch_shapes=scratch,
            compiler_params=PARAMS,
            name=name,
        )(where, *args)

    return run


def call_blocks(kernel, name, specs, outs, scratch=()):
    def run(where, *args):
        def whole(dims):
            return pl.BlockSpec(dims, lambda i, s: (0,) * len(dims))

        in_specs = [whole(a.shape) if p is None else p for a, p in zip(args, specs, strict=True)]
        return pl.pallas_call(
            kernel,
            grid_spec=pltpu.PrefetchScalarGridSpec(
                num_scalar_prefetch=1,
                grid=(1,),
                in_specs=in_specs,
                out_specs=[whole(o.shape) for o in outs],
                scratch_shapes=scratch,
            ),
            out_shape=outs,
            compiler_params=PARAMS,
            name=name,
        )(where, *args)

    return run


def pack_kernel(first, count, own, where, key, value, out, sems):
    column = where[0] if own else 1 - where[0]
    source = (pl.ds(first, count), pl.ds(pl.multiple_of(column * HD, HD), HD))
    copies = [
        pltpu.make_async_copy(ref.at[source], out.at[:, pl.ds(n * HD, HD)], sems.at[n])
        for n, ref in enumerate((key, value))
    ]
    for copy in copies:
        copy.start()
    for copy in copies:
        copy.wait()


def pack(where, key_rows, value_rows, first, count, own):
    return pl.pallas_call(
        functools.partial(pack_kernel, first, count, own),
        in_specs=[SM] + [pl.BlockSpec(memory_space=pl.ANY)] * 2,
        out_specs=VM,
        out_shape=shape((count, 2 * HD)),
        scratch_shapes=[pltpu.SemaphoreType.DMA((2,))],
        compiler_params=PARAMS,
        name="pack",
    )(where, in_hbm(key_rows), in_hbm(value_rows))


def pick_kernel(n, where, foreign, own, out):
    out[...] = jnp.where(where[0] == 0, foreign[...], own[n * HALF : (n + 1) * HALF, :])


def pick(where, foreign, own, n):
    return call(functools.partial(pick_kernel, n), "pick", [shape((HALF, 2 * HD))])(
        where, foreign, own
    )[0]


def pack_q_kernel(where, query, rates, sent):
    sent[0:BLK, :] = query[...]
    rate = jnp.where(where[0] == 0, rates[1:2, :], rates[0:1, :])
    parts = []
    for _ in range(3):
        part = rate.astype(BF)
        parts.append(part)
        rate = rate - part.astype(F32)
    row = lax.broadcasted_iota(jnp.int32, (RATE_ROWS, BLK), 0)
    tail = jnp.zeros((RATE_ROWS, BLK), F32)
    for n, part in enumerate(parts):
        tail = jnp.where(row == n, part.astype(F32), tail)
    sent[BLK : BLK + RATE_ROWS, :] = tail.astype(BF)


def factors(core, key, wg, wu, put):
    for c in range(2):
        rows = pl.ds(c * HALF, HALF)
        kc = rms(key(c))
        put(0, rows, slice(None), kc)
        for side in range(2):
            units = pl.ds(side * HALF, HALF)
            hg = mm_t(kc, wg[units, :])
            hu = mm_t(kc, wu[units, :])
            sig = jax.nn.sigmoid(hg)
            a = hg * sig
            put(1, rows, units, (a * hu).astype(BF))

            @pl.when(core == side)
            def _():
                put(2, rows, slice(None), hu * sig * (1.0 + hg * (1.0 - sig)))
                put(3, rows, slice(None), a)


def pre_own_kernel(where, own, own2, wg, wu, *outs):
    for n, kv in enumerate((own, own2)):

        def put(i, rows, columns, value):
            outs[4 * n + i][rows, columns] = value

        factors(where[1], lambda c: kv[c * HALF : (c + 1) * HALF, 0:HD], wg, wu, put)


def pick_factors(where, halves, mine, wg, wu, outs, work):
    def put(i, rows, columns, value):
        work[i][rows, columns] = value

    factors(where[1], lambda c: halves[c][:, 0:HD], wg, wu, put)
    bottom = where[0] == 0
    for i in range(4):
        outs[i][...] = jnp.where(bottom, mine[i][...], work[i][...])
        outs[4 + i][...] = jnp.where(bottom, work[i][...], mine[i][...])


def pre_kernel(where, *rest):
    pick_factors(where, rest[:2], rest[2:6], *rest[6:8], rest[8:16], rest[16:])


FACTORS = [
    shape((BLK, HD)),
    shape((BLK, HD)),
    shape((BLK, HALF), F32),
    shape((BLK, HALF), F32),
]


def pre_own(where, own, own2, wg, wu):
    return call(pre_own_kernel, "pre_own", FACTORS * 2)(where, own, own2, wg, wu)


def pre(where, halves, mine, wg, wu):
    work = [pltpu.VMEM(f.shape, f.dtype) for f in FACTORS]
    outs = call(pre_kernel, "pre", FACTORS * 2, work)(where, *halves, *mine, wg, wu)
    return outs[:4], outs[4:]


def attend(q, rate, tile_a, tile_b, tile_c, a_ok, b_ok, att, err):
    scale = 1.0 / math.sqrt(HD)
    p = lax.broadcasted_iota(jnp.int32, (HALF, HALF), 0)
    j = lax.broadcasted_iota(jnp.int32, (HALF, HALF), 1)
    causal = j <= p
    neg = jnp.float32(-jnp.inf)
    zero = jnp.zeros((HALF, HALF), BF)

    def key(tile):
        return tile[:, 0:HD]

    def value(tile):
        return tile[:, HD : 2 * HD]

    for c in range(2):
        rows = pl.ds(c * HALF, HALF)
        qc = q(rows)
        tiles = []
        for t in range(2):
            if t <= c:
                sc = mm_t(qc, key(tile_c(t))) * scale
            if t >= c:
                sa = mm_t(qc, key(tile_a(t))) * scale
                if a_ok is not None:
                    sa = jnp.where(a_ok, sa, neg)
            tiles.append(sc if t < c else sa if t > c else jnp.where(causal, sc, sa))
        for t in range(2):
            sb = mm_t(qc, key(tile_b(t))) * scale
            tiles.append(sb if b_ok is None else jnp.where(b_ok, sb, neg))
        top = functools.reduce(jnp.maximum, [jnp.max(s, -1, keepdims=True) for s in tiles])
        expo = [jnp.exp(s - top) for s in tiles]
        total = functools.reduce(jnp.add, [jnp.sum(e, -1, keepdims=True) for e in expo])
        inv = 1.0 / total
        w = [(e * inv).astype(BF) for e in expo]
        acc = mm_n(w[2], value(tile_b(0))) + mm_n(w[3], value(tile_b(1)))
        for t in range(2):
            if t <= c:
                acc += mm_n(
                    jnp.where(causal, w[t], zero) if t == c else w[t], value(tile_c(t))
                )
            if t >= c:
                acc += mm_n(
                    jnp.where(causal, zero, w[t]) if t == c else w[t], value(tile_a(t))
                )
        out = acc.astype(BF)
        att[rows, :] = out
        err[rows, :] = (-rate[c * HALF : (c + 1) * HALF] * out.astype(F32)).astype(BF)


def column(mine, side, rates, q_for):
    parts = q_for[BLK : BLK + RATE_ROWS, :].astype(F32)
    other = parts[0:1, :] + parts[1:2, :] + parts[2:3, :]
    own = jnp.where(side == 0, rates[0:1, :], rates[1:2, :])
    line = jnp.where(mine, own, other)
    return jnp.transpose(jnp.broadcast_to(line, (8, BLK)))[:, 0:1]


def rows_of(ref):
    return lambda t: ref[t * HALF : (t + 1) * HALF, :]


def upper_kernel(
    where, q_own, q_for, rates, own, for_a, for_b, own2, for2_a, for2_b, *rest
):
    att, err, low, low2, high, mid = rest
    bottom = where[0] == 0
    first = where[1] == 0
    for c, (f, f2) in enumerate(((for_a, for2_a), (for_b, for2_b))):
        rows = pl.ds(c * HALF, HALF)
        low[rows, :] = jnp.where(bottom, own[rows, :], f[...])
        high[rows, :] = jnp.where(bottom, f[...], own[rows, :])
        l2 = jnp.where(bottom, own2[rows, :], f2[...])
        low2[rows, :] = l2
        mid[rows, :] = jnp.where(first, l2, jnp.where(bottom, f2[...], own2[rows, :]))
    mine = where[0] == 1
    q = lambda rows: jnp.where(mine, q_own[rows, :], q_for[rows, :])
    r = column(mine, where[0], rates, q_for)
    attend(q, r, rows_of(low), rows_of(mid), rows_of(high), None, None, att, err)


def lower_kernel(
    where, q_own, q_for, rates, halo_a, halo_b, halo2_a, halo2_b, low2, c, att_up, *rest
):
    att_own, att_for, err, att, b = rest
    bottom = where[0] == 0
    first = where[1] == 0
    inner = where[2] > 0
    for t, h in enumerate((halo2_a, halo2_b)):
        rows = pl.ds(t * HALF, HALF)
        b[rows, :] = jnp.where(first, h[...], low2[rows, :])
    q = lambda rows: jnp.where(bottom, q_own[rows, :], q_for[rows, :])
    r = column(bottom, where[0], rates, q_for)
    halo = (halo_a, halo_b)
    attend(
        q, r, lambda t: halo[t][...], rows_of(b), rows_of(c), inner, inner | ~first, att, err
    )
    att_own[...] = jnp.where(bottom, att[...], att_up[...])
    att_for[...] = jnp.where(bottom, att_up[...], att[...])


def half_of(core, ref):
    return jnp.where(core == 0, ref[:, 0:HALF], ref[:, HALF:HD])


def add_products(where, errs, kns, gateds, slopes, acts, w, total):
    core = where[1]
    w_half = half_of(core, w)
    for e, kn, gated, slope, act in zip(errs, kns, gateds, slopes, acts, strict=True):
        back = mm_n(e[...], w_half)
        total[0] += mm_rows((back * slope[...]).astype(BF), kn[...])
        total[1] += mm_rows((back * act[...]).astype(BF), kn[...])
        total[2] += mm_rows(half_of(core, e), gated[...])


def grad_first_kernel(where, e0, e1, k0, k1, g0, g1, s0, s1, a0, a1, w, total):
    total[...] = jnp.zeros_like(total)
    add_products(where, (e0, e1), (k0, k1), (g0, g1), (s0, s1), (a0, a1), w, total)


def grad_second_kernel(
    zs, where, e0, e1, k0, k1, g0, g1, s0, s1, a0, a1, w, before, own, *rest
):
    sends, total = rest[:-1], rest[-1]
    total[...] = before[...]
    add_products(where, (e0, e1), (k0, k1), (g0, g1), (s0, s1), (a0, a1), w, total)
    rows = HALF // zs
    for d in range(zs):
        src = pl.ds(pl.multiple_of(lax.rem(where[2] + d, zs) * rows, rows), rows)
        for kind in range(3):
            if d == 0:
                own[kind] = total[kind, src, :]
            else:
                sends[d - 1][kind] = total[kind, src, :].astype(BF)


def update_kernel(zs, where, own, *rest):
    got, olds, piece = rest[:-4], rest[-4:-1], rest[-1]
    rows = HALF // zs
    mine = pl.ds(pl.multiple_of(where[1] * HALF + where[2] * rows, rows), rows)
    for kind in range(3):
        grad = own[kind]
        for g in got:
            grad = grad + g[kind].astype(F32)
        old = olds[kind][mine, :].astype(F32)
        raised = old - grad
        factor = jnp.sqrt(jnp.mean(old * old, -1, keepdims=True) + 1e-06) * lax.rsqrt(
            jnp.mean(raised * raised, -1, keepdims=True) + 1e-06
        )
        piece[kind] = (raised * factor).astype(BF)


def gather(zs, where, pieces, kinds, full):
    rows = HALF // zs
    for side, some in ((where[1], pieces[:zs]), (1 - where[1], pieces[zs:])):
        for d in range(zs):
            at = side * HALF + lax.rem(where[2] - d + zs, zs) * rows
            for kind in range(kinds):
                full[pl.ds(pl.multiple_of(kind * HD + at, rows), rows), :] = some[d][kind]


def read(qn, att, full, out, head, work, sems):
    column = pl.ds(pl.multiple_of(head * HD, HD), HD)
    copies = []
    for c in range(2):
        rows = pl.ds(c * HALF, HALF)
        x = qn(rows)
        hg = mm_t(x, full[0:HD, :])
        hu = mm_t(x, full[HD : 2 * HD, :])
        g = (hg * jax.nn.sigmoid(hg) * hu).astype(BF)
        fast = mm_t(g, full[2 * HD : 3 * HD, :])
        work[rows, :] = (att[rows, :].astype(F32) + fast).astype(BF)
        copy = pltpu.make_async_copy(work.at[rows, :], out.at[rows, column], sems.at[c])
        copy.start()
        copies.append(copy)
    for copy in copies:
        copy.wait()


def read_own_kernel(zs, where, *rest):
    pieces, (q, att, q_rest, out, full, qn_rest, work, sems) = rest[: 2 * zs], rest[2 * zs :]
    gather(zs, where, pieces, 3, full)
    qn_rest[...] = rms(q_rest[...])
    read(lambda rows: rms(q[rows, :]), att, full, out, where[0], work, sems)


def read_own(zs, where, pieces, q, att, q_rest):
    return pl.pallas_call(
        functools.partial(read_own_kernel, zs),
        in_specs=[SM] + [VM] * (2 * zs + 3),
        out_specs=[pl.BlockSpec(memory_space=pl.ANY), VM, VM],
        out_shape=[shape((BLK, H * HD)), shape((3 * HD, HD)), shape((BLK, HD))],
        scratch_shapes=[pltpu.VMEM((BLK, HD), BF), pltpu.SemaphoreType.DMA((2,))],
        compiler_params=PARAMS,
        name="read_own",
    )(where, *pieces, q, att, q_rest)


def read_other_kernel(zs, count, where, *rest):
    pieces, (qn, att, mine, half_filled, out, weights, full, work, sems) = (
        rest[: 2 * zs],
        rest[2 * zs :],
    )
    y, core, z = where[0], where[1], where[2]
    gather(zs, where, pieces, 3, full)
    step = math.gcd(count, HD)
    first = ((z * 2 + y) * 2 + core) * count
    for c in range(count // step):
        r = first + c * step
        head = lax.rem(lax.div(r, HD), 2)
        at = lax.div(r, 2 * HD) * HD + lax.rem(r, HD)
        rows = pl.ds(pl.multiple_of(at, step), step)
        weights[c * step : (c + 1) * step, :] = jnp.where(head == y, mine[rows, :], full[rows, :])
    read(lambda rows: qn[rows, :], att, full, out, 1 - y, work, sems)


def read_other(zs, where, count, pieces, qn, att, mine, half_filled):
    anyspec = pl.BlockSpec(memory_space=pl.ANY)
    return pl.pallas_call(
        functools.partial(read_other_kernel, zs, count),
        in_specs=[SM] + [VM] * (2 * zs + 3) + [anyspec],
        out_specs=[anyspec, VM],
        out_shape=[shape((BLK, H * HD)), shape((count, HD))],
        scratch_shapes=[
            pltpu.VMEM((3 * HD, HD), BF),
            pltpu.VMEM((BLK, HD), BF),
            pltpu.SemaphoreType.DMA((2,)),
        ],
        input_output_aliases={2 * zs + 4: 0},
        compiler_params=PARAMS,
        name="read_other",
    )(where, *pieces, qn, att, mine, half_filled)


def local(queries, key_rows, value_rows, step_rates, w_gate, w_up, w_down):
    zs = lax.axis_size("z")
    z, y, core = lax.axis_index("z"), lax.axis_index("y"), lax.axis_index("core")
    where = jnp.stack([y, core, z]).astype(jnp.int32)
    rows = HALF // zs

    def swap(value, axis):
        return lax.ppermute(value, axis, SWAP)

    def shift(value, d, ring=True):
        return lax.ppermute(
            value, "z", [(i, (i + d) % zs) for i in range(zs) if ring or i + d < zs]
        )

    two = [shape((BLK, HD))] * 2

    def after(value, earlier):
        return lax.optimization_barrier((value, earlier))[0]

    q_other = pl.BlockSpec((BLK, HD), lambda i, s: (0, 1 - s[0]))
    sent_a = pack(where, key_rows, value_rows, 0, HALF, False)
    sent_b = pack(where, after(key_rows, sent_a), value_rows, HALF, HALF, False)
    sent_q = call_blocks(
        pack_q_kernel, "pack_q", [q_other, None], [shape((BLK + RATE_ROWS, HD))]
    )(where, in_hbm(after(queries, sent_b)), step_rates)[0]
    own = pack(where, after(key_rows, sent_b), value_rows, 0, BLK, True)
    theirs = [swap(sent_a, "y"), swap(sent_b, "y")]
    q_own = jnp.where(y == 0, queries[:, :HD], queries[:, HD:])
    q_rest = jnp.where(y == 0, queries[:, HD:], queries[:, :HD])
    weights = [jnp.where(y == 0, w[:HD], w[HD:]) for w in (w_gate, w_up, w_down)]
    theirs[0], sent_q, q_own, (wg, wu, wd) = lax.optimization_barrier(
        (theirs[0], sent_q, q_own, weights)
    )
    q_for = swap(sent_q, "y")
    own2 = swap(own, "core")
    gone = pick(where, theirs[0], own, 0)
    halo_a = shift(gone, 1, ring=False)
    theirs2 = [swap(after(theirs[0], gone), "core")]
    mine = pre_own(where, own, own2, wg, wu)
    theirs[1], mine, theirs2[0] = lax.optimization_barrier((theirs[1], mine, theirs2[0]))
    gone = pick(where, theirs[1], own, 1)
    halo_b = shift(gone, 1, ring=False)
    theirs2.append(swap(after(theirs[1], gone), "core"))
    theirs2, halo_a = lax.optimization_barrier((theirs2, halo_a))
    low, high = pre(where, theirs, mine[:4], wg, wu)
    theirs2, low, q_for = lax.optimization_barrier((theirs2, low, q_for))
    low2, high2 = pre(where, theirs2, mine[4:], wg, wu)
    low2, q_for = lax.optimization_barrier((low2, q_for))

    pair = shape((BLK, 2 * HD))
    att_up, err_up, kv_low, kv_low2 = call(
        upper_kernel, "attend_upper", two + [pair] * 2, [pltpu.VMEM(pair.shape, BF)] * 2
    )(where, q_own, q_for, step_rates, own, *theirs, own2, *theirs2)
    err_up, halo = lax.optimization_barrier((err_up, (halo_a, halo_b)))
    halo2 = [swap(h, "core") for h in halo]
    err_up2 = swap(err_up, "core")
    att_own, att_for, err_low = call(
        lower_kernel,
        "attend_lower",
        [shape((BLK, HD))] * 3,
        [pltpu.VMEM((BLK, HD), BF), pltpu.VMEM((BLK, 2 * HD), BF)],
    )(where, q_own, q_for, step_rates, *halo, *halo2, kv_low2, kv_low, att_up)
    err_low2 = swap(err_low, "core")

    def factors_of(*blocks):
        return [block[n] for n in range(4) for block in blocks]

    total = shape((3, HALF, HD), F32)
    before = call(grad_first_kernel, "grad_first", [total])(
        where, err_up, err_up2, *factors_of(high, high2), wd
    )[0]
    own_sum, *sends = call(
        functools.partial(grad_second_kernel, zs),
        "grad_second",
        [shape((3, rows, HD), F32)] + [shape((3, rows, HD))] * (zs - 1),
        [pltpu.VMEM(total.shape, F32)],
    )(where, err_low, err_low2, *factors_of(low, low2), wd, before)
    got = [shift(s, d) for d, s in enumerate(sends, 1)]
    att_back = swap(after(att_for, own_sum), "y")
    got, att_back = lax.optimization_barrier((got, att_back))
    piece = call(functools.partial(update_kernel, zs), "update", [shape((3, rows, HD))])(
        where, own_sum, *got, wg, wu, wd
    )[0]
    order = [zs - 1, *range(1, zs - 1)]
    pieces = {0: piece} | {d: shift(piece, d) for d in order}
    others = {0: swap(piece, "y")}
    last = 0
    for d in order:
        if d == order[-1]:
            pieces[d], pieces[last] = lax.optimization_barrier((pieces[d], pieces[last]))
        elif d != order[0]:
            pieces[d], others[last] = lax.optimization_barrier((pieces[d], others[last]))
        others[d] = swap(pieces[d], "y")
        last = d
    final = order[-1]
    soon = [0, *order[:-1]]
    gate = (pieces[final], others[soon[-1]])
    arrived = after([pieces[d] for d in soon], gate)
    pieces2 = {d: swap(p, "core") for d, p in zip(soon, arrived, strict=True)}
    pieces2[final] = swap(after(pieces[final], gate), "core")
    arrived = after([others[d] for d in soon], gate)
    others2 = {d: swap(p, "core") for d, p in zip(soon, arrived, strict=True)}
    listed = lambda some: [some[d] for d in range(zs)]
    half_filled, full, qn_rest = read_own(
        zs, where, listed(pieces) + listed(pieces2), q_own, att_own, q_rest
    )
    others2[final] = swap(after(others[final], full), "core")
    count = 3 * H * HD // (4 * zs)
    return tuple(
        read_other(
            zs, where, count, listed(others) + listed(others2), qn_rest, att_back, full, half_filled
        )
    )


def solution(mesh):
    groups, ctx = mesh.devices.shape
    split = Mesh(mesh.devices.reshape(groups, ctx // 4, 2, 2), ("groups", "z", "y", "core"))
    tokens = ("groups", "z", "y", "core")
    return jax.shard_map(
        local,
        mesh=split,
        in_specs=(
            P(tokens, None),
            P(tokens, None),
            P(tokens, None),
            P(None, tokens),
            P("groups", None),
            P("groups", None),
            P("groups", None),
        ),
        out_specs=(P(tokens, None), P(tokens, None)),
        check_vma=False,
    )
```

```python
import functools
import math

import jax
import jax.numpy as jnp
from jax import lax
from jax.experimental import pallas as pl
from jax.experimental.pallas import tpu as pltpu
from jax.sharding import Mesh, PartitionSpec as P

H = 2
HD = 512
BLK = 512
HALF = 256
RATE_ROWS = 16
BF = jnp.bfloat16
F32 = jnp.float32
SWAP = [(0, 1), (1, 0)]
PARAMS = pltpu.CompilerParams(vmem_limit_bytes=20 << 20)
VM = pl.BlockSpec(memory_space=pltpu.VMEM)
SM = pl.BlockSpec(memory_space=pltpu.SMEM)


def mm(a, b, dims):
    return lax.dot_general(a, b, (dims, ((), ())), preferred_element_type=F32)


def mm_t(a, b):
    return mm(a, b, ((1,), (1,)))


def mm_n(a, b):
    return mm(a, b, ((1,), (0,)))


def mm_rows(a, b):
    return mm(a, b, ((0,), (0,)))


def rms(x):
    v = x.astype(F32)
    return (v * lax.rsqrt(jnp.mean(v * v, -1, keepdims=True) + 1e-06)).astype(BF)


def in_hbm(value):
    return pltpu.with_memory_space_constraint(value, pltpu.HBM)


def shape(dims, dtype=BF):
    return jax.ShapeDtypeStruct(dims, dtype)


def call(kernel, name, outs, scratch=()):
    def run(where, *args):
        return pl.pallas_call(
            kernel,
            in_specs=[SM] + [VM] * len(args),
            out_specs=[VM] * len(outs),
            out_shape=outs,
            scratch_shapes=scratch,
            compiler_params=PARAMS,
            name=name,
        )(where, *args)

    return run


def call_blocks(kernel, name, specs, outs, scratch=()):
    def run(where, *args):
        def whole(dims):
            return pl.BlockSpec(dims, lambda i, s: (0,) * len(dims))

        in_specs = [whole(a.shape) if p is None else p for a, p in zip(args, specs, strict=True)]
        return pl.pallas_call(
            kernel,
            grid_spec=pltpu.PrefetchScalarGridSpec(
                num_scalar_prefetch=1,
                grid=(1,),
                in_specs=in_specs,
                out_specs=[whole(o.shape) for o in outs],
                scratch_shapes=scratch,
            ),
            out_shape=outs,
            compiler_params=PARAMS,
            name=name,
        )(where, *args)

    return run


def pack_kernel(first, count, own, where, key, value, out, sems):
    column = where[0] if own else 1 - where[0]
    source = (pl.ds(first, count), pl.ds(pl.multiple_of(column * HD, HD), HD))
    copies = [
        pltpu.make_async_copy(ref.at[source], out.at[:, pl.ds(n * HD, HD)], sems.at[n])
        for n, ref in enumerate((key, value))
    ]
    for copy in copies:
        copy.start()
    for copy in copies:
        copy.wait()


def pack(where, key_rows, value_rows, first, count, own):
    return pl.pallas_call(
        functools.partial(pack_kernel, first, count, own),
        in_specs=[SM] + [pl.BlockSpec(memory_space=pl.ANY)] * 2,
        out_specs=VM,
        out_shape=shape((count, 2 * HD)),
        scratch_shapes=[pltpu.SemaphoreType.DMA((2,))],
        compiler_params=PARAMS,
        name="pack",
    )(where, in_hbm(key_rows), in_hbm(value_rows))


def pick_kernel(n, where, foreign, own, out):
    out[...] = jnp.where(where[0] == 0, foreign[...], own[n * HALF : (n + 1) * HALF, :])


def pick(where, foreign, own, n):
    return call(functools.partial(pick_kernel, n), "pick", [shape((HALF, 2 * HD))])(
        where, foreign, own
    )[0]


def pack_q_kernel(where, query, rates, sent):
    sent[0:BLK, :] = query[...]
    rate = jnp.where(where[0] == 0, rates[1:2, :], rates[0:1, :])
    parts = []
    for _ in range(3):
        part = rate.astype(BF)
        parts.append(part)
        rate = rate - part.astype(F32)
    row = lax.broadcasted_iota(jnp.int32, (RATE_ROWS, BLK), 0)
    tail = jnp.zeros((RATE_ROWS, BLK), F32)
    for n, part in enumerate(parts):
        tail = jnp.where(row == n, part.astype(F32), tail)
    sent[BLK : BLK + RATE_ROWS, :] = tail.astype(BF)


def factors(core, key, wg, wu, put):
    for c in range(2):
        rows = pl.ds(c * HALF, HALF)
        kc = rms(key(c))
        put(0, rows, slice(None), kc)
        for side in range(2):
            units = pl.ds(side * HALF, HALF)
            hg = mm_t(kc, wg[units, :])
            hu = mm_t(kc, wu[units, :])
            sig = jax.nn.sigmoid(hg)
            a = hg * sig
            put(1, rows, units, (a * hu).astype(BF))

            @pl.when(core == side)
            def _():
                put(2, rows, slice(None), hu * sig * (1.0 + hg * (1.0 - sig)))
                put(3, rows, slice(None), a)


def pre_own_kernel(where, own, own2, wg, wu, *outs):
    for n, kv in enumerate((own, own2)):

        def put(i, rows, columns, value):
            outs[4 * n + i][rows, columns] = value

        factors(where[1], lambda c: kv[c * HALF : (c + 1) * HALF, 0:HD], wg, wu, put)


def pick_factors(where, halves, mine, wg, wu, outs, work):
    def put(i, rows, columns, value):
        work[i][rows, columns] = value

    factors(where[1], lambda c: halves[c][:, 0:HD], wg, wu, put)
    bottom = where[0] == 0
    for i in range(4):
        outs[i][...] = jnp.where(bottom, mine[i][...], work[i][...])
        outs[4 + i][...] = jnp.where(bottom, work[i][...], mine[i][...])


def pre_kernel(where, *rest):
    pick_factors(where, rest[:2], rest[2:6], *rest[6:8], rest[8:16], rest[16:])


FACTORS = [
    shape((BLK, HD)),
    shape((BLK, HD)),
    shape((BLK, HALF), F32),
    shape((BLK, HALF), F32),
]


def pre_own(where, own, own2, wg, wu):
    return call(pre_own_kernel, "pre_own", FACTORS * 2)(where, own, own2, wg, wu)


def pre(where, halves, mine, wg, wu):
    work = [pltpu.VMEM(f.shape, f.dtype) for f in FACTORS]
    outs = call(pre_kernel, "pre", FACTORS * 2, work)(where, *halves, *mine, wg, wu)
    return outs[:4], outs[4:]


def attend(q, rate, tile_a, tile_b, tile_c, a_ok, b_ok, att, err):
    scale = 1.0 / math.sqrt(HD)
    p = lax.broadcasted_iota(jnp.int32, (HALF, HALF), 0)
    j = lax.broadcasted_iota(jnp.int32, (HALF, HALF), 1)
    causal = j <= p
    neg = jnp.float32(-jnp.inf)
    zero = jnp.zeros((HALF, HALF), BF)

    def key(tile):
        return tile[:, 0:HD]

    def value(tile):
        return tile[:, HD : 2 * HD]

    for c in range(2):
        rows = pl.ds(c * HALF, HALF)
        qc = q(rows)
        tiles = []
        for t in range(2):
            if t <= c:
                sc = mm_t(qc, key(tile_c(t))) * scale
            if t >= c:
                sa = mm_t(qc, key(tile_a(t))) * scale
                if a_ok is not None:
                    sa = jnp.where(a_ok, sa, neg)
            tiles.append(sc if t < c else sa if t > c else jnp.where(causal, sc, sa))
        for t in range(2):
            sb = mm_t(qc, key(tile_b(t))) * scale
            tiles.append(sb if b_ok is None else jnp.where(b_ok, sb, neg))
        top = functools.reduce(jnp.maximum, [jnp.max(s, -1, keepdims=True) for s in tiles])
        expo = [jnp.exp(s - top) for s in tiles]
        total = functools.reduce(jnp.add, [jnp.sum(e, -1, keepdims=True) for e in expo])
        inv = 1.0 / total
        w = [(e * inv).astype(BF) for e in expo]
        acc = mm_n(w[2], value(tile_b(0))) + mm_n(w[3], value(tile_b(1)))
        for t in range(2):
            if t <= c:
                acc += mm_n(
                    jnp.where(causal, w[t], zero) if t == c else w[t], value(tile_c(t))
                )
            if t >= c:
                acc += mm_n(
                    jnp.where(causal, zero, w[t]) if t == c else w[t], value(tile_a(t))
                )
        out = acc.astype(BF)
        att[rows, :] = out
        err[rows, :] = (-rate[c * HALF : (c + 1) * HALF] * out.astype(F32)).astype(BF)


def column(mine, side, rates, q_for):
    parts = q_for[BLK : BLK + RATE_ROWS, :].astype(F32)
    other = parts[0:1, :] + parts[1:2, :] + parts[2:3, :]
    own = jnp.where(side == 0, rates[0:1, :], rates[1:2, :])
    line = jnp.where(mine, own, other)
    return jnp.transpose(jnp.broadcast_to(line, (8, BLK)))[:, 0:1]


def rows_of(ref):
    return lambda t: ref[t * HALF : (t + 1) * HALF, :]


def upper_kernel(
    where, q_own, q_for, rates, own, for_a, for_b, own2, for2_a, for2_b, *rest
):
    att, err, low, low2, high, mid = rest
    bottom = where[0] == 0
    first = where[1] == 0
    for c, (f, f2) in enumerate(((for_a, for2_a), (for_b, for2_b))):
        rows = pl.ds(c * HALF, HALF)
        low[rows, :] = jnp.where(bottom, own[rows, :], f[...])
        high[rows, :] = jnp.where(bottom, f[...], own[rows, :])
        l2 = jnp.where(bottom, own2[rows, :], f2[...])
        low2[rows, :] = l2
        mid[rows, :] = jnp.where(first, l2, jnp.where(bottom, f2[...], own2[rows, :]))
    mine = where[0] == 1
    q = lambda rows: jnp.where(mine, q_own[rows, :], q_for[rows, :])
    r = column(mine, where[0], rates, q_for)
    attend(q, r, rows_of(low), rows_of(mid), rows_of(high), None, None, att, err)


def lower_kernel(
    where, q_own, q_for, rates, halo_a, halo_b, halo2_a, halo2_b, low2, c, att_up, *rest
):
    att_own, att_for, err, att, b = rest
    bottom = where[0] == 0
    first = where[1] == 0
    inner = where[2] > 0
    for t, h in enumerate((halo2_a, halo2_b)):
        rows = pl.ds(t * HALF, HALF)
        b[rows, :] = jnp.where(first, h[...], low2[rows, :])
    q = lambda rows: jnp.where(bottom, q_own[rows, :], q_for[rows, :])
    r = column(bottom, where[0], rates, q_for)
    halo = (halo_a, halo_b)
    attend(
        q, r, lambda t: halo[t][...], rows_of(b), rows_of(c), inner, inner | ~first, att, err
    )
    att_own[...] = jnp.where(bottom, att[...], att_up[...])
    att_for[...] = jnp.where(bottom, att_up[...], att[...])


def half_of(core, ref):
    return jnp.where(core == 0, ref[:, 0:HALF], ref[:, HALF:HD])


def add_products(where, errs, kns, gateds, slopes, acts, w, total):
    core = where[1]
    w_half = half_of(core, w)
    for e, kn, gated, slope, act in zip(errs, kns, gateds, slopes, acts, strict=True):
        back = mm_n(e[...], w_half)
        total[0] += mm_rows((back * slope[...]).astype(BF), kn[...])
        total[1] += mm_rows((back * act[...]).astype(BF), kn[...])
        total[2] += mm_rows(half_of(core, e), gated[...])


def grad_first_kernel(where, e0, e1, k0, k1, g0, g1, s0, s1, a0, a1, w, total):
    total[...] = jnp.zeros_like(total)
    add_products(where, (e0, e1), (k0, k1), (g0, g1), (s0, s1), (a0, a1), w, total)


def grad_second_kernel(
    zs, where, e0, e1, k0, k1, g0, g1, s0, s1, a0, a1, w, before, own, *rest
):
    sends, total = rest[:-1], rest[-1]
    total[...] = before[...]
    add_products(where, (e0, e1), (k0, k1), (g0, g1), (s0, s1), (a0, a1), w, total)
    rows = HALF // zs
    for d in range(zs):
        src = pl.ds(pl.multiple_of(lax.rem(where[2] + d, zs) * rows, rows), rows)
        for kind in range(3):
            if d == 0:
                own[kind] = total[kind, src, :]
            else:
                sends[d - 1][kind] = total[kind, src, :].astype(BF)


def update_kernel(zs, where, own, *rest):
    got, olds, piece = rest[:-4], rest[-4:-1], rest[-1]
    rows = HALF // zs
    mine = pl.ds(pl.multiple_of(where[1] * HALF + where[2] * rows, rows), rows)
    for kind in range(3):
        grad = own[kind]
        for g in got:
            grad = grad + g[kind].astype(F32)
        old = olds[kind][mine, :].astype(F32)
        raised = old - grad
        factor = jnp.sqrt(jnp.mean(old * old, -1, keepdims=True) + 1e-06) * lax.rsqrt(
            jnp.mean(raised * raised, -1, keepdims=True) + 1e-06
        )
        piece[kind] = (raised * factor).astype(BF)


def gather(zs, where, pieces, kinds, full):
    rows = HALF // zs
    for side, some in ((where[1], pieces[:zs]), (1 - where[1], pieces[zs:])):
        for d in range(zs):
            at = side * HALF + lax.rem(where[2] - d + zs, zs) * rows
            for kind in range(kinds):
                full[pl.ds(pl.multiple_of(kind * HD + at, rows), rows), :] = some[d][kind]


def read(qn, att, full, out, head, work, sems):
    column = pl.ds(pl.multiple_of(head * HD, HD), HD)
    copies = []
    for c in range(2):
        rows = pl.ds(c * HALF, HALF)
        x = qn(rows)
        hg = mm_t(x, full[0:HD, :])
        hu = mm_t(x, full[HD : 2 * HD, :])
        g = (hg * jax.nn.sigmoid(hg) * hu).astype(BF)
        fast = mm_t(g, full[2 * HD : 3 * HD, :])
        work[rows, :] = (att[rows, :].astype(F32) + fast).astype(BF)
        copy = pltpu.make_async_copy(work.at[rows, :], out.at[rows, column], sems.at[c])
        copy.start()
        copies.append(copy)
    for copy in copies:
        copy.wait()


def read_own_kernel(zs, where, *rest):
    pieces, (q, att, q_rest, out, full, qn_rest, work, sems) = rest[: 2 * zs], rest[2 * zs :]
    gather(zs, where, pieces, 3, full)
    qn_rest[...] = rms(q_rest[...])
    read(lambda rows: rms(q[rows, :]), att, full, out, where[0], work, sems)


def read_own(zs, where, pieces, q, att, q_rest):
    return pl.pallas_call(
        functools.partial(read_own_kernel, zs),
        in_specs=[SM] + [VM] * (2 * zs + 3),
        out_specs=[pl.BlockSpec(memory_space=pl.ANY), VM, VM],
        out_shape=[shape((BLK, H * HD)), shape((3 * HD, HD)), shape((BLK, HD))],
        scratch_shapes=[pltpu.VMEM((BLK, HD), BF), pltpu.SemaphoreType.DMA((2,))],
        compiler_params=PARAMS,
        name="read_own",
    )(where, *pieces, q, att, q_rest)


def read_other_kernel(zs, count, where, *rest):
    pieces, (qn, att, mine, half_filled, out, weights, full, work, sems) = (
        rest[: 2 * zs],
        rest[2 * zs :],
    )
    y, core, z = where[0], where[1], where[2]
    gather(zs, where, pieces, 3, full)
    step = math.gcd(count, HD)
    first = ((z * 2 + y) * 2 + core) * count
    for c in range(count // step):
        r = first + c * step
        head = lax.rem(lax.div(r, HD), 2)
        at = lax.div(r, 2 * HD) * HD + lax.rem(r, HD)
        rows = pl.ds(pl.multiple_of(at, step), step)
        weights[c * step : (c + 1) * step, :] = jnp.where(head == y, mine[rows, :], full[rows, :])
    read(lambda rows: qn[rows, :], att, full, out, 1 - y, work, sems)


def read_other(zs, where, count, pieces, qn, att, mine, half_filled):
    anyspec = pl.BlockSpec(memory_space=pl.ANY)
    return pl.pallas_call(
        functools.partial(read_other_kernel, zs, count),
        in_specs=[SM] + [VM] * (2 * zs + 3) + [anyspec],
        out_specs=[anyspec, VM],
        out_shape=[shape((BLK, H * HD)), shape((count, HD))],
        scratch_shapes=[
            pltpu.VMEM((3 * HD, HD), BF),
            pltpu.VMEM((BLK, HD), BF),
            pltpu.SemaphoreType.DMA((2,)),
        ],
        input_output_aliases={2 * zs + 4: 0},
        compiler_params=PARAMS,
        name="read_other",
    )(where, *pieces, qn, att, mine, half_filled)


def local(queries, key_rows, value_rows, step_rates, w_gate, w_up, w_down):
    zs = lax.axis_size("z")
    z, y, core = lax.axis_index("z"), lax.axis_index("y"), lax.axis_index("core")
    where = jnp.stack([y, core, z]).astype(jnp.int32)
    rows = HALF // zs

    def swap(value, axis):
        return lax.ppermute(value, axis, SWAP)

    def shift(value, d, ring=True):
        return lax.ppermute(
            value, "z", [(i, (i + d) % zs) for i in range(zs) if ring or i + d < zs]
        )

    two = [shape((BLK, HD))] * 2

    def after(value, earlier):
        return lax.optimization_barrier((value, earlier))[0]

    q_other = pl.BlockSpec((BLK, HD), lambda i, s: (0, 1 - s[0]))
    sent_a = pack(where, key_rows, value_rows, 0, HALF, False)
    sent_b = pack(where, after(key_rows, sent_a), value_rows, HALF, HALF, False)
    sent_q = call_blocks(
        pack_q_kernel, "pack_q", [q_other, None], [shape((BLK + RATE_ROWS, HD))]
    )(where, in_hbm(after(queries, sent_b)), step_rates)[0]
    own = pack(where, after(key_rows, sent_b), value_rows, 0, BLK, True)
    theirs = [swap(sent_a, "y"), swap(sent_b, "y")]
    q_own = jnp.where(y == 0, queries[:, :HD], queries[:, HD:])
    q_rest = jnp.where(y == 0, queries[:, HD:], queries[:, :HD])
    weights = [jnp.where(y == 0, w[:HD], w[HD:]) for w in (w_gate, w_up, w_down)]
    theirs[0], sent_q, q_own, (wg, wu, wd) = lax.optimization_barrier(
        (theirs[0], sent_q, q_own, weights)
    )
    q_for = swap(sent_q, "y")
    own2 = swap(own, "core")
    gone = pick(where, theirs[0], own, 0)
    halo_a = shift(gone, 1, ring=False)
    theirs2 = [swap(after(theirs[0], gone), "core")]
    mine = pre_own(where, own, own2, wg, wu)
    theirs[1], mine, theirs2[0] = lax.optimization_barrier((theirs[1], mine, theirs2[0]))
    gone = pick(where, theirs[1], own, 1)
    halo_b = shift(gone, 1, ring=False)
    theirs2.append(swap(after(theirs[1], gone), "core"))
    theirs2, halo_a = lax.optimization_barrier((theirs2, halo_a))
    low, high = pre(where, theirs, mine[:4], wg, wu)
    theirs2, low, q_for = lax.optimization_barrier((theirs2, low, q_for))
    low2, high2 = pre(where, theirs2, mine[4:], wg, wu)
    low2, q_for = lax.optimization_barrier((low2, q_for))

    pair = shape((BLK, 2 * HD))
    att_up, err_up, kv_low, kv_low2 = call(
        upper_kernel, "attend_upper", two + [pair] * 2, [pltpu.VMEM(pair.shape, BF)] * 2
    )(where, q_own, q_for, step_rates, own, *theirs, own2, *theirs2)
    err_up, halo = lax.optimization_barrier((err_up, (halo_a, halo_b)))
    halo2 = [swap(h, "core") for h in halo]
    err_up2 = swap(err_up, "core")
    att_own, att_for, err_low = call(
        lower_kernel,
        "attend_lower",
        [shape((BLK, HD))] * 3,
        [pltpu.VMEM((BLK, HD), BF), pltpu.VMEM((BLK, 2 * HD), BF)],
    )(where, q_own, q_for, step_rates, *halo, *halo2, kv_low2, kv_low, att_up)
    err_low2 = swap(err_low, "core")

    def factors_of(*blocks):
        return [block[n] for n in range(4) for block in blocks]

    total = shape((3, HALF, HD), F32)
    before = call(grad_first_kernel, "grad_first", [total])(
        where, err_up, err_up2, *factors_of(high, high2), wd
    )[0]
    own_sum, *sends = call(
        functools.partial(grad_second_kernel, zs),
        "grad_second",
        [shape((3, rows, HD), F32)] + [shape((3, rows, HD))] * (zs - 1),
        [pltpu.VMEM(total.shape, F32)],
    )(where, err_low, err_low2, *factors_of(low, low2), wd, before)
    got = [shift(s, d) for d, s in enumerate(sends, 1)]
    att_back = swap(after(att_for, own_sum), "y")
    got, att_back = lax.optimization_barrier((got, att_back))
    piece = call(functools.partial(update_kernel, zs), "update", [shape((3, rows, HD))])(
        where, own_sum, *got, wg, wu, wd
    )[0]
    order = [*range(2, zs - 1), 1, zs - 1]
    pieces = {d: shift(piece, d) for d in order}
    pieces = [piece] + [pieces[d] for d in range(1, zs)]
    others = {d: swap(pieces[d], "y") for d in [*order, 0]}
    others = [others[d] for d in range(zs)]
    gate = [*pieces[1:], others[0], others[zs - 1], others[1]]
    pieces2 = [swap(after(p, gate), "core") for p in pieces]
    pieces2, others = lax.optimization_barrier((pieces2, others))
    others2 = [swap(p, "core") for d, p in enumerate(others)]
    half_filled, full, qn_rest = read_own(zs, where, pieces + pieces2, q_own, att_own, q_rest)
    count = 3 * H * HD // (4 * zs)
    return tuple(
        read_other(
            zs, where, count, others + others2, qn_rest, att_back, full, half_filled
        )
    )


def solution(mesh):
    groups, ctx = mesh.devices.shape
    split = Mesh(mesh.devices.reshape(groups, ctx // 4, 2, 2), ("groups", "z", "y", "core"))
    tokens = ("groups", "z", "y", "core")
    return jax.shard_map(
        local,
        mesh=split,
        in_specs=(
            P(tokens, None),
            P(tokens, None),
            P(tokens, None),
            P(None, tokens),
            P("groups", None),
            P("groups", None),
            P("groups", None),
        ),
        out_specs=(P(tokens, None), P(tokens, None)),
        check_vma=False,
    )
```

```python
import functools
import math

import jax
import jax.numpy as jnp
from jax import lax
from jax.experimental import pallas as pl
from jax.experimental.pallas import tpu as pltpu
from jax.sharding import Mesh, PartitionSpec as P

H = 2
HD = 512
BLK = 512
HALF = 256
RATE_ROWS = 16
BF = jnp.bfloat16
F32 = jnp.float32
SWAP = [(0, 1), (1, 0)]
PARAMS = pltpu.CompilerParams(vmem_limit_bytes=20 << 20)
VM = pl.BlockSpec(memory_space=pltpu.VMEM)
SM = pl.BlockSpec(memory_space=pltpu.SMEM)


def mm(a, b, dims):
    return lax.dot_general(a, b, (dims, ((), ())), preferred_element_type=F32)


def mm_t(a, b):
    return mm(a, b, ((1,), (1,)))


def mm_n(a, b):
    return mm(a, b, ((1,), (0,)))


def mm_rows(a, b):
    return mm(a, b, ((0,), (0,)))


def rms(x):
    v = x.astype(F32)
    return (v * lax.rsqrt(jnp.mean(v * v, -1, keepdims=True) + 1e-06)).astype(BF)


def in_hbm(value):
    return pltpu.with_memory_space_constraint(value, pltpu.HBM)


def shape(dims, dtype=BF):
    return jax.ShapeDtypeStruct(dims, dtype)


def call(kernel, name, outs, scratch=()):
    def run(where, *args):
        return pl.pallas_call(
            kernel,
            in_specs=[SM] + [VM] * len(args),
            out_specs=[VM] * len(outs),
            out_shape=outs,
            scratch_shapes=scratch,
            compiler_params=PARAMS,
            name=name,
        )(where, *args)

    return run


def call_blocks(kernel, name, specs, outs, scratch=()):
    def run(where, *args):
        def whole(dims):
            return pl.BlockSpec(dims, lambda i, s: (0,) * len(dims))

        in_specs = [whole(a.shape) if p is None else p for a, p in zip(args, specs, strict=True)]
        return pl.pallas_call(
            kernel,
            grid_spec=pltpu.PrefetchScalarGridSpec(
                num_scalar_prefetch=1,
                grid=(1,),
                in_specs=in_specs,
                out_specs=[whole(o.shape) for o in outs],
                scratch_shapes=scratch,
            ),
            out_shape=outs,
            compiler_params=PARAMS,
            name=name,
        )(where, *args)

    return run


def pack_kernel(first, count, own, where, key, value, out, sems):
    column = where[0] if own else 1 - where[0]
    source = (pl.ds(first, count), pl.ds(pl.multiple_of(column * HD, HD), HD))
    copies = [
        pltpu.make_async_copy(ref.at[source], out.at[:, pl.ds(n * HD, HD)], sems.at[n])
        for n, ref in enumerate((key, value))
    ]
    for copy in copies:
        copy.start()
    for copy in copies:
        copy.wait()


def pack(where, key_rows, value_rows, first, count, own):
    return pl.pallas_call(
        functools.partial(pack_kernel, first, count, own),
        in_specs=[SM] + [pl.BlockSpec(memory_space=pl.ANY)] * 2,
        out_specs=VM if own else pl.BlockSpec(memory_space=pl.ANY),
        out_shape=shape((count, 2 * HD)),
        scratch_shapes=[pltpu.SemaphoreType.DMA((2,))],
        compiler_params=PARAMS,
        name="pack",
    )(where, in_hbm(key_rows), in_hbm(value_rows))


def pick_kernel(n, where, foreign, own, out):
    out[...] = jnp.where(where[0] == 0, foreign[...], own[n * HALF : (n + 1) * HALF, :])


def pick(where, foreign, own, n):
    return call(functools.partial(pick_kernel, n), "pick", [shape((HALF, 2 * HD))])(
        where, foreign, own
    )[0]


def pack_q_kernel(where, query, rates, sent):
    sent[0:BLK, :] = query[...]
    rate = jnp.where(where[0] == 0, rates[1:2, :], rates[0:1, :])
    parts = []
    for _ in range(3):
        part = rate.astype(BF)
        parts.append(part)
        rate = rate - part.astype(F32)
    row = lax.broadcasted_iota(jnp.int32, (RATE_ROWS, BLK), 0)
    tail = jnp.zeros((RATE_ROWS, BLK), F32)
    for n, part in enumerate(parts):
        tail = jnp.where(row == n, part.astype(F32), tail)
    sent[BLK : BLK + RATE_ROWS, :] = tail.astype(BF)


def factors(core, key, wg, wu, put):
    for c in range(2):
        rows = pl.ds(c * HALF, HALF)
        kc = rms(key(c))
        put(0, rows, slice(None), kc)
        for side in range(2):
            units = pl.ds(side * HALF, HALF)
            hg = mm_t(kc, wg[units, :])
            hu = mm_t(kc, wu[units, :])
            sig = jax.nn.sigmoid(hg)
            a = hg * sig
            put(1, rows, units, (a * hu).astype(BF))

            @pl.when(core == side)
            def _():
                put(2, rows, slice(None), hu * sig * (1.0 + hg * (1.0 - sig)))
                put(3, rows, slice(None), a)


def pre_own_kernel(where, own, own2, wg, wu, *outs):
    for n, kv in enumerate((own, own2)):

        def put(i, rows, columns, value):
            outs[4 * n + i][rows, columns] = value

        factors(where[1], lambda c: kv[c * HALF : (c + 1) * HALF, 0:HD], wg, wu, put)


def pick_factors(where, halves, mine, wg, wu, outs, work):
    def put(i, rows, columns, value):
        work[i][rows, columns] = value

    factors(where[1], lambda c: halves[c][:, 0:HD], wg, wu, put)
    bottom = where[0] == 0
    for i in range(4):
        outs[i][...] = jnp.where(bottom, mine[i][...], work[i][...])
        outs[4 + i][...] = jnp.where(bottom, work[i][...], mine[i][...])


def pre_kernel(where, *rest):
    pick_factors(where, rest[:2], rest[2:6], *rest[6:8], rest[8:16], rest[16:])


FACTORS = [
    shape((BLK, HD)),
    shape((BLK, HD)),
    shape((BLK, HALF), F32),
    shape((BLK, HALF), F32),
]


def pre_own(where, own, own2, wg, wu):
    return call(pre_own_kernel, "pre_own", FACTORS * 2)(where, own, own2, wg, wu)


def pre(where, halves, mine, wg, wu):
    work = [pltpu.VMEM(f.shape, f.dtype) for f in FACTORS]
    outs = call(pre_kernel, "pre", FACTORS * 2, work)(where, *halves, *mine, wg, wu)
    return outs[:4], outs[4:]


def attend(q, rate, tile_a, tile_b, tile_c, a_ok, b_ok, att, err):
    scale = 1.0 / math.sqrt(HD)
    p = lax.broadcasted_iota(jnp.int32, (HALF, HALF), 0)
    j = lax.broadcasted_iota(jnp.int32, (HALF, HALF), 1)
    causal = j <= p
    neg = jnp.float32(-jnp.inf)
    zero = jnp.zeros((HALF, HALF), BF)

    def key(tile):
        return tile[:, 0:HD]

    def value(tile):
        return tile[:, HD : 2 * HD]

    for c in range(2):
        rows = pl.ds(c * HALF, HALF)
        qc = q(rows)
        tiles = []
        for t in range(2):
            if t <= c:
                sc = mm_t(qc, key(tile_c(t))) * scale
            if t >= c:
                sa = mm_t(qc, key(tile_a(t))) * scale
                if a_ok is not None:
                    sa = jnp.where(a_ok, sa, neg)
            tiles.append(sc if t < c else sa if t > c else jnp.where(causal, sc, sa))
        for t in range(2):
            sb = mm_t(qc, key(tile_b(t))) * scale
            tiles.append(sb if b_ok is None else jnp.where(b_ok, sb, neg))
        top = functools.reduce(jnp.maximum, [jnp.max(s, -1, keepdims=True) for s in tiles])
        expo = [jnp.exp(s - top) for s in tiles]
        total = functools.reduce(jnp.add, [jnp.sum(e, -1, keepdims=True) for e in expo])
        inv = 1.0 / total
        w = [(e * inv).astype(BF) for e in expo]
        acc = mm_n(w[2], value(tile_b(0))) + mm_n(w[3], value(tile_b(1)))
        for t in range(2):
            if t <= c:
                acc += mm_n(
                    jnp.where(causal, w[t], zero) if t == c else w[t], value(tile_c(t))
                )
            if t >= c:
                acc += mm_n(
                    jnp.where(causal, zero, w[t]) if t == c else w[t], value(tile_a(t))
                )
        out = acc.astype(BF)
        att[rows, :] = out
        err[rows, :] = (-rate[c * HALF : (c + 1) * HALF] * out.astype(F32)).astype(BF)


def column(mine, side, rates, q_for):
    parts = q_for[BLK : BLK + RATE_ROWS, :].astype(F32)
    other = parts[0:1, :] + parts[1:2, :] + parts[2:3, :]
    own = jnp.where(side == 0, rates[0:1, :], rates[1:2, :])
    line = jnp.where(mine, own, other)
    return jnp.transpose(jnp.broadcast_to(line, (8, BLK)))[:, 0:1]


def rows_of(ref):
    return lambda t: ref[t * HALF : (t + 1) * HALF, :]


def upper_kernel(
    where, q_own, q_for, rates, own, for_a, for_b, own2, for2_a, for2_b, *rest
):
    att, err, low, low2, high, mid = rest
    bottom = where[0] == 0
    first = where[1] == 0
    for c, (f, f2) in enumerate(((for_a, for2_a), (for_b, for2_b))):
        rows = pl.ds(c * HALF, HALF)
        low[rows, :] = jnp.where(bottom, own[rows, :], f[...])
        high[rows, :] = jnp.where(bottom, f[...], own[rows, :])
        l2 = jnp.where(bottom, own2[rows, :], f2[...])
        low2[rows, :] = l2
        mid[rows, :] = jnp.where(first, l2, jnp.where(bottom, f2[...], own2[rows, :]))
    mine = where[0] == 1
    q = lambda rows: jnp.where(mine, q_own[rows, :], q_for[rows, :])
    r = column(mine, where[0], rates, q_for)
    attend(q, r, rows_of(low), rows_of(mid), rows_of(high), None, None, att, err)


def lower_kernel(
    where, q_own, q_for, rates, halo_a, halo_b, halo2_a, halo2_b, low2, c, att_up, *rest
):
    att_own, att_for, err, att, b = rest
    bottom = where[0] == 0
    first = where[1] == 0
    inner = where[2] > 0
    for t, h in enumerate((halo2_a, halo2_b)):
        rows = pl.ds(t * HALF, HALF)
        b[rows, :] = jnp.where(first, h[...], low2[rows, :])
    q = lambda rows: jnp.where(bottom, q_own[rows, :], q_for[rows, :])
    r = column(bottom, where[0], rates, q_for)
    halo = (halo_a, halo_b)
    attend(
        q, r, lambda t: halo[t][...], rows_of(b), rows_of(c), inner, inner | ~first, att, err
    )
    att_own[...] = jnp.where(bottom, att[...], att_up[...])
    att_for[...] = jnp.where(bottom, att_up[...], att[...])


def half_of(core, ref):
    return jnp.where(core == 0, ref[:, 0:HALF], ref[:, HALF:HD])


def add_products(where, errs, kns, gateds, slopes, acts, w, total):
    core = where[1]
    w_half = half_of(core, w)
    for e, kn, gated, slope, act in zip(errs, kns, gateds, slopes, acts, strict=True):
        back = mm_n(e[...], w_half)
        total[0] += mm_rows((back * slope[...]).astype(BF), kn[...])
        total[1] += mm_rows((back * act[...]).astype(BF), kn[...])
        total[2] += mm_rows(half_of(core, e), gated[...])


def grad_first_kernel(where, e0, e1, k0, k1, g0, g1, s0, s1, a0, a1, w, total):
    total[...] = jnp.zeros_like(total)
    add_products(where, (e0, e1), (k0, k1), (g0, g1), (s0, s1), (a0, a1), w, total)


def grad_second_kernel(
    zs, where, e0, e1, k0, k1, g0, g1, s0, s1, a0, a1, w, before, own, *rest
):
    sends, total = rest[:-1], rest[-1]
    total[...] = before[...]
    add_products(where, (e0, e1), (k0, k1), (g0, g1), (s0, s1), (a0, a1), w, total)
    rows = HALF // zs
    for d in range(zs):
        src = pl.ds(pl.multiple_of(lax.rem(where[2] + d, zs) * rows, rows), rows)
        for kind in range(3):
            if d == 0:
                own[kind] = total[kind, src, :]
            else:
                sends[d - 1][kind] = total[kind, src, :].astype(BF)


def update_kernel(zs, where, own, *rest):
    got, olds, piece = rest[:-4], rest[-4:-1], rest[-1]
    rows = HALF // zs
    mine = pl.ds(pl.multiple_of(where[1] * HALF + where[2] * rows, rows), rows)
    for kind in range(3):
        grad = own[kind]
        for g in got:
            grad = grad + g[kind].astype(F32)
        old = olds[kind][mine, :].astype(F32)
        raised = old - grad
        factor = jnp.sqrt(jnp.mean(old * old, -1, keepdims=True) + 1e-06) * lax.rsqrt(
            jnp.mean(raised * raised, -1, keepdims=True) + 1e-06
        )
        piece[kind] = (raised * factor).astype(BF)


def gather(zs, where, pieces, kinds, full):
    rows = HALF // zs
    for side, some in ((where[1], pieces[:zs]), (1 - where[1], pieces[zs:])):
        for d in range(zs):
            at = side * HALF + lax.rem(where[2] - d + zs, zs) * rows
            for kind in range(kinds):
                full[pl.ds(pl.multiple_of(kind * HD + at, rows), rows), :] = some[d][kind]


def read(qn, att, full, out, head, work, sems):
    column = pl.ds(pl.multiple_of(head * HD, HD), HD)
    copies = []
    for c in range(2):
        rows = pl.ds(c * HALF, HALF)
        x = qn(rows)
        hg = mm_t(x, full[0:HD, :])
        hu = mm_t(x, full[HD : 2 * HD, :])
        g = (hg * jax.nn.sigmoid(hg) * hu).astype(BF)
        fast = mm_t(g, full[2 * HD : 3 * HD, :])
        work[rows, :] = (att[rows, :].astype(F32) + fast).astype(BF)
        copy = pltpu.make_async_copy(work.at[rows, :], out.at[rows, column], sems.at[c])
        copy.start()
        copies.append(copy)
    for copy in copies:
        copy.wait()


def read_own_kernel(zs, where, *rest):
    pieces, (q, att, q_rest, out, full, qn_rest, work, sems) = rest[: 2 * zs], rest[2 * zs :]
    gather(zs, where, pieces, 3, full)
    qn_rest[...] = rms(q_rest[...])
    read(lambda rows: rms(q[rows, :]), att, full, out, where[0], work, sems)


def read_own(zs, where, pieces, q, att, q_rest):
    return pl.pallas_call(
        functools.partial(read_own_kernel, zs),
        in_specs=[SM] + [VM] * (2 * zs + 3),
        out_specs=[pl.BlockSpec(memory_space=pl.ANY), VM, VM],
        out_shape=[shape((BLK, H * HD)), shape((3 * HD, HD)), shape((BLK, HD))],
        scratch_shapes=[pltpu.VMEM((BLK, HD), BF), pltpu.SemaphoreType.DMA((2,))],
        compiler_params=PARAMS,
        name="read_own",
    )(where, *pieces, q, att, q_rest)


def collect_kernel(zs, count, where, *rest):
    pieces, (mine, full, weights) = rest[: 2 * zs], rest[2 * zs :]
    y, core, z = where[0], where[1], where[2]
    gather(zs, where, pieces, 3, full)
    step = math.gcd(count, HD)
    first = ((z * 2 + y) * 2 + core) * count
    for c in range(count // step):
        r = first + c * step
        head = lax.rem(lax.div(r, HD), 2)
        at = lax.div(r, 2 * HD) * HD + lax.rem(r, HD)
        rows = pl.ds(pl.multiple_of(at, step), step)
        weights[c * step : (c + 1) * step, :] = jnp.where(head == y, mine[rows, :], full[rows, :])


def read_other_kernel(where, qn, att, full, half_filled, out, work, sems):
    read(lambda rows: qn[rows, :], att, full, out, 1 - where[0], work, sems)


def read_other(where, qn, att, full, half_filled):
    anyspec = pl.BlockSpec(memory_space=pl.ANY)
    return pl.pallas_call(
        read_other_kernel,
        in_specs=[SM] + [VM] * 3 + [anyspec],
        out_specs=anyspec,
        out_shape=shape((BLK, H * HD)),
        scratch_shapes=[pltpu.VMEM((BLK, HD), BF), pltpu.SemaphoreType.DMA((2,))],
        input_output_aliases={4: 0},
        compiler_params=PARAMS,
        name="read_other",
    )(where, qn, att, full, half_filled)


def local(queries, key_rows, value_rows, step_rates, w_gate, w_up, w_down):
    zs = lax.axis_size("z")
    z, y, core = lax.axis_index("z"), lax.axis_index("y"), lax.axis_index("core")
    where = jnp.stack([y, core, z]).astype(jnp.int32)
    rows = HALF // zs

    def swap(value, axis):
        return lax.ppermute(value, axis, SWAP)

    def shift(value, d, ring=True):
        return lax.ppermute(
            value, "z", [(i, (i + d) % zs) for i in range(zs) if ring or i + d < zs]
        )

    two = [shape((BLK, HD))] * 2

    def after(value, earlier):
        return lax.optimization_barrier((value, earlier))[0]

    q_other = pl.BlockSpec((BLK, HD), lambda i, s: (0, 1 - s[0]))
    sent_a = pack(where, key_rows, value_rows, 0, HALF, False)
    sent_b = pack(where, after(key_rows, sent_a), value_rows, HALF, HALF, False)
    sent_q = call_blocks(
        pack_q_kernel, "pack_q", [q_other, None], [shape((BLK + RATE_ROWS, HD))]
    )(where, in_hbm(after(queries, sent_b)), step_rates)[0]
    own = pack(where, after(key_rows, sent_b), value_rows, 0, BLK, True)
    theirs = [swap(sent_a, "y"), swap(sent_b, "y")]
    q_own = jnp.where(y == 0, queries[:, :HD], queries[:, HD:])
    q_rest = jnp.where(y == 0, queries[:, HD:], queries[:, :HD])
    weights = [jnp.where(y == 0, w[:HD], w[HD:]) for w in (w_gate, w_up, w_down)]
    theirs[0], sent_q, q_own, (wg, wu, wd) = lax.optimization_barrier(
        (theirs[0], sent_q, q_own, weights)
    )
    q_for = swap(sent_q, "y")
    own2 = swap(own, "core")
    gone = pick(where, theirs[0], own, 0)
    halo_a = shift(gone, 1, ring=False)
    theirs2 = [swap(after(theirs[0], gone), "core")]
    mine = pre_own(where, own, own2, wg, wu)
    theirs[1], mine, theirs2[0] = lax.optimization_barrier((theirs[1], mine, theirs2[0]))
    gone = pick(where, theirs[1], own, 1)
    halo_b = shift(gone, 1, ring=False)
    theirs2.append(swap(after(theirs[1], gone), "core"))
    theirs2, halo_a = lax.optimization_barrier((theirs2, halo_a))
    low, high = pre(where, theirs, mine[:4], wg, wu)
    theirs2, low, q_for = lax.optimization_barrier((theirs2, low, q_for))
    low2, high2 = pre(where, theirs2, mine[4:], wg, wu)
    low2, q_for = lax.optimization_barrier((low2, q_for))

    pair = shape((BLK, 2 * HD))
    att_up, err_up, kv_low, kv_low2 = call(
        upper_kernel, "attend_upper", two + [pair] * 2, [pltpu.VMEM(pair.shape, BF)] * 2
    )(where, q_own, q_for, step_rates, own, *theirs, own2, *theirs2)
    err_up, halo = lax.optimization_barrier((err_up, (halo_a, halo_b)))
    halo2 = [swap(h, "core") for h in halo]
    err_up2 = swap(err_up, "core")
    att_own, att_for, err_low = call(
        lower_kernel,
        "attend_lower",
        [shape((BLK, HD))] * 3,
        [pltpu.VMEM((BLK, HD), BF), pltpu.VMEM((BLK, 2 * HD), BF)],
    )(where, q_own, q_for, step_rates, *halo, *halo2, kv_low2, kv_low, att_up)
    err_low2 = swap(err_low, "core")

    def factors_of(*blocks):
        return [block[n] for n in range(4) for block in blocks]

    total = shape((3, HALF, HD), F32)
    before = call(grad_first_kernel, "grad_first", [total])(
        where, err_up, err_up2, *factors_of(high, high2), wd
    )[0]
    own_sum, *sends = call(
        functools.partial(grad_second_kernel, zs),
        "grad_second",
        [shape((3, rows, HD), F32)] + [shape((3, rows, HD))] * (zs - 1),
        [pltpu.VMEM(total.shape, F32)],
    )(where, err_low, err_low2, *factors_of(low, low2), wd, before)
    got = [shift(s, d) for d, s in enumerate(sends, 1)]
    att_back = swap(after(att_for, own_sum), "y")
    got, att_back = lax.optimization_barrier((got, att_back))
    piece = call(functools.partial(update_kernel, zs), "update", [shape((3, rows, HD))])(
        where, own_sum, *got, wg, wu, wd
    )[0]
    order = [*range(2, zs - 1), 1, zs - 1]
    pieces = {d: shift(piece, d) for d in order}
    pieces = [piece] + [pieces[d] for d in range(1, zs)]
    others = {d: swap(pieces[d], "y") for d in [*order, 0]}
    others = [others[d] for d in range(zs)]
    gate = [*pieces[1:], others[0], others[zs - 1], others[1]]
    pieces2 = [swap(after(p, gate), "core") for p in pieces]
    half_filled, full, qn_rest = read_own(zs, where, pieces + pieces2, q_own, att_own, q_rest)
    far = range(2, zs - 1)
    others2 = [swap(after(p, full) if d in far else p, "core") for d, p in enumerate(others)]
    count = 3 * H * HD // (4 * zs)
    full_rest, own_weights = call(
        functools.partial(collect_kernel, zs, count),
        "collect",
        [shape((3 * HD, HD)), shape((count, HD))],
    )(where, *others, *others2, full)
    return read_other(where, qn_rest, att_back, full_rest, half_filled), own_weights


def solution(mesh):
    groups, ctx = mesh.devices.shape
    split = Mesh(mesh.devices.reshape(groups, ctx // 4, 2, 2), ("groups", "z", "y", "core"))
    tokens = ("groups", "z", "y", "core")
    return jax.shard_map(
        local,
        mesh=split,
        in_specs=(
            P(tokens, None),
            P(tokens, None),
            P(tokens, None),
            P(None, tokens),
            P("groups", None),
            P("groups", None),
            P("groups", None),
        ),
        out_specs=(P(tokens, None), P(tokens, None)),
        check_vma=False,
    )
```

```python
import functools
import math

import jax
import jax.numpy as jnp
from jax import lax
from jax.experimental import pallas as pl
from jax.experimental.pallas import tpu as pltpu
from jax.sharding import Mesh, PartitionSpec as P

H = 2
HD = 512
BLK = 512
HALF = 256
RATE_ROWS = 16
BF = jnp.bfloat16
F32 = jnp.float32
SWAP = [(0, 1), (1, 0)]
PARAMS = pltpu.CompilerParams(vmem_limit_bytes=20 << 20)
VM = pl.BlockSpec(memory_space=pltpu.VMEM)
SM = pl.BlockSpec(memory_space=pltpu.SMEM)


def mm(a, b, dims):
    return lax.dot_general(a, b, (dims, ((), ())), preferred_element_type=F32)


def mm_t(a, b):
    return mm(a, b, ((1,), (1,)))


def mm_n(a, b):
    return mm(a, b, ((1,), (0,)))


def mm_rows(a, b):
    return mm(a, b, ((0,), (0,)))


def rms(x):
    v = x.astype(F32)
    return (v * lax.rsqrt(jnp.mean(v * v, -1, keepdims=True) + 1e-06)).astype(BF)


def in_hbm(value):
    return pltpu.with_memory_space_constraint(value, pltpu.HBM)


def shape(dims, dtype=BF):
    return jax.ShapeDtypeStruct(dims, dtype)


def call(kernel, name, outs, scratch=()):
    def run(where, *args):
        return pl.pallas_call(
            kernel,
            in_specs=[SM] + [VM] * len(args),
            out_specs=[VM] * len(outs),
            out_shape=outs,
            scratch_shapes=scratch,
            compiler_params=PARAMS,
            name=name,
        )(where, *args)

    return run


def call_blocks(kernel, name, specs, outs, scratch=()):
    def run(where, *args):
        def whole(dims):
            return pl.BlockSpec(dims, lambda i, s: (0,) * len(dims))

        in_specs = [whole(a.shape) if p is None else p for a, p in zip(args, specs, strict=True)]
        return pl.pallas_call(
            kernel,
            grid_spec=pltpu.PrefetchScalarGridSpec(
                num_scalar_prefetch=1,
                grid=(1,),
                in_specs=in_specs,
                out_specs=[whole(o.shape) for o in outs],
                scratch_shapes=scratch,
            ),
            out_shape=outs,
            compiler_params=PARAMS,
            name=name,
        )(where, *args)

    return run


def pack_kernel(first, count, own, where, key, value, out, sems):
    column = where[0] if own else 1 - where[0]
    source = (pl.ds(first, count), pl.ds(pl.multiple_of(column * HD, HD), HD))
    copies = [
        pltpu.make_async_copy(ref.at[source], out.at[:, pl.ds(n * HD, HD)], sems.at[n])
        for n, ref in enumerate((key, value))
    ]
    for copy in copies:
        copy.start()
    for copy in copies:
        copy.wait()


def pack(where, key_rows, value_rows, first, count, own):
    return pl.pallas_call(
        functools.partial(pack_kernel, first, count, own),
        in_specs=[SM] + [pl.BlockSpec(memory_space=pl.ANY)] * 2,
        out_specs=VM,
        out_shape=shape((count, 2 * HD)),
        scratch_shapes=[pltpu.SemaphoreType.DMA((2,))],
        compiler_params=PARAMS,
        name="pack",
    )(where, in_hbm(key_rows), in_hbm(value_rows))


def pick_kernel(n, where, foreign, own, out):
    out[...] = jnp.where(where[0] == 0, foreign[...], own[n * HALF : (n + 1) * HALF, :])


def pick(where, foreign, own, n):
    return call(functools.partial(pick_kernel, n), "pick", [shape((HALF, 2 * HD))])(
        where, foreign, own
    )[0]


def pack_q_kernel(where, query, rates, sent):
    sent[0:BLK, :] = query[...]
    rate = jnp.where(where[0] == 0, rates[1:2, :], rates[0:1, :])
    parts = []
    for _ in range(3):
        part = rate.astype(BF)
        parts.append(part)
        rate = rate - part.astype(F32)
    row = lax.broadcasted_iota(jnp.int32, (RATE_ROWS, BLK), 0)
    tail = jnp.zeros((RATE_ROWS, BLK), F32)
    for n, part in enumerate(parts):
        tail = jnp.where(row == n, part.astype(F32), tail)
    sent[BLK : BLK + RATE_ROWS, :] = tail.astype(BF)


def factors(core, key, wg, wu, put):
    for c in range(2):
        rows = pl.ds(c * HALF, HALF)
        kc = rms(key(c))
        put(0, rows, slice(None), kc)
        for side in range(2):
            units = pl.ds(side * HALF, HALF)
            hg = mm_t(kc, wg[units, :])
            hu = mm_t(kc, wu[units, :])
            sig = jax.nn.sigmoid(hg)
            a = hg * sig
            put(1, rows, units, (a * hu).astype(BF))

            @pl.when(core == side)
            def _():
                put(2, rows, slice(None), hu * sig * (1.0 + hg * (1.0 - sig)))
                put(3, rows, slice(None), a)


def pre_own_kernel(where, own, own2, wg, wu, *outs):
    for n, kv in enumerate((own, own2)):

        def put(i, rows, columns, value):
            outs[4 * n + i][rows, columns] = value

        factors(where[1], lambda c: kv[c * HALF : (c + 1) * HALF, 0:HD], wg, wu, put)


def pick_factors(where, halves, mine, wg, wu, outs, work):
    def put(i, rows, columns, value):
        work[i][rows, columns] = value

    factors(where[1], lambda c: halves[c][:, 0:HD], wg, wu, put)
    bottom = where[0] == 0
    for i in range(4):
        outs[i][...] = jnp.where(bottom, mine[i][...], work[i][...])
        outs[4 + i][...] = jnp.where(bottom, work[i][...], mine[i][...])


def pre_kernel(where, *rest):
    pick_factors(where, rest[:2], rest[2:6], *rest[6:8], rest[8:16], rest[16:])


FACTORS = [
    shape((BLK, HD)),
    shape((BLK, HD)),
    shape((BLK, HALF), F32),
    shape((BLK, HALF), F32),
]


def pre_own(where, own, own2, wg, wu):
    return call(pre_own_kernel, "pre_own", FACTORS * 2)(where, own, own2, wg, wu)


def pre(where, halves, mine, wg, wu):
    work = [pltpu.VMEM(f.shape, f.dtype) for f in FACTORS]
    outs = call(pre_kernel, "pre", FACTORS * 2, work)(where, *halves, *mine, wg, wu)
    return outs[:4], outs[4:]


def attend(q, rate, tile_a, tile_b, tile_c, a_ok, b_ok, att, err):
    scale = 1.0 / math.sqrt(HD)
    p = lax.broadcasted_iota(jnp.int32, (HALF, HALF), 0)
    j = lax.broadcasted_iota(jnp.int32, (HALF, HALF), 1)
    causal = j <= p
    neg = jnp.float32(-jnp.inf)
    zero = jnp.zeros((HALF, HALF), BF)

    def key(tile):
        return tile[:, 0:HD]

    def value(tile):
        return tile[:, HD : 2 * HD]

    for c in range(2):
        rows = pl.ds(c * HALF, HALF)
        qc = q(rows)
        tiles = []
        for t in range(2):
            if t <= c:
                sc = mm_t(qc, key(tile_c(t))) * scale
            if t >= c:
                sa = mm_t(qc, key(tile_a(t))) * scale
                if a_ok is not None:
                    sa = jnp.where(a_ok, sa, neg)
            tiles.append(sc if t < c else sa if t > c else jnp.where(causal, sc, sa))
        for t in range(2):
            sb = mm_t(qc, key(tile_b(t))) * scale
            tiles.append(sb if b_ok is None else jnp.where(b_ok, sb, neg))
        top = functools.reduce(jnp.maximum, [jnp.max(s, -1, keepdims=True) for s in tiles])
        expo = [jnp.exp(s - top) for s in tiles]
        total = functools.reduce(jnp.add, [jnp.sum(e, -1, keepdims=True) for e in expo])
        inv = 1.0 / total
        w = [(e * inv).astype(BF) for e in expo]
        acc = mm_n(w[2], value(tile_b(0))) + mm_n(w[3], value(tile_b(1)))
        for t in range(2):
            if t <= c:
                acc += mm_n(
                    jnp.where(causal, w[t], zero) if t == c else w[t], value(tile_c(t))
                )
            if t >= c:
                acc += mm_n(
                    jnp.where(causal, zero, w[t]) if t == c else w[t], value(tile_a(t))
                )
        out = acc.astype(BF)
        att[rows, :] = out
        err[rows, :] = (-rate[c * HALF : (c + 1) * HALF] * out.astype(F32)).astype(BF)


def column(mine, side, rates, q_for):
    parts = q_for[BLK : BLK + RATE_ROWS, :].astype(F32)
    other = parts[0:1, :] + parts[1:2, :] + parts[2:3, :]
    own = jnp.where(side == 0, rates[0:1, :], rates[1:2, :])
    line = jnp.where(mine, own, other)
    return jnp.transpose(jnp.broadcast_to(line, (8, BLK)))[:, 0:1]


def rows_of(ref):
    return lambda t: ref[t * HALF : (t + 1) * HALF, :]


def upper_kernel(
    where, q_own, q_for, rates, own, for_a, for_b, own2, for2_a, for2_b, *rest
):
    att, err, low, low2, high, mid = rest
    bottom = where[0] == 0
    first = where[1] == 0
    for c, (f, f2) in enumerate(((for_a, for2_a), (for_b, for2_b))):
        rows = pl.ds(c * HALF, HALF)
        low[rows, :] = jnp.where(bottom, own[rows, :], f[...])
        high[rows, :] = jnp.where(bottom, f[...], own[rows, :])
        l2 = jnp.where(bottom, own2[rows, :], f2[...])
        low2[rows, :] = l2
        mid[rows, :] = jnp.where(first, l2, jnp.where(bottom, f2[...], own2[rows, :]))
    mine = where[0] == 1
    q = lambda rows: jnp.where(mine, q_own[rows, :], q_for[rows, :])
    r = column(mine, where[0], rates, q_for)
    attend(q, r, rows_of(low), rows_of(mid), rows_of(high), None, None, att, err)


def lower_kernel(
    where, q_own, q_for, rates, halo_a, halo_b, halo2_a, halo2_b, low2, c, att_up, *rest
):
    att_own, att_for, err, att, b = rest
    bottom = where[0] == 0
    first = where[1] == 0
    inner = where[2] > 0
    for t, h in enumerate((halo2_a, halo2_b)):
        rows = pl.ds(t * HALF, HALF)
        b[rows, :] = jnp.where(first, h[...], low2[rows, :])
    q = lambda rows: jnp.where(bottom, q_own[rows, :], q_for[rows, :])
    r = column(bottom, where[0], rates, q_for)
    halo = (halo_a, halo_b)
    attend(
        q, r, lambda t: halo[t][...], rows_of(b), rows_of(c), inner, inner | ~first, att, err
    )
    att_own[...] = jnp.where(bottom, att[...], att_up[...])
    att_for[...] = jnp.where(bottom, att_up[...], att[...])


def half_of(core, ref):
    return jnp.where(core == 0, ref[:, 0:HALF], ref[:, HALF:HD])


def add_products(where, errs, kns, gateds, slopes, acts, w, total):
    core = where[1]
    w_half = half_of(core, w)
    for e, kn, gated, slope, act in zip(errs, kns, gateds, slopes, acts, strict=True):
        back = mm_n(e[...], w_half)
        total[0] += mm_rows((back * slope[...]).astype(BF), kn[...])
        total[1] += mm_rows((back * act[...]).astype(BF), kn[...])
        total[2] += mm_rows(half_of(core, e), gated[...])


def grad_first_kernel(where, e0, e1, k0, k1, g0, g1, s0, s1, a0, a1, w, total):
    total[...] = jnp.zeros_like(total)
    add_products(where, (e0, e1), (k0, k1), (g0, g1), (s0, s1), (a0, a1), w, total)


def grad_second_kernel(
    zs, where, e0, e1, k0, k1, g0, g1, s0, s1, a0, a1, w, before, own, *rest
):
    sends, total = rest[:-1], rest[-1]
    total[...] = before[...]
    add_products(where, (e0, e1), (k0, k1), (g0, g1), (s0, s1), (a0, a1), w, total)
    rows = HALF // zs
    for d in range(zs):
        src = pl.ds(pl.multiple_of(lax.rem(where[2] + d, zs) * rows, rows), rows)
        for kind in range(3):
            if d == 0:
                own[kind] = total[kind, src, :]
            else:
                sends[d - 1][kind] = total[kind, src, :].astype(BF)


def update_kernel(zs, where, own, *rest):
    got, olds, piece = rest[:-4], rest[-4:-1], rest[-1]
    rows = HALF // zs
    mine = pl.ds(pl.multiple_of(where[1] * HALF + where[2] * rows, rows), rows)
    for kind in range(3):
        grad = own[kind]
        for g in got:
            grad = grad + g[kind].astype(F32)
        old = olds[kind][mine, :].astype(F32)
        raised = old - grad
        factor = jnp.sqrt(jnp.mean(old * old, -1, keepdims=True) + 1e-06) * lax.rsqrt(
            jnp.mean(raised * raised, -1, keepdims=True) + 1e-06
        )
        piece[kind] = (raised * factor).astype(BF)


def gather(zs, where, pieces, kinds, full):
    rows = HALF // zs
    for side, some in ((where[1], pieces[:zs]), (1 - where[1], pieces[zs:])):
        for d in range(zs):
            at = side * HALF + lax.rem(where[2] - d + zs, zs) * rows
            for kind in range(kinds):
                full[pl.ds(pl.multiple_of(kind * HD + at, rows), rows), :] = some[d][kind]


def read(qn, att, full, out, head, work, sems):
    column = pl.ds(pl.multiple_of(head * HD, HD), HD)
    copies = []
    for c in range(2):
        rows = pl.ds(c * HALF, HALF)
        x = qn(rows)
        hg = mm_t(x, full[0:HD, :])
        hu = mm_t(x, full[HD : 2 * HD, :])
        g = (hg * jax.nn.sigmoid(hg) * hu).astype(BF)
        fast = mm_t(g, full[2 * HD : 3 * HD, :])
        work[rows, :] = (att[rows, :].astype(F32) + fast).astype(BF)
        copy = pltpu.make_async_copy(work.at[rows, :], out.at[rows, column], sems.at[c])
        copy.start()
        copies.append(copy)
    for copy in copies:
        copy.wait()


def read_own_kernel(zs, where, *rest):
    pieces, (q, att, q_rest, out, full, qn_rest, work, sems) = rest[: 2 * zs], rest[2 * zs :]
    gather(zs, where, pieces, 3, full)
    qn_rest[...] = rms(q_rest[...])
    read(lambda rows: rms(q[rows, :]), att, full, out, where[0], work, sems)


def read_own(zs, where, pieces, q, att, q_rest):
    return pl.pallas_call(
        functools.partial(read_own_kernel, zs),
        in_specs=[SM] + [VM] * (2 * zs + 3),
        out_specs=[pl.BlockSpec(memory_space=pl.ANY), VM, VM],
        out_shape=[shape((BLK, H * HD)), shape((3 * HD, HD)), shape((BLK, HD))],
        scratch_shapes=[pltpu.VMEM((BLK, HD), BF), pltpu.SemaphoreType.DMA((2,))],
        compiler_params=PARAMS,
        name="read_own",
    )(where, *pieces, q, att, q_rest)


def read_other_kernel(zs, count, where, *rest):
    pieces, (qn, att, mine, half_filled, out, weights, full, work, sems) = (
        rest[: 2 * zs],
        rest[2 * zs :],
    )
    y, core, z = where[0], where[1], where[2]
    gather(zs, where, pieces, 3, full)
    step = math.gcd(count, HD)
    first = ((z * 2 + y) * 2 + core) * count
    for c in range(count // step):
        r = first + c * step
        head = lax.rem(lax.div(r, HD), 2)
        at = lax.div(r, 2 * HD) * HD + lax.rem(r, HD)
        rows = pl.ds(pl.multiple_of(at, step), step)
        weights[c * step : (c + 1) * step, :] = jnp.where(head == y, mine[rows, :], full[rows, :])
    read(lambda rows: qn[rows, :], att, full, out, 1 - y, work, sems)


def read_other(zs, where, count, pieces, qn, att, mine, half_filled):
    anyspec = pl.BlockSpec(memory_space=pl.ANY)
    return pl.pallas_call(
        functools.partial(read_other_kernel, zs, count),
        in_specs=[SM] + [VM] * (2 * zs + 3) + [anyspec],
        out_specs=[anyspec, VM],
        out_shape=[shape((BLK, H * HD)), shape((count, HD))],
        scratch_shapes=[
            pltpu.VMEM((3 * HD, HD), BF),
            pltpu.VMEM((BLK, HD), BF),
            pltpu.SemaphoreType.DMA((2,)),
        ],
        input_output_aliases={2 * zs + 4: 0},
        compiler_params=PARAMS,
        name="read_other",
    )(where, *pieces, qn, att, mine, half_filled)


def local(queries, key_rows, value_rows, step_rates, w_gate, w_up, w_down):
    zs = lax.axis_size("z")
    z, y, core = lax.axis_index("z"), lax.axis_index("y"), lax.axis_index("core")
    where = jnp.stack([y, core, z]).astype(jnp.int32)
    rows = HALF // zs

    def swap(value, axis):
        return lax.ppermute(value, axis, SWAP)

    def shift(value, d, ring=True):
        return lax.ppermute(
            value, "z", [(i, (i + d) % zs) for i in range(zs) if ring or i + d < zs]
        )

    two = [shape((BLK, HD))] * 2

    def after(value, earlier):
        return lax.optimization_barrier((value, earlier))[0]

    q_other = pl.BlockSpec((BLK, HD), lambda i, s: (0, 1 - s[0]))
    def paired(first, keys):
        rows = slice(first, first + HALF)
        left = jnp.concatenate([keys[rows, :HD], value_rows[rows, :HD]], 1)
        right = jnp.concatenate([keys[rows, HD:], value_rows[rows, HD:]], 1)
        return jnp.where(y == 0, right, left)

    sent_a = paired(0, key_rows)
    sent_b = paired(HALF, after(key_rows, sent_a))
    sent_q = call_blocks(
        pack_q_kernel, "pack_q", [q_other, None], [shape((BLK + RATE_ROWS, HD))]
    )(where, in_hbm(after(queries, sent_b)), step_rates)[0]
    own = pack(where, after(key_rows, sent_b), value_rows, 0, BLK, True)
    theirs = [swap(sent_a, "y"), swap(sent_b, "y")]
    q_own = jnp.where(y == 0, queries[:, :HD], queries[:, HD:])
    q_rest = jnp.where(y == 0, queries[:, HD:], queries[:, :HD])
    weights = [jnp.where(y == 0, w[:HD], w[HD:]) for w in (w_gate, w_up, w_down)]
    theirs[0], sent_q, q_own, (wg, wu, wd) = lax.optimization_barrier(
        (theirs[0], sent_q, q_own, weights)
    )
    q_for = swap(sent_q, "y")
    own2 = swap(own, "core")
    gone = pick(where, theirs[0], own, 0)
    halo_a = shift(gone, 1, ring=False)
    theirs2 = [swap(after(theirs[0], gone), "core")]
    mine = pre_own(where, own, own2, wg, wu)
    theirs[1], mine, theirs2[0] = lax.optimization_barrier((theirs[1], mine, theirs2[0]))
    gone = pick(where, theirs[1], own, 1)
    halo_b = shift(gone, 1, ring=False)
    theirs2.append(swap(after(theirs[1], gone), "core"))
    theirs2, halo_a = lax.optimization_barrier((theirs2, halo_a))
    low, high = pre(where, theirs, mine[:4], wg, wu)
    theirs2, low, q_for = lax.optimization_barrier((theirs2, low, q_for))
    low2, high2 = pre(where, theirs2, mine[4:], wg, wu)
    low2, q_for = lax.optimization_barrier((low2, q_for))

    pair = shape((BLK, 2 * HD))
    att_up, err_up, kv_low, kv_low2 = call(
        upper_kernel, "attend_upper", two + [pair] * 2, [pltpu.VMEM(pair.shape, BF)] * 2
    )(where, q_own, q_for, step_rates, own, *theirs, own2, *theirs2)
    err_up, halo = lax.optimization_barrier((err_up, (halo_a, halo_b)))
    halo2 = [swap(h, "core") for h in halo]
    err_up2 = swap(err_up, "core")
    att_own, att_for, err_low = call(
        lower_kernel,
        "attend_lower",
        [shape((BLK, HD))] * 3,
        [pltpu.VMEM((BLK, HD), BF), pltpu.VMEM((BLK, 2 * HD), BF)],
    )(where, q_own, q_for, step_rates, *halo, *halo2, kv_low2, kv_low, att_up)
    err_low2 = swap(err_low, "core")

    def factors_of(*blocks):
        return [block[n] for n in range(4) for block in blocks]

    total = shape((3, HALF, HD), F32)
    before = call(grad_first_kernel, "grad_first", [total])(
        where, err_up, err_up2, *factors_of(high, high2), wd
    )[0]
    own_sum, *sends = call(
        functools.partial(grad_second_kernel, zs),
        "grad_second",
        [shape((3, rows, HD), F32)] + [shape((3, rows, HD))] * (zs - 1),
        [pltpu.VMEM(total.shape, F32)],
    )(where, err_low, err_low2, *factors_of(low, low2), wd, before)
    got = [shift(s, d) for d, s in enumerate(sends, 1)]
    att_back = swap(after(att_for, own_sum), "y")
    got, att_back = lax.optimization_barrier((got, att_back))
    piece = call(functools.partial(update_kernel, zs), "update", [shape((3, rows, HD))])(
        where, own_sum, *got, wg, wu, wd
    )[0]
    order = [*range(2, zs - 1), 1, zs - 1]
    pieces = {d: shift(piece, d) for d in order}
    pieces = [piece] + [pieces[d] for d in range(1, zs)]
    others = {d: swap(pieces[d], "y") for d in [*order, 0]}
    others = [others[d] for d in range(zs)]
    gate = [*pieces[1:], others[0], others[zs - 1], others[1]]
    pieces2 = [swap(after(p, gate), "core") for p in pieces]
    pieces2, others = lax.optimization_barrier((pieces2, others))
    others2 = [swap(p, "core") for d, p in enumerate(others)]
    half_filled, full, qn_rest = read_own(zs, where, pieces + pieces2, q_own, att_own, q_rest)
    count = 3 * H * HD // (4 * zs)
    return tuple(
        read_other(
            zs, where, count, others + others2, qn_rest, att_back, full, half_filled
        )
    )


def solution(mesh):
    groups, ctx = mesh.devices.shape
    split = Mesh(mesh.devices.reshape(groups, ctx // 4, 2, 2), ("groups", "z", "y", "core"))
    tokens = ("groups", "z", "y", "core")
    return jax.shard_map(
        local,
        mesh=split,
        in_specs=(
            P(tokens, None),
            P(tokens, None),
            P(tokens, None),
            P(None, tokens),
            P("groups", None),
            P("groups", None),
            P("groups", None),
        ),
        out_specs=(P(tokens, None), P(tokens, None)),
        check_vma=False,
    )
```

```python
import functools
import math

import jax
import jax.numpy as jnp
from jax import lax
from jax.experimental import pallas as pl
from jax.experimental.pallas import tpu as pltpu
from jax.sharding import Mesh, PartitionSpec as P

H = 2
HD = 512
BLK = 512
HALF = 256
RATE_ROWS = 16
BF = jnp.bfloat16
F32 = jnp.float32
SWAP = [(0, 1), (1, 0)]
PARAMS = pltpu.CompilerParams(vmem_limit_bytes=20 << 20)
VM = pl.BlockSpec(memory_space=pltpu.VMEM)
SM = pl.BlockSpec(memory_space=pltpu.SMEM)


def mm(a, b, dims):
    return lax.dot_general(a, b, (dims, ((), ())), preferred_element_type=F32)


def mm_t(a, b):
    return mm(a, b, ((1,), (1,)))


def mm_n(a, b):
    return mm(a, b, ((1,), (0,)))


def mm_rows(a, b):
    return mm(a, b, ((0,), (0,)))


def rms(x):
    v = x.astype(F32)
    return (v * lax.rsqrt(jnp.mean(v * v, -1, keepdims=True) + 1e-06)).astype(BF)


def in_hbm(value):
    return pltpu.with_memory_space_constraint(value, pltpu.HBM)


def shape(dims, dtype=BF):
    return jax.ShapeDtypeStruct(dims, dtype)


def call(kernel, name, outs, scratch=()):
    def run(where, *args):
        return pl.pallas_call(
            kernel,
            in_specs=[SM] + [VM] * len(args),
            out_specs=[VM] * len(outs),
            out_shape=outs,
            scratch_shapes=scratch,
            compiler_params=PARAMS,
            name=name,
        )(where, *args)

    return run


def call_blocks(kernel, name, specs, outs, scratch=()):
    def run(where, *args):
        def whole(dims):
            return pl.BlockSpec(dims, lambda i, s: (0,) * len(dims))

        in_specs = [whole(a.shape) if p is None else p for a, p in zip(args, specs, strict=True)]
        return pl.pallas_call(
            kernel,
            grid_spec=pltpu.PrefetchScalarGridSpec(
                num_scalar_prefetch=1,
                grid=(1,),
                in_specs=in_specs,
                out_specs=[whole(o.shape) for o in outs],
                scratch_shapes=scratch,
            ),
            out_shape=outs,
            compiler_params=PARAMS,
            name=name,
        )(where, *args)

    return run


def pack_kernel(first, count, own, where, key, value, out, sems):
    column = where[0] if own else 1 - where[0]
    source = (pl.ds(first, count), pl.ds(pl.multiple_of(column * HD, HD), HD))
    copies = [
        pltpu.make_async_copy(ref.at[source], out.at[:, pl.ds(n * HD, HD)], sems.at[n])
        for n, ref in enumerate((key, value))
    ]
    for copy in copies:
        copy.start()
    for copy in copies:
        copy.wait()


def pack(where, key_rows, value_rows, first, count, own):
    return pl.pallas_call(
        functools.partial(pack_kernel, first, count, own),
        in_specs=[SM] + [pl.BlockSpec(memory_space=pl.ANY)] * 2,
        out_specs=VM,
        out_shape=shape((count, 2 * HD)),
        scratch_shapes=[pltpu.SemaphoreType.DMA((2,))],
        compiler_params=PARAMS,
        name="pack",
    )(where, in_hbm(key_rows), in_hbm(value_rows))


def pick_kernel(n, where, foreign, own, out):
    out[...] = jnp.where(where[0] == 0, foreign[...], own[n * HALF : (n + 1) * HALF, :])


def pick(where, foreign, own, n):
    return call(functools.partial(pick_kernel, n), "pick", [shape((HALF, 2 * HD))])(
        where, foreign, own
    )[0]


def pack_q_kernel(where, query, rates, sent):
    sent[0:BLK, :] = query[...]
    rate = jnp.where(where[0] == 0, rates[1:2, :], rates[0:1, :])
    parts = []
    for _ in range(3):
        part = rate.astype(BF)
        parts.append(part)
        rate = rate - part.astype(F32)
    row = lax.broadcasted_iota(jnp.int32, (RATE_ROWS, BLK), 0)
    tail = jnp.zeros((RATE_ROWS, BLK), F32)
    for n, part in enumerate(parts):
        tail = jnp.where(row == n, part.astype(F32), tail)
    sent[BLK : BLK + RATE_ROWS, :] = tail.astype(BF)


def factors(core, key, wg, wu, put):
    for c in range(2):
        rows = pl.ds(c * HALF, HALF)
        kc = rms(key(c))
        put(0, rows, slice(None), kc)
        for side in range(2):
            units = pl.ds(side * HALF, HALF)
            hg = mm_t(kc, wg[units, :])
            hu = mm_t(kc, wu[units, :])
            sig = jax.nn.sigmoid(hg)
            a = hg * sig
            put(1, rows, units, (a * hu).astype(BF))

            @pl.when(core == side)
            def _():
                put(2, rows, slice(None), hu * sig * (1.0 + hg * (1.0 - sig)))
                put(3, rows, slice(None), a)


def pre_own_kernel(where, own, own2, wg, wu, *outs):
    for n, kv in enumerate((own, own2)):

        def put(i, rows, columns, value):
            outs[4 * n + i][rows, columns] = value

        factors(where[1], lambda c: kv[c * HALF : (c + 1) * HALF, 0:HD], wg, wu, put)


def pick_factors(where, halves, mine, wg, wu, outs, work):
    def put(i, rows, columns, value):
        work[i][rows, columns] = value

    factors(where[1], lambda c: halves[c][:, 0:HD], wg, wu, put)
    bottom = where[0] == 0
    for i in range(4):
        outs[i][...] = jnp.where(bottom, mine[i][...], work[i][...])
        outs[4 + i][...] = jnp.where(bottom, work[i][...], mine[i][...])


def pre_kernel(where, *rest):
    pick_factors(where, rest[:2], rest[2:6], *rest[6:8], rest[8:16], rest[16:])


FACTORS = [
    shape((BLK, HD)),
    shape((BLK, HD)),
    shape((BLK, HALF), F32),
    shape((BLK, HALF), F32),
]


def pre_own(where, own, own2, wg, wu):
    return call(pre_own_kernel, "pre_own", FACTORS * 2)(where, own, own2, wg, wu)


def pre(where, halves, mine, wg, wu):
    work = [pltpu.VMEM(f.shape, f.dtype) for f in FACTORS]
    outs = call(pre_kernel, "pre", FACTORS * 2, work)(where, *halves, *mine, wg, wu)
    return outs[:4], outs[4:]


def attend(q, rate, tile_a, tile_b, tile_c, a_ok, b_ok, att, err):
    scale = 1.0 / math.sqrt(HD)
    p = lax.broadcasted_iota(jnp.int32, (HALF, HALF), 0)
    j = lax.broadcasted_iota(jnp.int32, (HALF, HALF), 1)
    causal = j <= p
    neg = jnp.float32(-jnp.inf)
    zero = jnp.zeros((HALF, HALF), BF)

    def key(tile):
        return tile[:, 0:HD]

    def value(tile):
        return tile[:, HD : 2 * HD]

    for c in range(2):
        rows = pl.ds(c * HALF, HALF)
        qc = q(rows)
        tiles = []
        for t in range(2):
            if t <= c:
                sc = mm_t(qc, key(tile_c(t))) * scale
            if t >= c:
                sa = mm_t(qc, key(tile_a(t))) * scale
                if a_ok is not None:
                    sa = jnp.where(a_ok, sa, neg)
            tiles.append(sc if t < c else sa if t > c else jnp.where(causal, sc, sa))
        for t in range(2):
            sb = mm_t(qc, key(tile_b(t))) * scale
            tiles.append(sb if b_ok is None else jnp.where(b_ok, sb, neg))
        top = functools.reduce(jnp.maximum, [jnp.max(s, -1, keepdims=True) for s in tiles])
        expo = [jnp.exp(s - top) for s in tiles]
        total = functools.reduce(jnp.add, [jnp.sum(e, -1, keepdims=True) for e in expo])
        inv = 1.0 / total
        w = [(e * inv).astype(BF) for e in expo]
        acc = mm_n(w[2], value(tile_b(0))) + mm_n(w[3], value(tile_b(1)))
        for t in range(2):
            if t <= c:
                acc += mm_n(
                    jnp.where(causal, w[t], zero) if t == c else w[t], value(tile_c(t))
                )
            if t >= c:
                acc += mm_n(
                    jnp.where(causal, zero, w[t]) if t == c else w[t], value(tile_a(t))
                )
        out = acc.astype(BF)
        att[rows, :] = out
        err[rows, :] = (-rate[c * HALF : (c + 1) * HALF] * out.astype(F32)).astype(BF)


def column(mine, side, rates, q_for):
    parts = q_for[BLK : BLK + RATE_ROWS, :].astype(F32)
    other = parts[0:1, :] + parts[1:2, :] + parts[2:3, :]
    own = jnp.where(side == 0, rates[0:1, :], rates[1:2, :])
    line = jnp.where(mine, own, other)
    return jnp.transpose(jnp.broadcast_to(line, (8, BLK)))[:, 0:1]


def rows_of(ref):
    return lambda t: ref[t * HALF : (t + 1) * HALF, :]


def upper_kernel(
    where, q_own, q_for, rates, own, for_a, for_b, own2, for2_a, for2_b, *rest
):
    att, err, low, low2, high, mid = rest
    bottom = where[0] == 0
    first = where[1] == 0
    for c, (f, f2) in enumerate(((for_a, for2_a), (for_b, for2_b))):
        rows = pl.ds(c * HALF, HALF)
        low[rows, :] = jnp.where(bottom, own[rows, :], f[...])
        high[rows, :] = jnp.where(bottom, f[...], own[rows, :])
        l2 = jnp.where(bottom, own2[rows, :], f2[...])
        low2[rows, :] = l2
        mid[rows, :] = jnp.where(first, l2, jnp.where(bottom, f2[...], own2[rows, :]))
    mine = where[0] == 1
    q = lambda rows: jnp.where(mine, q_own[rows, :], q_for[rows, :])
    r = column(mine, where[0], rates, q_for)
    attend(q, r, rows_of(low), rows_of(mid), rows_of(high), None, None, att, err)


def lower_kernel(
    where, q_own, q_for, rates, halo_a, halo_b, halo2_a, halo2_b, low2, c, att_up, *rest
):
    att_own, att_for, err, att, b = rest
    bottom = where[0] == 0
    first = where[1] == 0
    inner = where[2] > 0
    for t, h in enumerate((halo2_a, halo2_b)):
        rows = pl.ds(t * HALF, HALF)
        b[rows, :] = jnp.where(first, h[...], low2[rows, :])
    q = lambda rows: jnp.where(bottom, q_own[rows, :], q_for[rows, :])
    r = column(bottom, where[0], rates, q_for)
    halo = (halo_a, halo_b)
    attend(
        q, r, lambda t: halo[t][...], rows_of(b), rows_of(c), inner, inner | ~first, att, err
    )
    att_own[...] = jnp.where(bottom, att[...], att_up[...])
    att_for[...] = jnp.where(bottom, att_up[...], att[...])


def half_of(core, ref):
    return jnp.where(core == 0, ref[:, 0:HALF], ref[:, HALF:HD])


def add_products(where, errs, kns, gateds, slopes, acts, w, total):
    core = where[1]
    w_half = half_of(core, w)
    for e, kn, gated, slope, act in zip(errs, kns, gateds, slopes, acts, strict=True):
        back = mm_n(e[...], w_half)
        total[0] += mm_rows((back * slope[...]).astype(BF), kn[...])
        total[1] += mm_rows((back * act[...]).astype(BF), kn[...])
        total[2] += mm_rows(half_of(core, e), gated[...])


def grad_first_kernel(where, e0, e1, k0, k1, g0, g1, s0, s1, a0, a1, w, total):
    total[...] = jnp.zeros_like(total)
    add_products(where, (e0, e1), (k0, k1), (g0, g1), (s0, s1), (a0, a1), w, total)


def grad_second_kernel(
    zs, where, e0, e1, k0, k1, g0, g1, s0, s1, a0, a1, w, before, own, *rest
):
    sends, total = rest[:-1], rest[-1]
    total[...] = before[...]
    add_products(where, (e0, e1), (k0, k1), (g0, g1), (s0, s1), (a0, a1), w, total)
    rows = HALF // zs
    for d in range(zs):
        src = pl.ds(pl.multiple_of(lax.rem(where[2] + d, zs) * rows, rows), rows)
        for kind in range(3):
            if d == 0:
                own[kind] = total[kind, src, :]
            else:
                sends[d - 1][kind] = total[kind, src, :].astype(BF)


def update_kernel(zs, where, own, *rest):
    got, olds, piece = rest[:-4], rest[-4:-1], rest[-1]
    rows = HALF // zs
    mine = pl.ds(pl.multiple_of(where[1] * HALF + where[2] * rows, rows), rows)
    for kind in range(3):
        grad = own[kind]
        for g in got:
            grad = grad + g[kind].astype(F32)
        old = olds[kind][mine, :].astype(F32)
        raised = old - grad
        factor = jnp.sqrt(jnp.mean(old * old, -1, keepdims=True) + 1e-06) * lax.rsqrt(
            jnp.mean(raised * raised, -1, keepdims=True) + 1e-06
        )
        piece[kind] = (raised * factor).astype(BF)


def gather(zs, where, pieces, kinds, full):
    rows = HALF // zs
    for side, some in ((where[1], pieces[:zs]), (1 - where[1], pieces[zs:])):
        for d in range(zs):
            at = side * HALF + lax.rem(where[2] - d + zs, zs) * rows
            for kind in range(kinds):
                full[pl.ds(pl.multiple_of(kind * HD + at, rows), rows), :] = some[d][kind]


def read(qn, att, full, out, head, work, sems):
    column = pl.ds(pl.multiple_of(head * HD, HD), HD)
    copies = []
    for c in range(1):
        rows = pl.ds(0, BLK)
        x = qn(rows)
        hg = mm_t(x, full[0:HD, :])
        hu = mm_t(x, full[HD : 2 * HD, :])
        g = (hg * jax.nn.sigmoid(hg) * hu).astype(BF)
        fast = mm_t(g, full[2 * HD : 3 * HD, :])
        work[rows, :] = (att[rows, :].astype(F32) + fast).astype(BF)
        copy = pltpu.make_async_copy(work.at[rows, :], out.at[rows, column], sems.at[c])
        copy.start()
        copies.append(copy)
    for copy in copies:
        copy.wait()


def read_own_kernel(zs, where, *rest):
    pieces, (q, att, q_rest, out, full, qn_rest, work, sems) = rest[: 2 * zs], rest[2 * zs :]
    gather(zs, where, pieces, 3, full)
    qn_rest[...] = rms(q_rest[...])
    read(lambda rows: rms(q[rows, :]), att, full, out, where[0], work, sems)


def read_own(zs, where, pieces, q, att, q_rest):
    return pl.pallas_call(
        functools.partial(read_own_kernel, zs),
        in_specs=[SM] + [VM] * (2 * zs + 3),
        out_specs=[pl.BlockSpec(memory_space=pl.ANY), VM, VM],
        out_shape=[shape((BLK, H * HD)), shape((3 * HD, HD)), shape((BLK, HD))],
        scratch_shapes=[pltpu.VMEM((BLK, HD), BF), pltpu.SemaphoreType.DMA((2,))],
        compiler_params=PARAMS,
        name="read_own",
    )(where, *pieces, q, att, q_rest)


def read_other_kernel(zs, count, where, *rest):
    pieces, (qn, att, mine, half_filled, out, weights, full, work, sems) = (
        rest[: 2 * zs],
        rest[2 * zs :],
    )
    y, core, z = where[0], where[1], where[2]
    gather(zs, where, pieces, 3, full)
    step = math.gcd(count, HD)
    first = ((z * 2 + y) * 2 + core) * count
    for c in range(count // step):
        r = first + c * step
        head = lax.rem(lax.div(r, HD), 2)
        at = lax.div(r, 2 * HD) * HD + lax.rem(r, HD)
        rows = pl.ds(pl.multiple_of(at, step), step)
        weights[c * step : (c + 1) * step, :] = jnp.where(head == y, mine[rows, :], full[rows, :])
    read(lambda rows: qn[rows, :], att, full, out, 1 - y, work, sems)


def read_other(zs, where, count, pieces, qn, att, mine, half_filled):
    anyspec = pl.BlockSpec(memory_space=pl.ANY)
    return pl.pallas_call(
        functools.partial(read_other_kernel, zs, count),
        in_specs=[SM] + [VM] * (2 * zs + 3) + [anyspec],
        out_specs=[anyspec, VM],
        out_shape=[shape((BLK, H * HD)), shape((count, HD))],
        scratch_shapes=[
            pltpu.VMEM((3 * HD, HD), BF),
            pltpu.VMEM((BLK, HD), BF),
            pltpu.SemaphoreType.DMA((2,)),
        ],
        input_output_aliases={2 * zs + 4: 0},
        compiler_params=PARAMS,
        name="read_other",
    )(where, *pieces, qn, att, mine, half_filled)


def local(queries, key_rows, value_rows, step_rates, w_gate, w_up, w_down):
    zs = lax.axis_size("z")
    z, y, core = lax.axis_index("z"), lax.axis_index("y"), lax.axis_index("core")
    where = jnp.stack([y, core, z]).astype(jnp.int32)
    rows = HALF // zs

    def swap(value, axis):
        return lax.ppermute(value, axis, SWAP)

    def shift(value, d, ring=True):
        return lax.ppermute(
            value, "z", [(i, (i + d) % zs) for i in range(zs) if ring or i + d < zs]
        )

    two = [shape((BLK, HD))] * 2

    def after(value, earlier):
        return lax.optimization_barrier((value, earlier))[0]

    q_other = pl.BlockSpec((BLK, HD), lambda i, s: (0, 1 - s[0]))
    def paired(first, keys):
        rows = slice(first, first + HALF)
        left = jnp.concatenate([keys[rows, :HD], value_rows[rows, :HD]], 1)
        right = jnp.concatenate([keys[rows, HD:], value_rows[rows, HD:]], 1)
        return jnp.where(y == 0, right, left)

    sent_a = paired(0, key_rows)
    sent_b = paired(HALF, after(key_rows, sent_a))
    sent_q = call_blocks(
        pack_q_kernel, "pack_q", [q_other, None], [shape((BLK + RATE_ROWS, HD))]
    )(where, in_hbm(after(queries, sent_b)), step_rates)[0]
    own = pack(where, after(key_rows, sent_b), value_rows, 0, BLK, True)
    theirs = [swap(sent_a, "y"), swap(sent_b, "y")]
    q_own = jnp.where(y == 0, queries[:, :HD], queries[:, HD:])
    q_rest = jnp.where(y == 0, queries[:, HD:], queries[:, :HD])
    weights = [jnp.where(y == 0, w[:HD], w[HD:]) for w in (w_gate, w_up, w_down)]
    theirs[0], sent_q, q_own, (wg, wu, wd) = lax.optimization_barrier(
        (theirs[0], sent_q, q_own, weights)
    )
    q_for = swap(sent_q, "y")
    own2 = swap(own, "core")
    gone = pick(where, theirs[0], own, 0)
    halo_a = shift(gone, 1, ring=False)
    theirs2 = [swap(after(theirs[0], gone), "core")]
    mine = pre_own(where, own, own2, wg, wu)
    theirs[1], mine, theirs2[0] = lax.optimization_barrier((theirs[1], mine, theirs2[0]))
    gone = pick(where, theirs[1], own, 1)
    halo_b = shift(gone, 1, ring=False)
    theirs2.append(swap(after(theirs[1], gone), "core"))
    theirs2, halo_a = lax.optimization_barrier((theirs2, halo_a))
    low, high = pre(where, theirs, mine[:4], wg, wu)
    theirs2, low, q_for = lax.optimization_barrier((theirs2, low, q_for))
    low2, high2 = pre(where, theirs2, mine[4:], wg, wu)
    low2, q_for = lax.optimization_barrier((low2, q_for))

    pair = shape((BLK, 2 * HD))
    att_up, err_up, kv_low, kv_low2 = call(
        upper_kernel, "attend_upper", two + [pair] * 2, [pltpu.VMEM(pair.shape, BF)] * 2
    )(where, q_own, q_for, step_rates, own, *theirs, own2, *theirs2)
    err_up, halo = lax.optimization_barrier((err_up, (halo_a, halo_b)))
    halo2 = [swap(h, "core") for h in halo]
    err_up2 = swap(err_up, "core")
    att_own, att_for, err_low = call(
        lower_kernel,
        "attend_lower",
        [shape((BLK, HD))] * 3,
        [pltpu.VMEM((BLK, HD), BF), pltpu.VMEM((BLK, 2 * HD), BF)],
    )(where, q_own, q_for, step_rates, *halo, *halo2, kv_low2, kv_low, att_up)
    err_low2 = swap(err_low, "core")

    def factors_of(*blocks):
        return [block[n] for n in range(4) for block in blocks]

    total = shape((3, HALF, HD), F32)
    before = call(grad_first_kernel, "grad_first", [total])(
        where, err_up, err_up2, *factors_of(high, high2), wd
    )[0]
    own_sum, *sends = call(
        functools.partial(grad_second_kernel, zs),
        "grad_second",
        [shape((3, rows, HD), F32)] + [shape((3, rows, HD))] * (zs - 1),
        [pltpu.VMEM(total.shape, F32)],
    )(where, err_low, err_low2, *factors_of(low, low2), wd, before)
    got = [shift(s, d) for d, s in enumerate(sends, 1)]
    att_back = swap(after(att_for, before), "y")
    got, att_back = lax.optimization_barrier((got, att_back))
    piece = call(functools.partial(update_kernel, zs), "update", [shape((3, rows, HD))])(
        where, own_sum, *got, wg, wu, wd
    )[0]
    order = [*range(2, zs - 1), 1, zs - 1]
    pieces = {d: shift(piece, d) for d in order}
    pieces = [piece] + [pieces[d] for d in range(1, zs)]
    others = {d: swap(pieces[d], "y") for d in [*order, 0]}
    others = [others[d] for d in range(zs)]
    gate = [*pieces[1:], others[0], others[zs - 1], others[1]]
    pieces2 = [swap(after(p, gate), "core") for p in pieces]
    pieces2, others = lax.optimization_barrier((pieces2, others))
    others2 = [swap(p, "core") for d, p in enumerate(others)]
    half_filled, full, qn_rest = read_own(zs, where, pieces + pieces2, q_own, att_own, q_rest)
    count = 3 * H * HD // (4 * zs)
    return tuple(
        read_other(
            zs, where, count, others + others2, qn_rest, att_back, full, half_filled
        )
    )


def solution(mesh):
    groups, ctx = mesh.devices.shape
    split = Mesh(mesh.devices.reshape(groups, ctx // 4, 2, 2), ("groups", "z", "y", "core"))
    tokens = ("groups", "z", "y", "core")
    return jax.shard_map(
        local,
        mesh=split,
        in_specs=(
            P(tokens, None),
            P(tokens, None),
            P(tokens, None),
            P(None, tokens),
            P("groups", None),
            P("groups", None),
            P("groups", None),
        ),
        out_specs=(P(tokens, None), P(tokens, None)),
        check_vma=False,
    )
```
